256 devices in a mesh: patch: 128 (over z, y, x), width: 2 (over core).
Axes of the slice: x: 4, y: 4, z: 8, core: 2. Of those that a mesh axis runs over, the one named last changes fastest.
Arguments:
- node_latents: bfloat16 [512, 16384], P('width', 'patch'), may hold values from -6 to 6
- edge_latents: bfloat16 [512, 131072], P('width', 'patch'), may hold values from -6 to 6
- senders: int32 [131072], P('patch'), may hold values from 0 to 16383, as said below
- receivers: int32 [131072], P('patch'), may hold values from 0 to 16383, as said below
- edge_count: int32 [128], P('patch'), may hold values from 512 to 1024, as said below
- edge_in_weight: bfloat16 [2, 512, 1536], P(None, 'width'), may hold values from -0.15625 to 0.15625
- edge_in_bias: float32 [2, 512], P(None, 'width'), may hold values from -3 to 3
- edge_out_weight: bfloat16 [2, 512, 512], P(None, 'width'), may hold values from -0.25 to 0.25
- edge_out_bias: float32 [2, 512], P(None, 'width'), may hold values from -3 to 3
- edge_gain: float32 [2, 512], P(None, 'width'), may hold values from 0.1 to 1.9
- edge_shift: float32 [2, 512], P(None, 'width'), may hold values from -3 to 3
- node_in_weight: bfloat16 [2, 512, 1024], P(None, 'width'), may hold values from -0.1875 to 0.1875
- node_in_bias: float32 [2, 512], P(None, 'width'), may hold values from -3 to 3
- node_out_weight: bfloat16 [2, 512, 512], P(None, 'width'), may hold values from -0.25 to 0.25
- node_out_bias: float32 [2, 512], P(None, 'width'), may hold values from -3 to 3
- node_gain: float32 [2, 512], P(None, 'width'), may hold values from 0.1 to 1.9
- node_shift: float32 [2, 512], P(None, 'width'), may hold values from -3 to 3
Outputs:
- nodes_out: bfloat16 [512, 16384], P('width', 'patch')
- edges_out: bfloat16 [512, 131072], P('width', 'patch')
The draws below stay inside these ranges and needn't reach their ends.
Inputs may be any that keep to these rules, and one draw needn't show every extreme that they name: `senders`: the sender of a slot of patch p is a node of patch p, of patch p - 1 or p + 1 (counted around, modulo the number of patches), or one of the first 16 nodes of some patch. `receivers`: row r names a node of patch r // 1024, from (r // 1024) * 128 to that plus 128 - 1. Slots p * 1024 to p * 1024 + edge_count[p] - 1 of patch p are live, the rest are padding; some patch has all 1024 slots live.
All inputs are finite; a program needn't handle non-finite values.
Results may differ from the reference program's by a relative error of at most 0.014.
Values may be sent and summed in bfloat16 or wider, within the bound.
No kernel may reach another device: no remote copies, remote signals or barrier semaphores. Data moves between devices by JAX's collectives and lax.ppermute only.
A program may use at most 64 MiB of HBM per device.

```python
import jax
import jax.numpy as jnp
from jax import lax

D = 512
H = 512
LAYERS = 2
NODE_DEV = 128
COARSE = 16
EDGE_DEV = 1024
NODES = 16384
EDGES = 131072


def draw_graph(key):
    base = jax.random.fold_in(key, 17)
    keys = jax.random.split(base, 8)
    patches = NODES // NODE_DEV
    slots = jnp.arange(EDGES, dtype=jnp.int32)
    block = slots // EDGE_DEV
    local = jax.random.randint(keys[0], (EDGES,), 0, NODE_DEV).astype(jnp.int32)
    receivers = block * NODE_DEV + local
    kinds = jax.random.randint(keys[1], (EDGES,), 0, 4)
    offset = jax.random.randint(keys[2], (EDGES,), -8, 9).astype(jnp.int32)
    near = block * NODE_DEV + (local + offset) % NODE_DEV
    sideways = jax.random.randint(keys[3], (EDGES,), 0, 2).astype(jnp.int32) * 2 - 1
    beside = (block + sideways) % patches * NODE_DEV + jax.random.randint(keys[4], (EDGES,), 0, NODE_DEV).astype(jnp.int32)
    random_patch = jax.random.randint(keys[5], (EDGES,), 0, patches).astype(jnp.int32)
    opposite = ((block + patches // 2) % patches).astype(jnp.int32)
    toward = jax.random.randint(keys[7], (EDGES,), 0, 2)
    far_patch = jnp.where(toward == 1, opposite, random_patch)
    anywhere = far_patch * NODE_DEV + jax.random.randint(keys[6], (EDGES,), 0, COARSE).astype(jnp.int32)
    senders = jnp.where(kinds < 2, near, jnp.where(kinds == 2, beside, anywhere))
    return (senders.astype(jnp.int32), receivers.astype(jnp.int32))


def draw_senders(key, part):
    return draw_graph(key)[0]


def draw_receivers(key, part):
    return draw_graph(key)[1]


def draw_edge_count(key, part):
    patches = NODES // NODE_DEV
    first, second = jax.random.split(jax.random.fold_in(key, 29))
    counts = jax.random.randint(first, (patches,), EDGE_DEV // 2, EDGE_DEV + 1).astype(jnp.int32)
    filled = jax.random.randint(second, (), 0, patches)
    return jnp.where(jnp.arange(patches) == filled, EDGE_DEV, counts).astype(jnp.int32)


def levels(rng, extent, shards, low, largest):
    def one(dim, shards_of):
        draws = jax.random.uniform(jax.random.fold_in(jax.random.fold_in(rng, 6), dim), (shards_of,), jnp.float32, low / len(shards), largest / len(shards))
        return jnp.repeat(jnp.exp(draws), extent[dim] // shards_of).reshape((-1,) + (1,) * (len(extent) - dim - 1))

    level = one(*shards[0])
    for cut in shards[1:]:
        level = level * one(*cut)
    return level


def gaussian(rng, shape, width, bound, shards=(), held_as=jnp.bfloat16):
    drawn = width * jax.random.normal(rng, shape, jnp.float32)
    if shards:
        drawn = drawn * levels(rng, shape, shards, -0.22, 0.18)
    return jnp.clip(drawn, -bound, bound).astype(held_as)


def setup_inputs(seed: int = 0) -> dict:
    key_of = jax.random.split(jax.random.key(seed), 18)
    return {
        "node_latents": gaussian(key_of[0], (D, NODES), 1.0, 6.0, ((0, 2), (1, 128))),
        "edge_latents": gaussian(key_of[1], (D, EDGES), 1.0, 6.0, ((0, 2), (1, 128))),
        "senders": draw_senders(jax.random.fold_in(key_of[17], 71), 0),
        "receivers": draw_receivers(jax.random.fold_in(key_of[17], 71), 0),
        "edge_count": draw_edge_count(jax.random.fold_in(key_of[17], 71), 0),
        "edge_in_weight": gaussian(key_of[5], (LAYERS, H, 3 * D), (3 * D) ** -0.5, 0.15625, ((1, 2),)),
        "edge_in_bias": gaussian(key_of[6], (LAYERS, H), 0.5, 3.0, ((1, 2),), jnp.float32),
        "edge_out_weight": gaussian(key_of[7], (LAYERS, H, D), H ** -0.5, 0.25, ((1, 2),)),
        "edge_out_bias": gaussian(key_of[8], (LAYERS, D), 0.5, 3.0, ((1, 2),), jnp.float32),
        "edge_gain": jnp.clip(1.0 + 0.18 * jax.random.normal(key_of[9], (LAYERS, D), jnp.float32), 0.1, 1.9),
        "edge_shift": gaussian(key_of[10], (LAYERS, D), 0.5, 3.0, ((1, 2),), jnp.float32),
        "node_in_weight": gaussian(key_of[11], (LAYERS, H, 2 * D), (2 * D) ** -0.5, 0.1875, ((1, 2),)),
        "node_in_bias": gaussian(key_of[12], (LAYERS, H), 0.5, 3.0, ((1, 2),), jnp.float32),
        "node_out_weight": gaussian(key_of[13], (LAYERS, H, D), H ** -0.5, 0.25, ((1, 2),)),
        "node_out_bias": gaussian(key_of[14], (LAYERS, D), 0.5, 3.0, ((1, 2),), jnp.float32),
        "node_gain": jnp.clip(1.0 + 0.18 * jax.random.normal(key_of[15], (LAYERS, D), jnp.float32), 0.1, 1.9),
        "node_shift": gaussian(key_of[16], (LAYERS, D), 0.5, 3.0, ((1, 2),), jnp.float32),
    }


def layer_norm(values, gain, shift):
    mean = lax.optimization_barrier(jnp.sum(values, axis=-1, keepdims=True)) / D
    square = lax.optimization_barrier(jnp.sum(values * values, axis=-1, keepdims=True)) / D
    return (values - mean) * jax.lax.rsqrt(square - mean * mean + 1e-05) * gain + shift

def reference(node_latents, edge_latents, senders, receivers, edge_count, edge_in_weight, edge_in_bias, edge_out_weight, edge_out_bias, edge_gain, edge_shift, node_in_weight, node_in_bias, node_out_weight, node_out_bias, node_gain, node_shift):
    slots = jnp.arange(EDGES, dtype=jnp.int32)
    live = slots % EDGE_DEV < edge_count[slots // EDGE_DEV]
    nodes = node_latents.T
    edges = edge_latents.T
    for layer in range(LAYERS):
        w_edge = edge_in_weight[layer].T
        w_node = node_in_weight[layer].T
        sender_part = jnp.dot(nodes, w_edge[D:2 * D], preferred_element_type=jnp.float32).astype(jnp.bfloat16)
        receiver_part = jnp.dot(nodes, w_edge[2 * D:], preferred_element_type=jnp.float32).astype(jnp.bfloat16)
        node_first = jnp.dot(nodes, w_node[:D], preferred_element_type=jnp.float32)
        before = jnp.dot(edges, w_edge[:D], preferred_element_type=jnp.float32)
        before = before + sender_part[senders].astype(jnp.float32) + receiver_part[receivers].astype(jnp.float32) + edge_in_bias[layer]
        edge_hidden = jax.nn.silu(before).astype(jnp.bfloat16)
        edge_mlp = jnp.dot(edge_hidden, edge_out_weight[layer], preferred_element_type=jnp.float32) + edge_out_bias[layer]
        updated = edges.astype(jnp.float32) + layer_norm(edge_mlp, edge_gain[layer], edge_shift[layer])
        edges = jnp.where(live[:, None], updated, jnp.float32(0.0)).astype(jnp.bfloat16)
        aggregate = jax.ops.segment_sum(edges.astype(jnp.float32), receivers, num_segments=NODES).astype(jnp.bfloat16)
        node_before = node_first + jnp.dot(aggregate, w_node[D:], preferred_element_type=jnp.float32) + node_in_bias[layer]
        node_hidden = jax.nn.silu(node_before).astype(jnp.bfloat16)
        node_mlp = jnp.dot(node_hidden, node_out_weight[layer], preferred_element_type=jnp.float32) + node_out_bias[layer]
        nodes = (nodes.astype(jnp.float32) + layer_norm(node_mlp, node_gain[layer], node_shift[layer])).astype(jnp.bfloat16)
    return (nodes.T, edges.T)
```

```python
import functools

import jax
import jax.numpy as jnp
from jax import lax
from jax.experimental import pallas as pl
from jax.experimental.pallas import tpu as pltpu
from jax.sharding import Mesh
from jax.sharding import PartitionSpec as P

Z, Y, X = "patch_0", "patch_1", "patch_2"
PATCH = (Z, Y, X)
PLANE = (Y, X)
EPSILON = 1e-05
EDGE_BLOCK = 256
VMEM_LIMIT = 48 * 1024 * 1024


def dot(left, right, contract=((1,), (0,))):
    return lax.dot_general(left, right, (contract, ((), ())), preferred_element_type=jnp.float32)


def silu(v):
    h = 0.5 * v
    return h + h * jnp.tanh(h)


def layer_norm(values, gain, shift):
    width = values.shape[0]
    mean = jnp.sum(values, axis=0, keepdims=True) * (1.0 / width)
    square = jnp.sum(values * values, axis=0, keepdims=True) * (1.0 / width)
    return (values - mean) * lax.rsqrt(square - mean * mean + EPSILON) * gain + shift


def in_order(first, mine, other):
    return jnp.concatenate([jnp.where(first, mine, other), jnp.where(first, other, mine)], axis=0)


def gather_kernel(index_ref, below_ref, here_ref, above_ref, coarse_ref, out_ref):
    index = index_ref[...]
    rows = index.shape[0]
    lane = lax.broadcasted_iota(jnp.int32, (rows, 128), 1)

    def selection(start, length):
        tiles = []
        for j in range(start, start + length, 128):
            tiles.append(jnp.where(index == lane + j, 1.0, 0.0).astype(jnp.bfloat16))
        return jnp.concatenate(tiles, axis=1) if len(tiles) > 1 else tiles[0]

    near = jnp.concatenate([below_ref[...], here_ref[...], above_ref[...]], axis=0)
    total = dot(selection(0, near.shape[0]), near)
    total = total + dot(selection(near.shape[0], coarse_ref.shape[0]), coarse_ref[...])
    out_ref[...] = total.astype(jnp.bfloat16)


def gathered(index, below, here, above, coarse):
    slots = index.shape[0]
    width = here.shape[1]
    whole = lambda a: pl.BlockSpec(a.shape, lambda i: (0, 0))
    return pl.pallas_call(
        gather_kernel,
        grid=(slots // EDGE_BLOCK,),
        in_specs=[
            pl.BlockSpec((EDGE_BLOCK, 128), lambda i: (i, 0)),
            whole(below),
            whole(here),
            whole(above),
            whole(coarse),
        ],
        out_specs=pl.BlockSpec((EDGE_BLOCK, width), lambda i: (i, 0)),
        out_shape=jax.ShapeDtypeStruct((slots, width), jnp.bfloat16),
        compiler_params=pltpu.CompilerParams(vmem_limit_bytes=VMEM_LIMIT),
        cost_estimate=pl.CostEstimate(
            flops=2 * slots * width * 2432, bytes_accessed=3 << 20, transcendentals=0
        ),
        name="gather_senders",
    )(index, below, here, above, coarse)


def update_kernel(
    first_layer,
    last_layer,
    scalar_ref,
    edge_a_ref,
    edge_b_ref,
    sent_a_ref,
    sent_b_ref,
    receiver_ref,
    node_a_ref,
    node_b_ref,
    wa_ref,
    wb_ref,
    ea_ref,
    eb_ref,
    va_ref,
    vb_ref,
    oa_ref,
    ob_ref,
    vec_a_ref,
    vec_b_ref,
    *rest,
):
    if last_layer:
        edge_out_ref, node_out_ref, part_ref, out_weight_ref, sum_ref = rest
        rows_out_ref = None
    else:
        edge_out_ref, node_out_ref, rows_out_ref, part_ref, out_weight_ref, sum_ref = rest
    step = pl.program_id(0)
    first = scalar_ref[0] == 0
    count = scalar_ref[1]
    half = vec_a_ref.shape[1]
    width = 2 * half

    def stacked(a, b):
        return jnp.concatenate([a, b], axis=0)

    def nodes_now():
        if first_layer:
            return in_order(first, node_a_ref[...], node_b_ref[...])
        return node_a_ref[...]

    w = stacked(wa_ref[0], wb_ref[0])
    vec_a, vec_b = vec_a_ref[0], vec_b_ref[0]
    hidden_vec = stacked(vec_a, vec_b)
    feature_vec = in_order(first, vec_a, vec_b)

    @pl.when(step == 0)
    def _():
        part_ref[...] = dot(w[:, 2 * width :], nodes_now()).astype(jnp.bfloat16)
        out_weight_ref[...] = stacked(ea_ref[0], eb_ref[0]).T
        sum_ref[...] = jnp.zeros_like(sum_ref)

    if first_layer:
        edges = in_order(first, edge_a_ref[...], edge_b_ref[...])
    else:
        edges = edge_a_ref[...]
    slots = edges.shape[1]
    sent_a, sent_b = sent_a_ref[...], sent_b_ref[...]
    sent = jnp.concatenate(
        [jnp.where(first, sent_a, sent_b), jnp.where(first, sent_b, sent_a)], axis=1
    )
    nodes_here = sum_ref.shape[1]
    live = lax.broadcasted_iota(jnp.int32, (1, slots), 1) + step * slots < count
    receiver = receiver_ref[...]
    incidence = jnp.where(
        (lax.broadcasted_iota(jnp.int32, (nodes_here, slots), 0) == receiver) & live, 1.0, 0.0
    ).astype(jnp.bfloat16)
    before = dot(w[:, :width], edges) + dot(w[:, width : 2 * width], sent, ((1,), (1,)))
    before = before + dot(part_ref[...], incidence) + hidden_vec[:, 0:1]
    hidden = silu(before).astype(jnp.bfloat16)
    mlp = dot(out_weight_ref[...], hidden) + feature_vec[:, 1:2]
    updated = edges.astype(jnp.float32) + layer_norm(mlp, feature_vec[:, 2:3], feature_vec[:, 3:4])
    updated = jnp.where(live, updated, 0.0).astype(jnp.bfloat16)
    sum_ref[...] += dot(updated, incidence, ((1,), (1,)))
    if last_layer:
        edge_out_ref[...] = jnp.where(first, updated[:half], updated[half:])
    else:
        edge_out_ref[...] = updated

    @pl.when(step == pl.num_programs(0) - 1)
    def _():
        nodes = nodes_now()
        v = stacked(va_ref[0], vb_ref[0])
        aggregate = sum_ref[...].astype(jnp.bfloat16)
        node_before = dot(v[:, :width], nodes) + dot(v[:, width:], aggregate)
        node_hidden = silu(node_before + hidden_vec[:, 4:5]).astype(jnp.bfloat16)
        node_weight = stacked(oa_ref[0], ob_ref[0]).T
        node_mlp = dot(node_weight, node_hidden) + feature_vec[:, 5:6]
        new = nodes.astype(jnp.float32) + layer_norm(
            node_mlp, feature_vec[:, 6:7], feature_vec[:, 7:8]
        )
        new = new.astype(jnp.bfloat16)
        mine = jnp.where(first, new[:half], new[half:])
        if last_layer:
            node_out_ref[...] = mine
        else:
            node_out_ref[...] = new
            rows_out_ref[...] = mine.T


def updated_graph(layer, layers, scalars, edges, sent, receiver, nodes, weights):
    first_layer, last_layer = layer == 0, layer == layers - 1
    slots = edges[0].shape[1]
    node_rows = nodes[0].shape[1]
    half = sent[0].shape[1]
    width = 2 * half

    def by_slot(a):
        return pl.BlockSpec((a.shape[0], EDGE_BLOCK), lambda i: (0, i))

    def by_row(a):
        return pl.BlockSpec((EDGE_BLOCK, a.shape[1]), lambda i: (i, 0))

    def whole(a):
        return pl.BlockSpec(a.shape, lambda i: (0, 0))

    def of_layer(a):
        return pl.BlockSpec((1, *a.shape[1:]), lambda i: (layer, 0, 0))

    edge_width = half if last_layer else width
    out_shape = [
        jax.ShapeDtypeStruct((edge_width, slots), jnp.bfloat16),
        jax.ShapeDtypeStruct((edge_width, node_rows), jnp.bfloat16),
    ]
    out_specs = [
        pl.BlockSpec((edge_width, EDGE_BLOCK), lambda i: (0, i)),
        pl.BlockSpec((edge_width, node_rows), lambda i: (0, 0)),
    ]
    if not last_layer:
        out_shape.append(jax.ShapeDtypeStruct((node_rows, half), jnp.bfloat16))
        out_specs.append(pl.BlockSpec((node_rows, half), lambda i: (0, 0)))
    flops = 2 * slots * width * (3 * width + 2 * node_rows)
    return pl.pallas_call(
        functools.partial(update_kernel, first_layer, last_layer),
        grid=(slots // EDGE_BLOCK,),
        in_specs=[
            pl.BlockSpec(memory_space=pltpu.SMEM),
            by_slot(edges[0]),
            by_slot(edges[1]),
            by_row(sent[0]),
            by_row(sent[1]),
            by_slot(receiver),
            whole(nodes[0]),
            whole(nodes[1]),
            *[of_layer(a) for a in weights],
        ],
        out_specs=out_specs,
        out_shape=out_shape,
        scratch_shapes=[
            pltpu.VMEM((width, node_rows), jnp.bfloat16),
            pltpu.VMEM((width, width), jnp.bfloat16),
            pltpu.VMEM((width, node_rows), jnp.float32),
        ],
        compiler_params=pltpu.CompilerParams(vmem_limit_bytes=VMEM_LIMIT),
        cost_estimate=pl.CostEstimate(
            flops=flops, bytes_accessed=8 << 20, transcendentals=slots * width
        ),
        name="update_graph",
    )(scalars, *edges, *sent, receiver, *nodes, *weights)


def from_other(a):
    return lax.ppermute(a, "width", [(0, 1), (1, 0)])


def from_everyone(shard, axes):
    copies = jnp.broadcast_to(shard, (lax.axis_size(axes), *shard.shape))
    parts = lax.all_to_all(copies, axes, split_axis=0, concat_axis=0, tiled=True)
    return parts.reshape(-1, shard.shape[-1])


def beside(rows):
    size = lax.axis_size(PATCH)
    up = [(i, (i + 1) % size) for i in range(size)]
    down = [(j, i) for i, j in up]
    return lax.ppermute(rows, PATCH, up), lax.ppermute(rows, PATCH, down)


def on_device(
    node_latents,
    edge_latents,
    senders,
    receivers,
    edge_count,
    edge_in_weight,
    edge_in_bias,
    edge_out_weight,
    edge_out_bias,
    edge_gain,
    edge_shift,
    node_in_weight,
    node_in_bias,
    node_out_weight,
    node_out_bias,
    node_gain,
    node_shift,
):
    node_rows = node_latents.shape[1]
    layers = edge_in_weight.shape[0]
    coarse_rows = node_rows // 8
    patch_here = lax.axis_index(PATCH)
    patches = lax.axis_size(PATCH)
    plane = lax.axis_size(PLANE)
    scalars = jnp.stack([lax.axis_index("width"), edge_count[0]]).astype(jnp.int32)

    rows = node_latents.T
    below, above = beside(rows)
    coarse = from_everyone(from_everyone(rows[:coarse_rows], Z), PLANE)

    vectors = jnp.stack(
        [
            edge_in_bias,
            edge_out_bias,
            edge_gain,
            edge_shift,
            node_in_bias,
            node_out_bias,
            node_gain,
            node_shift,
        ],
        axis=2,
    )
    own = (edge_in_weight, edge_out_weight, node_in_weight, node_out_weight, vectors)
    weights = []
    for a in own:
        weights += [a, from_other(a)]

    owner = senders // node_rows
    within = senders - owner * node_rows
    place = (owner % plane) * (patches // plane) + owner // plane
    index = jnp.where(
        owner == patch_here,
        node_rows + within,
        jnp.where(
            owner == (patch_here + patches - 1) % patches,
            within,
            jnp.where(
                owner == (patch_here + 1) % patches,
                2 * node_rows + within,
                3 * node_rows + place * coarse_rows + within,
            ),
        ),
    )
    index = jnp.broadcast_to(index[:, None], (index.shape[0], 128))
    receiver = (receivers - patch_here * node_rows)[None, :]

    edges = (edge_latents, from_other(edge_latents))
    nodes = (node_latents, from_other(node_latents))
    for layer in range(layers):
        sent = gathered(index, below, rows, above, coarse)
        sent = (sent, from_other(sent))
        results = updated_graph(
            layer, layers, scalars, edges, sent, receiver, nodes, weights
        )
        if layer < layers - 1:
            edges, nodes, rows = results
            edges, nodes = (edges, edges), (nodes, nodes)
            below, above = beside(rows)
            coarse = from_everyone(from_everyone(rows[:coarse_rows], Z), PLANE)
    return (results[1], results[0])


def solution(mesh):
    finer = Mesh(
        mesh.devices.reshape(8, 4, 4, mesh.shape["width"]),
        (*PATCH, "width"),
    )
    in_specs = (
        P("width", PATCH),
        P("width", PATCH),
        P(PATCH),
        P(PATCH),
        P(PATCH),
        P(None, "width", None),
        P(None, "width"),
        P(None, "width", None),
        P(None, "width"),
        P(None, "width"),
        P(None, "width"),
        P(None, "width", None),
        P(None, "width"),
        P(None, "width", None),
        P(None, "width"),
        P(None, "width"),
        P(None, "width"),
    )
    out_specs = (P("width", PATCH), P("width", PATCH))
    return jax.shard_map(
        on_device, mesh=finer, in_specs=in_specs, out_specs=out_specs, check_vma=False
    )
```

```python
import functools

import jax
import jax.numpy as jnp
from jax import lax
from jax.experimental import pallas as pl
from jax.experimental.pallas import tpu as pltpu
from jax.sharding import Mesh
from jax.sharding import PartitionSpec as P

Z, Y, X = "patch_0", "patch_1", "patch_2"
PATCH = (Z, Y, X)
PLANE = (Y, X)
EPSILON = 1e-05
EDGE_BLOCK = 512
VMEM_LIMIT = 32 * 1024 * 1024


def dot(left, right, contract=((1,), (0,))):
    return lax.dot_general(left, right, (contract, ((), ())), preferred_element_type=jnp.float32)


def silu(v):
    h = 0.5 * v
    return h + h * jnp.tanh(h)


def layer_norm(values, gain, shift):
    width = values.shape[0]
    mean = jnp.sum(values, axis=0, keepdims=True) * (1.0 / width)
    square = jnp.sum(values * values, axis=0, keepdims=True) * (1.0 / width)
    return (values - mean) * lax.rsqrt(square - mean * mean + EPSILON) * gain + shift


def in_order(first, mine, other):
    return jnp.concatenate([jnp.where(first, mine, other), jnp.where(first, other, mine)], axis=0)


VMEM = pl.BlockSpec(memory_space=pltpu.VMEM)
SMEM = pl.BlockSpec(memory_space=pltpu.SMEM)
HBM = pl.BlockSpec(memory_space=pltpu.HBM)


def shape(dims, dtype=jnp.bfloat16):
    return jax.ShapeDtypeStruct(dims, dtype)


def kernel_call(body, name, out_shape, inputs, in_specs, out_specs, scratch, flops):
    inputs = [
        pltpu.with_memory_space_constraint(a, pltpu.HBM) if spec is HBM else a
        for a, spec in zip(inputs, in_specs)
    ]
    if isinstance(out_specs, list):
        out_shape = [
            pltpu.HBM(a.shape, a.dtype) if spec is HBM else a
            for a, spec in zip(out_shape, out_specs)
        ]
    return pl.pallas_call(
        body,
        in_specs=in_specs,
        out_specs=out_specs,
        out_shape=out_shape,
        scratch_shapes=scratch,
        compiler_params=pltpu.CompilerParams(vmem_limit_bytes=VMEM_LIMIT),
        cost_estimate=pl.CostEstimate(flops=flops, bytes_accessed=4 << 20, transcendentals=0),
        name=name,
    )(*inputs)


def started(pairs, sems):
    copies = [pltpu.make_async_copy(a, b, sems.at[i]) for i, (a, b) in enumerate(pairs)]
    for copy in copies:
        copy.start()
    return copies


def finish(copies):
    for copy in copies:
        copy.wait()


def held(arrays):
    return [pltpu.VMEM(a.shape, a.dtype) for a in arrays]


def columns_of(ref, start, length):
    return ref.at[:, pl.ds(start, length)]


def store_rows(mine, rows_ref, copies_ref):
    rows = mine.T
    rows_ref[...] = rows
    for i in range(copies_ref.shape[0]):
        copies_ref[i] = rows[: copies_ref.shape[1]]


def rows_kernel(nodes_ref, rows_ref, copies_ref, held_ref, sem):
    copies = started([(nodes_ref, held_ref)], sem)
    finish(copies)
    store_rows(held_ref[...], rows_ref, copies_ref)


def node_rows_of(nodes, columns):
    half, node_rows = nodes.shape
    return kernel_call(
        rows_kernel,
        "node_rows",
        [shape((node_rows, half)), shape((columns, node_rows // 8, half))],
        (nodes,),
        [HBM],
        [VMEM, VMEM],
        held([nodes]) + [pltpu.SemaphoreType.DMA((1,))],
        0,
    )


def gather_kernel(
    index_in, below_in, here_in, above_in, coarse_in, out_ref, index_ref, near_ref, coarse_ref, sems
):
    rows = here_in.shape[0]
    copies = started(
        [
            (index_in, index_ref),
            (below_in, near_ref.at[pl.ds(0, rows)]),
            (here_in, near_ref.at[pl.ds(rows, rows)]),
            (above_in, near_ref.at[pl.ds(2 * rows, rows)]),
            (coarse_in, coarse_ref),
        ],
        sems,
    )
    finish(copies[:4])
    columns = index_ref[...].T
    lane = lax.broadcasted_iota(jnp.int32, (128, 128), 1)

    def selection(start, first, length):
        blocks = []
        for k in range(start // 128, (start + EDGE_BLOCK) // 128):
            index = jnp.broadcast_to(columns[:, k : k + 1], (128, 128))
            tiles = []
            for j in range(first, first + length, 128):
                tiles.append(jnp.where(index == lane + j, 1.0, 0.0).astype(jnp.bfloat16))
            blocks.append(jnp.concatenate(tiles, axis=1))
        return jnp.concatenate(blocks, axis=0)

    for start in range(0, out_ref.shape[0], EDGE_BLOCK):
        total = dot(selection(start, 0, 3 * rows), near_ref[...])
        if start == 0:
            finish(copies[4:])
        total = total + dot(selection(start, 3 * rows, coarse_ref.shape[0]), coarse_ref[...])
        out_ref[start : start + EDGE_BLOCK, :] = total.astype(jnp.bfloat16)


def gathered(index, below, here, above, coarse):
    slots = index.size
    rows, width = here.shape
    table = 3 * rows + coarse.shape[0]
    return kernel_call(
        gather_kernel,
        "gather_senders",
        shape((slots, width)),
        (index, below, here, above, coarse),
        [HBM] * 4 + [pl.BlockSpec(memory_space=pl.ANY)],
        VMEM,
        held([index, shape((3 * rows, width)), coarse]) + [pltpu.SemaphoreType.DMA((5,))],
        2 * slots * width * table,
    )


def prepare_kernel(layer, n_in, n_out, scalar_ref, *refs):
    ins, outs = refs[:n_in], refs[n_in : n_in + n_out]
    held_in = refs[n_in + n_out : 2 * n_in + n_out]
    held_out = refs[2 * n_in + n_out : 2 * (n_in + n_out)]
    in_sems, out_sems = refs[2 * (n_in + n_out) :]
    copies = started(
        [(a.at[layer] if len(a.shape) == 3 else a, b) for a, b in zip(ins, held_in)], in_sems
    )
    first = scalar_ref[0] == 0
    count = scalar_ref[1]
    sent = [pltpu.make_async_copy(held_out[i], outs[i], out_sems.at[i]) for i in range(n_out)]
    if layer == 0:
        edge_a, edge_b, receiver_ref, node_a, node_b = held_in[:5]
    else:
        edge_a, receiver_ref, node_a = held_in[:3]
        edge_b, node_b = edge_a, node_a
    wa, wb, ea, eb, va, vb, oa, ob, vec_a_ref, vec_b_ref = held_in[-10:]
    (
        before_ref,
        node_before_ref,
        incidence_ref,
        sent_weight_ref,
        out_weight_ref,
        aggregate_weight_ref,
        node_weight_ref,
        vectors_ref,
    ) = held_out[:8]
    width = out_weight_ref.shape[0]
    nodes_here, slots = incidence_ref.shape

    def stacked(a, b):
        return jnp.concatenate([a, b], axis=0)

    finish(copies)
    if layer == 0:
        edges = in_order(first, edge_a[...], edge_b[...])
        nodes = in_order(first, node_a[...], node_b[...])
        held_out[8][...] = edges
        held_out[9][...] = nodes
        sent[8].start()
        sent[9].start()
    else:
        edges, nodes = edge_a[...], node_a[...]
    w = stacked(wa[...], wb[...])
    v = stacked(va[...], vb[...])
    sent_weight_ref[...] = w[:, width : 2 * width]
    sent[3].start()
    out_weight_ref[...] = stacked(ea[...], eb[...]).T
    sent[4].start()
    aggregate_weight_ref[...] = v[:, width:]
    sent[5].start()
    node_weight_ref[...] = stacked(oa[...], ob[...]).T
    sent[6].start()
    vec_a, vec_b = vec_a_ref[...].T, vec_b_ref[...].T
    hidden_vec = stacked(vec_a, vec_b)
    vectors_ref[...] = in_order(first, vec_a, vec_b)
    sent[7].start()
    live = lax.broadcasted_iota(jnp.int32, (1, slots), 1) < count
    incidence_ref[...] = jnp.where(
        (lax.broadcasted_iota(jnp.int32, (nodes_here, slots), 0) == receiver_ref[...]) & live,
        1.0,
        0.0,
    ).astype(jnp.bfloat16)
    sent[2].start()
    node_before_ref[...] = dot(v[:, :width], nodes) + hidden_vec[:, 4:5]
    sent[1].start()
    part = dot(w[:, 2 * width :], nodes).astype(jnp.bfloat16)
    before = dot(w[:, :width], edges) + dot(part, incidence_ref[...])
    before_ref[...] = before + hidden_vec[:, 0:1]
    sent[0].start()
    finish(sent)


def prepared(layer, scalars, edges, receiver, nodes, weights):
    slots = edges[0].shape[1]
    node_rows = nodes[0].shape[1]
    width = weights[0].shape[1] * 2
    inputs = (*edges, receiver, *nodes, *weights)
    out_shape = [
        shape((width, slots), jnp.float32),
        shape((width, node_rows), jnp.float32),
        shape((node_rows, slots)),
        shape((width, width)),
        shape((width, width)),
        shape((width, width)),
        shape((width, width)),
        shape((width, 8), jnp.float32),
    ]
    if layer == 0:
        out_shape += [shape((width, slots)), shape((width, node_rows))]
    n_in, n_out = len(inputs), len(out_shape)
    one_layer = [shape(a.shape[-2:], a.dtype) for a in inputs]
    ready = kernel_call(
        functools.partial(prepare_kernel, layer, n_in, n_out),
        "prepare_layer",
        out_shape,
        (scalars, *inputs),
        [SMEM] + [HBM] * n_in,
        [HBM] * n_out,
        held(one_layer)
        + held(out_shape)
        + [pltpu.SemaphoreType.DMA((n_in,)), pltpu.SemaphoreType.DMA((n_out,))],
        2 * slots * width * (width + node_rows),
    )
    if layer == 0:
        return (ready[8], ready[9], *ready[:8])
    return (edges[0], nodes[0], *ready)


def update_kernel(last_layer, n_out, scalar_ref, sent_a_ref, sent_b_ref, *refs):
    ins, outs, held_in = refs[:10], refs[10 : 10 + n_out], refs[10 + n_out : 20 + n_out]
    held_out = refs[20 + n_out : 20 + 2 * n_out]
    in_sems, out_sems = refs[20 + 2 * n_out :]
    edges_ref, nodes_ref, before_ref, node_before_ref, incidence_ref = held_in[:5]
    sent_weight_ref, out_weight_ref, aggregate_weight_ref, node_weight_ref, vectors_ref = held_in[
        5:
    ]
    slots = edges_ref.shape[1]
    starts = range(0, slots, EDGE_BLOCK)
    early = [(ins[5], sent_weight_ref)]
    for start in starts:
        early.append(tuple(columns_of(r, start, EDGE_BLOCK) for r in (ins[2], before_ref)))
        if start == 0:
            early += [(ins[6], out_weight_ref), (ins[9], vectors_ref)]
        for i in (0, 4):
            early.append(tuple(columns_of(r, start, EDGE_BLOCK) for r in (ins[i], held_in[i])))
    late = [(ins[i], held_in[i]) for i in (1, 3, 7, 8)]
    copies = started(early + late, in_sems)
    groups = [copies[:6], copies[6:9], copies[9:]]

    first = scalar_ref[0] == 0
    count = scalar_ref[1]
    half = sent_a_ref.shape[1]
    total = None
    edge_out_ref, node_out_ref = held_out[:2]
    sent_out = []

    def send(source, target):
        copy = pltpu.make_async_copy(source, target, out_sems.at[len(sent_out)])
        copy.start()
        sent_out.append(copy)

    for turn, start in enumerate(starts):
        finish(groups[turn])
        vectors = vectors_ref[...]
        here = slice(start, start + EDGE_BLOCK)
        sent_a, sent_b = sent_a_ref[here, :], sent_b_ref[here, :]
        low = jnp.where(first, sent_a, sent_b)
        high = jnp.where(first, sent_b, sent_a)
        sent = jnp.concatenate([low, high], axis=1)
        before = before_ref[:, here] + dot(sent_weight_ref[...], sent, ((1,), (1,)))
        hidden = silu(before).astype(jnp.bfloat16)
        mlp = dot(out_weight_ref[...], hidden) + vectors[:, 1:2]
        live = lax.broadcasted_iota(jnp.int32, (1, EDGE_BLOCK), 1) + start < count
        updated = edges_ref[:, here].astype(jnp.float32) + layer_norm(
            mlp, vectors[:, 2:3], vectors[:, 3:4]
        )
        updated = jnp.where(live, updated, 0.0).astype(jnp.bfloat16)
        part = dot(updated, incidence_ref[:, here], ((1,), (1,)))
        total = part if total is None else total + part
        if last_layer:
            edge_out_ref[:, here] = jnp.where(first, updated[:half], updated[half:])
        else:
            edge_out_ref[:, here] = updated
        send(
            columns_of(edge_out_ref, start, EDGE_BLOCK), columns_of(outs[0], start, EDGE_BLOCK)
        )
    finish(groups[2])
    aggregate = total.astype(jnp.bfloat16)
    node_before = node_before_ref[...] + dot(aggregate_weight_ref[...], aggregate)
    node_hidden = silu(node_before).astype(jnp.bfloat16)
    node_mlp = dot(node_weight_ref[...], node_hidden) + vectors[:, 5:6]
    new = nodes_ref[...].astype(jnp.float32) + layer_norm(
        node_mlp, vectors[:, 6:7], vectors[:, 7:8]
    )
    new = new.astype(jnp.bfloat16)
    mine = jnp.where(first, new[:half], new[half:])
    if last_layer:
        node_out_ref[...] = mine
    else:
        store_rows(mine, *held_out[2:])
        for i in (2, 3):
            send(held_out[i], outs[i])
        node_out_ref[...] = new
    send(node_out_ref, outs[1])
    finish(sent_out)


def updated_graph(last_layer, scalars, sent, ready, copies):
    slots = ready[0].shape[1]
    node_rows = ready[1].shape[1]
    half = sent[0].shape[1]
    width = 2 * half
    out_width = half if last_layer else width
    out_shape = [shape((out_width, slots)), shape((out_width, node_rows))]
    if not last_layer:
        out_shape += [shape((node_rows, half)), shape((copies, node_rows // 8, half))]
    n_out = len(out_shape)
    blocks = slots // EDGE_BLOCK
    return kernel_call(
        functools.partial(update_kernel, last_layer, n_out),
        "update_graph",
        out_shape,
        (scalars, *sent, *ready),
        [SMEM, VMEM, VMEM] + [HBM] * 10,
        [HBM] * n_out,
        held(ready)
        + held(out_shape)
        + [
            pltpu.SemaphoreType.DMA((3 * blocks + 7,)),
            pltpu.SemaphoreType.DMA((n_out - 1 + blocks,)),
        ],
        2 * slots * width * (2 * width + node_rows),
    )


def from_other(a):
    return lax.ppermute(a, "width", [(0, 1), (1, 0)])


def exchanged(rows, copies):
    size = lax.axis_size(PATCH)
    up = [(i, (i + 1) % size) for i in range(size)]
    down = [(j, i) for i, j in up]
    below, above = lax.ppermute(rows, PATCH, up), lax.ppermute(rows, PATCH, down)
    column = lax.all_to_all(copies, Z, split_axis=0, concat_axis=0, tiled=True)
    column = column.reshape(-1, rows.shape[1])
    column, below, above = lax.optimization_barrier((column, below, above))
    plane = jnp.broadcast_to(column, (lax.axis_size(PLANE), *column.shape))
    coarse = lax.all_to_all(plane, PLANE, split_axis=0, concat_axis=0, tiled=True)
    return below, rows, above, coarse.reshape(-1, rows.shape[1])


def on_device(
    node_latents,
    edge_latents,
    senders,
    receivers,
    edge_count,
    edge_in_weight,
    edge_in_bias,
    edge_out_weight,
    edge_out_bias,
    edge_gain,
    edge_shift,
    node_in_weight,
    node_in_bias,
    node_out_weight,
    node_out_bias,
    node_gain,
    node_shift,
):
    half, node_rows = node_latents.shape
    layers = edge_in_weight.shape[0]
    coarse_rows = node_rows // 8
    patch_here = lax.axis_index(PATCH)
    patches = lax.axis_size(PATCH)
    plane = lax.axis_size(PLANE)
    columns = lax.axis_size(Z)
    scalars = jnp.stack([lax.axis_index("width"), edge_count[0]]).astype(jnp.int32)

    rows, copies = node_rows_of(node_latents, columns)
    table = exchanged(rows, copies)

    vectors = jnp.stack(
        [
            edge_in_bias,
            edge_out_bias,
            edge_gain,
            edge_shift,
            node_in_bias,
            node_out_bias,
            node_gain,
            node_shift,
        ],
        axis=1,
    )
    own = (edge_in_weight, edge_out_weight, node_in_weight, node_out_weight, vectors)
    weights = []
    for a in own:
        weights += [a, from_other(a)]

    owner = senders // node_rows
    within = senders - owner * node_rows
    place = (owner % plane) * (patches // plane) + owner // plane
    index = jnp.where(
        owner == patch_here,
        node_rows + within,
        jnp.where(
            owner == (patch_here + patches - 1) % patches,
            within,
            jnp.where(
                owner == (patch_here + 1) % patches,
                2 * node_rows + within,
                3 * node_rows + place * coarse_rows + within,
            ),
        ),
    )
    index = index.reshape(-1, 128)
    receiver = (receivers - patch_here * node_rows)[None, :]

    edges = (edge_latents, from_other(edge_latents))
    nodes = (node_latents, from_other(node_latents))
    for layer in range(layers):
        last_layer = layer == layers - 1
        ready = prepared(layer, scalars, edges, receiver, nodes, weights)
        table, ready = lax.optimization_barrier((table, ready))
        sent = gathered(index, *table)
        sent = (sent, from_other(sent))
        results = updated_graph(last_layer, scalars, sent, ready, columns)
        if not last_layer:
            edges, nodes = results[:1], results[1:2]
            table = exchanged(results[2], results[3])
    return (results[1], results[0])


def solution(mesh):
    finer = Mesh(
        mesh.devices.reshape(8, 4, 4, mesh.shape["width"]),
        (*PATCH, "width"),
    )
    in_specs = (
        P("width", PATCH),
        P("width", PATCH),
        P(PATCH),
        P(PATCH),
        P(PATCH),
        P(None, "width", None),
        P(None, "width"),
        P(None, "width", None),
        P(None, "width"),
        P(None, "width"),
        P(None, "width"),
        P(None, "width", None),
        P(None, "width"),
        P(None, "width", None),
        P(None, "width"),
        P(None, "width"),
        P(None, "width"),
    )
    out_specs = (P("width", PATCH), P("width", PATCH))
    return jax.shard_map(
        on_device, mesh=finer, in_specs=in_specs, out_specs=out_specs, check_vma=False
    )
```

```python
import functools

import jax
import jax.numpy as jnp
from jax import lax
from jax.experimental import pallas as pl
from jax.experimental.pallas import tpu as pltpu
from jax.sharding import Mesh
from jax.sharding import PartitionSpec as P

Z, Y, X = "patch_0", "patch_1", "patch_2"
PATCH = (Z, Y, X)
PLANE = (Y, X)
EPSILON = 1e-05
EDGE_BLOCK = 512
ROWS = 32
VMEM_LIMIT = 32 * 1024 * 1024


def dot(left, right, contract=((1,), (0,))):
    return lax.dot_general(left, right, (contract, ((), ())), preferred_element_type=jnp.float32)


def silu(v):
    h = 0.5 * v
    return h + h * jnp.tanh(h)


def layer_norm(values, gain, shift):
    width = values.shape[0]
    mean = jnp.sum(values, axis=0, keepdims=True) * (1.0 / width)
    square = jnp.sum(values * values, axis=0, keepdims=True) * (1.0 / width)
    return (values - mean) * lax.rsqrt(square - mean * mean + EPSILON) * gain + shift


def in_order(first, mine, other):
    return jnp.concatenate([jnp.where(first, mine, other), jnp.where(first, other, mine)], axis=0)


VMEM = pl.BlockSpec(memory_space=pltpu.VMEM)
SMEM = pl.BlockSpec(memory_space=pltpu.SMEM)
HBM = pl.BlockSpec(memory_space=pltpu.HBM)


def shape(dims, dtype=jnp.bfloat16):
    return jax.ShapeDtypeStruct(dims, dtype)


def kernel_call(body, name, out_shape, inputs, in_specs, out_specs, scratch, flops):
    inputs = [
        pltpu.with_memory_space_constraint(a, pltpu.HBM) if spec is HBM else a
        for a, spec in zip(inputs, in_specs)
    ]
    if isinstance(out_specs, list):
        out_shape = [
            pltpu.HBM(a.shape, a.dtype) if spec is HBM else a
            for a, spec in zip(out_shape, out_specs)
        ]
    return pl.pallas_call(
        body,
        in_specs=in_specs,
        out_specs=out_specs,
        out_shape=out_shape,
        scratch_shapes=scratch,
        compiler_params=pltpu.CompilerParams(vmem_limit_bytes=VMEM_LIMIT),
        cost_estimate=pl.CostEstimate(flops=flops, bytes_accessed=4 << 20, transcendentals=0),
        name=name,
    )(*inputs)


def started(pairs, sems):
    copies = [pltpu.make_async_copy(a, b, sems.at[i]) for i, (a, b) in enumerate(pairs)]
    for copy in copies:
        copy.start()
    return copies


def finish(copies):
    for copy in copies:
        copy.wait()


def held(arrays):
    return [pltpu.VMEM(a.shape, a.dtype) for a in arrays]


def columns_of(ref, start, length):
    return ref.at[:, pl.ds(start, length)]


def store_rows(mine, rows_ref, copies_ref):
    rows = mine.T
    rows_ref[...] = rows
    for i in range(copies_ref.shape[0]):
        copies_ref[i] = rows[: copies_ref.shape[1]]


def rows_kernel(nodes_ref, rows_ref, copies_ref, held_ref, sem):
    copies = started([(nodes_ref, held_ref)], sem)
    finish(copies)
    store_rows(held_ref[...], rows_ref, copies_ref)


def node_rows_of(nodes, columns):
    half, node_rows = nodes.shape
    return kernel_call(
        rows_kernel,
        "node_rows",
        [shape((node_rows, half)), shape((columns, node_rows // 8, half))],
        (nodes,),
        [HBM],
        [VMEM, VMEM],
        held([nodes]) + [pltpu.SemaphoreType.DMA((1,))],
        0,
    )


def gather_kernel(
    index_in, below_in, here_in, above_in, coarse_in, out_ref, index_ref, near_ref, coarse_ref, sems
):
    rows = here_in.shape[0]
    copies = started(
        [
            (index_in, index_ref),
            (below_in, near_ref.at[pl.ds(0, rows)]),
            (here_in, near_ref.at[pl.ds(rows, rows)]),
            (above_in, near_ref.at[pl.ds(2 * rows, rows)]),
            (coarse_in, coarse_ref),
        ],
        sems,
    )
    finish(copies[:4])
    columns = index_ref[...].T
    lane = lax.broadcasted_iota(jnp.int32, (128, 128), 1)

    def selection(start, first, length):
        blocks = []
        for k in range(start // 128, (start + EDGE_BLOCK) // 128):
            index = jnp.broadcast_to(columns[:, k : k + 1], (128, 128))
            tiles = []
            for j in range(first, first + length, 128):
                tiles.append(jnp.where(index == lane + j, 1.0, 0.0).astype(jnp.bfloat16))
            blocks.append(jnp.concatenate(tiles, axis=1))
        return jnp.concatenate(blocks, axis=0)

    for start in range(0, out_ref.shape[0], EDGE_BLOCK):
        total = dot(selection(start, 0, 3 * rows), near_ref[...])
        if start == 0:
            finish(copies[4:])
        total = total + dot(selection(start, 3 * rows, coarse_ref.shape[0]), coarse_ref[...])
        out_ref[start : start + EDGE_BLOCK, :] = total.astype(jnp.bfloat16)


def gathered(index, below, here, above, coarse):
    slots = index.size
    rows, width = here.shape
    table = 3 * rows + coarse.shape[0]
    return kernel_call(
        gather_kernel,
        "gather_senders",
        shape((slots, width)),
        (index, below, here, above, coarse),
        [HBM] * 4 + [pl.BlockSpec(memory_space=pl.ANY)],
        VMEM,
        held([index, shape((3 * rows, width)), coarse]) + [pltpu.SemaphoreType.DMA((5,))],
        2 * slots * width * table,
    )


def before_kernel(layer, n_in, scalar_ref, *refs):
    ins, outs = refs[:n_in], refs[n_in : n_in + 6]
    edge_held, node_held, hidden_weight_ref, out_held, vec_held, receiver_ref, sems = refs[
        n_in + 6 :
    ]
    before_ref, edges_ref, incidence_ref, sent_weight_ref, out_weight_ref, vectors_ref = outs
    first = scalar_ref[0] == 0
    count = scalar_ref[1]
    receiver, (wa, wb, ea, eb, vec_a, vec_b) = ins[0], ins[1:7]
    edges_in, nodes_in = ins[7 : 7 + (n_in - 7) // 2], ins[7 + (n_in - 7) // 2 :]
    half = wa.shape[1]
    width = 2 * half

    def top(ref):
        return ref.at[pl.ds(0, half)]

    def bottom(ref):
        return ref.at[pl.ds(half, half)]

    def part(ref, start):
        return ref.at[layer, :, pl.ds(start, width)]

    def both(sources, target):
        if len(sources) == 1:
            return [(sources[0], target)]
        return [(sources[0], top(target)), (sources[1], bottom(target))]

    edge_target = edge_held if layer == 0 else edges_ref
    pairs = both(nodes_in, node_held) + [(receiver, receiver_ref)]
    pairs += [(vec_a.at[layer], vec_held.at[0]), (vec_b.at[layer], vec_held.at[1])]
    for k, target in ((2, hidden_weight_ref.at[1]), (0, hidden_weight_ref.at[0])):
        pairs += both((part(wa, k * width), part(wb, k * width)), target)
    pairs += both(edges_in, edge_target)
    split = len(pairs)
    pairs += both((ea.at[layer], eb.at[layer]), out_held)
    pairs += both((part(wa, width), part(wb, width)), sent_weight_ref)
    copies = started(pairs, sems)
    finish(copies[:split])

    vec = [vec_held[0].T, vec_held[1].T]
    hidden_vec = jnp.concatenate(vec, axis=0)
    feature_vec = in_order(first, *vec)
    nodes = node_held[...]
    if layer == 0:
        nodes = in_order(first, nodes[:half], nodes[half:])
        edges_ref[...] = in_order(first, edge_held[:half, :], edge_held[half:, :])
    for i, column in enumerate((1, 2, 3)):
        vectors_ref[i] = jnp.broadcast_to(feature_vec[:, column : column + 1], (width, 128))
    vectors_ref[3] = jnp.concatenate([hidden_vec, feature_vec] + [hidden_vec] * 14, axis=1)
    slots = incidence_ref.shape[1]
    live = lax.broadcasted_iota(jnp.int32, (1, slots), 1) < count
    incidence_ref[...] = jnp.where(
        (lax.broadcasted_iota(jnp.int32, incidence_ref.shape, 0) == receiver_ref[...]) & live,
        1.0,
        0.0,
    ).astype(jnp.bfloat16)
    receiver_part = dot(hidden_weight_ref[1], nodes).astype(jnp.bfloat16)
    before = dot(hidden_weight_ref[0], edges_ref[...]) + dot(receiver_part, incidence_ref[...])
    before_ref[...] = before + hidden_vec[:, 0:1]
    finish(copies[split:])
    out_weight_ref[...] = out_held[...].T


def before_sent(layer, scalars, edges, receiver, nodes, weights):
    slots = edges[0].shape[1]
    node_rows = nodes[0].shape[1]
    width = weights[0].shape[1] * 2
    inputs = (receiver, *weights[:4], *weights[8:], *edges, *nodes)
    out_shape = [
        shape((width, slots), jnp.float32),
        shape((width, slots)),
        shape((node_rows, slots)),
        shape((width, width)),
        shape((width, width)),
        shape((4, width, 128), jnp.float32),
    ]
    edge_held = shape((width, slots) if layer == 0 else (16, 128))
    return kernel_call(
        functools.partial(before_kernel, layer, len(inputs)),
        "before_sent",
        out_shape,
        (scalars, *inputs),
        [SMEM] + [HBM] * len(inputs),
        [VMEM] * len(out_shape),
        held(
            [
                edge_held,
                shape((width, node_rows)),
                shape((2, width, width)),
                shape((width, width)),
                shape((2, *weights[8].shape[1:]), jnp.float32),
                receiver,
            ]
        )
        + [pltpu.SemaphoreType.DMA((15,))],
        2 * slots * width * (width + node_rows),
    )


def update_kernel(layer, last_layer, n_nodes, n_out, scalar_ref, *refs):
    (
        sent_a_ref,
        sent_b_ref,
        before_ref,
        edges_ref,
        incidence_ref,
        sent_weight_ref,
        out_weight_ref,
        vectors_ref,
        va,
        vb,
        oa,
        ob,
    ) = refs[:12]
    nodes_in, outs = refs[12 : 12 + n_nodes], refs[12 + n_nodes : 12 + n_nodes + n_out]
    refs = refs[12 + n_nodes + n_out :]
    held_out, (node_held, in_held, out_held, hidden_ref, mlp_ref) = refs[:n_out], refs[n_out:-2]
    in_sems, out_sems = refs[-2:]
    half = sent_a_ref.shape[1]
    width = 2 * half
    first = scalar_ref[0] == 0
    count = scalar_ref[1]

    def top(ref):
        return ref.at[pl.ds(0, half)]

    def bottom(ref):
        return ref.at[pl.ds(half, half)]

    pairs = [(va.at[layer], top(in_held)), (vb.at[layer], bottom(in_held))]
    pairs += [(oa.at[layer], top(out_held)), (ob.at[layer], bottom(out_held))]
    if n_nodes == 1:
        pairs += [(nodes_in[0], node_held)]
    else:
        pairs += [(nodes_in[0], top(node_held)), (nodes_in[1], bottom(node_held))]
    copies = started(pairs, in_sems)
    edge_out_ref, node_out_ref = held_out[:2]
    sent_out = []

    def send(source, target):
        copy = pltpu.make_async_copy(source, target, out_sems.at[len(sent_out)])
        copy.start()
        sent_out.append(copy)

    slots = edges_ref.shape[1]
    total = None
    for start in range(0, slots, EDGE_BLOCK):
        here = slice(start, start + EDGE_BLOCK)
        sent_a, sent_b = sent_a_ref[here, :], sent_b_ref[here, :]
        low = jnp.where(first, sent_a, sent_b)
        high = jnp.where(first, sent_b, sent_a)
        sent = jnp.concatenate([low, high], axis=1)
        mlp_ref[...] = dot(sent_weight_ref[...], sent, ((1,), (1,)))
        for row in range(0, width, ROWS):
            rows = slice(row, row + ROWS)
            value = silu(mlp_ref[rows, :] + before_ref[rows, here])
            hidden_ref[rows, :] = value.astype(jnp.bfloat16)
        mlp_ref[...] = dot(out_weight_ref[...], hidden_ref[...])

        def spread(index, rows):
            return jnp.concatenate([vectors_ref[index, rows, :]] * (EDGE_BLOCK // 128), axis=1)

        new_ref = hidden_ref if last_layer else columns_of(edge_out_ref, start, EDGE_BLOCK)
        sums = jnp.zeros((8, EDGE_BLOCK), jnp.float32)
        squares = jnp.zeros((8, EDGE_BLOCK), jnp.float32)
        for row in range(0, width, ROWS):
            rows = slice(row, row + ROWS)
            value = mlp_ref[rows, :] + spread(0, rows)
            mlp_ref[rows, :] = value
            sums = sums + jnp.sum(value.reshape(ROWS // 8, 8, EDGE_BLOCK), axis=0)
            squares = squares + jnp.sum((value * value).reshape(ROWS // 8, 8, EDGE_BLOCK), axis=0)
        mean = jnp.sum(sums, axis=0, keepdims=True) * (1.0 / width)
        square = jnp.sum(squares, axis=0, keepdims=True) * (1.0 / width)
        scale = lax.rsqrt(square - mean * mean + EPSILON)
        live = lax.broadcasted_iota(jnp.int32, (1, EDGE_BLOCK), 1) + start < count
        for row in range(0, width, ROWS):
            rows = slice(row, row + ROWS)
            value = (mlp_ref[rows, :] - mean) * scale * spread(1, rows) + spread(2, rows)
            value = value + edges_ref[rows, here].astype(jnp.float32)
            new_ref[rows, :] = jnp.where(live, value, 0.0).astype(jnp.bfloat16)
        updated = new_ref[...]
        part = dot(updated, incidence_ref[:, here], ((1,), (1,)))
        total = part if total is None else total + part
        if last_layer:
            edge_out_ref[:, here] = jnp.where(first, updated[:half], updated[half:])
        send(new_ref if not last_layer else columns_of(edge_out_ref, start, EDGE_BLOCK),
             columns_of(outs[0], start, EDGE_BLOCK))
    finish(copies)
    small = vectors_ref[3]
    hidden_vec, feature_vec = small[:, 0:8], small[:, 8:16]
    nodes = node_held[...]
    if n_nodes == 2:
        nodes = in_order(first, nodes[:half], nodes[half:])
    aggregate = total.astype(jnp.bfloat16)
    node_before = dot(in_held[:, :width], nodes) + dot(in_held[:, width:], aggregate)
    node_hidden = silu(node_before + hidden_vec[:, 4:5]).astype(jnp.bfloat16)
    node_mlp = dot(out_held[...].T, node_hidden) + feature_vec[:, 5:6]
    new = nodes.astype(jnp.float32) + layer_norm(
        node_mlp, feature_vec[:, 6:7], feature_vec[:, 7:8]
    )
    new = new.astype(jnp.bfloat16)
    mine = jnp.where(first, new[:half], new[half:])
    if last_layer:
        node_out_ref[...] = mine
    else:
        store_rows(mine, *held_out[2:])
        for i in (2, 3):
            send(held_out[i], outs[i])
        node_out_ref[...] = new
    send(node_out_ref, outs[1])
    finish(sent_out)


def updated_graph(layer, last_layer, scalars, sent, ready, nodes, weights, copies):
    slots = ready[0].shape[1]
    node_rows = nodes[0].shape[1]
    half = sent[0].shape[1]
    width = 2 * half
    out_width = half if last_layer else width
    out_shape = [shape((out_width, slots)), shape((out_width, node_rows))]
    if not last_layer:
        out_shape += [shape((node_rows, half)), shape((copies, node_rows // 8, half))]
    n_out = len(out_shape)
    return kernel_call(
        functools.partial(update_kernel, layer, last_layer, len(nodes), n_out),
        "update_graph",
        out_shape,
        (scalars, *sent, *ready, *weights[4:8], *nodes),
        [SMEM] + [VMEM] * (2 + len(ready)) + [HBM] * (4 + len(nodes)),
        [HBM] * n_out,
        held(out_shape)
        + held(
            [
                shape((width, node_rows)),
                shape((width, 2 * width)),
                shape((width, width)),
                shape((width, EDGE_BLOCK)),
                shape((width, EDGE_BLOCK), jnp.float32),
            ]
        )
        + [
            pltpu.SemaphoreType.DMA((6,)),
            pltpu.SemaphoreType.DMA((n_out - 1 + slots // EDGE_BLOCK,)),
        ],
        2 * slots * width * (2 * width + node_rows),
    )


def from_other(a):
    return lax.ppermute(a, "width", [(0, 1), (1, 0)])


def exchanged(rows, copies):
    size = lax.axis_size(PATCH)
    up = [(i, (i + 1) % size) for i in range(size)]
    down = [(j, i) for i, j in up]
    below, above = lax.ppermute(rows, PATCH, up), lax.ppermute(rows, PATCH, down)
    column = lax.all_to_all(copies, Z, split_axis=0, concat_axis=0, tiled=True)
    column = column.reshape(-1, rows.shape[1])
    plane = jnp.broadcast_to(column, (lax.axis_size(PLANE), *column.shape))
    coarse = lax.all_to_all(plane, PLANE, split_axis=0, concat_axis=0, tiled=True)
    return below, rows, above, coarse.reshape(-1, rows.shape[1])


def on_device(
    node_latents,
    edge_latents,
    senders,
    receivers,
    edge_count,
    edge_in_weight,
    edge_in_bias,
    edge_out_weight,
    edge_out_bias,
    edge_gain,
    edge_shift,
    node_in_weight,
    node_in_bias,
    node_out_weight,
    node_out_bias,
    node_gain,
    node_shift,
):
    half, node_rows = node_latents.shape
    layers = edge_in_weight.shape[0]
    coarse_rows = node_rows // 8
    patch_here = lax.axis_index(PATCH)
    patches = lax.axis_size(PATCH)
    plane = lax.axis_size(PLANE)
    columns = lax.axis_size(Z)
    scalars = jnp.stack([lax.axis_index("width"), edge_count[0]]).astype(jnp.int32)

    rows, copies = node_rows_of(node_latents, columns)
    table = exchanged(rows, copies)

    vectors = jnp.stack(
        [
            edge_in_bias,
            edge_out_bias,
            edge_gain,
            edge_shift,
            node_in_bias,
            node_out_bias,
            node_gain,
            node_shift,
        ],
        axis=1,
    )
    own = (edge_in_weight, edge_out_weight, node_in_weight, node_out_weight, vectors)
    weights = []
    for a in own:
        weights += [a, from_other(a)]

    owner = senders // node_rows
    within = senders - owner * node_rows
    place = (owner % plane) * (patches // plane) + owner // plane
    index = jnp.where(
        owner == patch_here,
        node_rows + within,
        jnp.where(
            owner == (patch_here + patches - 1) % patches,
            within,
            jnp.where(
                owner == (patch_here + 1) % patches,
                2 * node_rows + within,
                3 * node_rows + place * coarse_rows + within,
            ),
        ),
    )
    index = index.reshape(-1, 128)
    receiver = (receivers - patch_here * node_rows)[None, :]

    edges = (edge_latents, from_other(edge_latents))
    nodes = (node_latents, from_other(node_latents))
    table, weights, edges, nodes = lax.optimization_barrier((table, weights, edges, nodes))
    for layer in range(layers):
        last_layer = layer == layers - 1
        sent = gathered(index, *table)
        sent = (sent, from_other(sent))
        ready = before_sent(layer, scalars, edges, receiver, nodes, weights)
        results = updated_graph(
            layer, last_layer, scalars, sent, ready, nodes, weights, columns
        )
        if not last_layer:
            edges, nodes = results[:1], results[1:2]
            table = exchanged(results[2], results[3])
    return (results[1], results[0])


def solution(mesh):
    finer = Mesh(
        mesh.devices.reshape(8, 4, 4, mesh.shape["width"]),
        (*PATCH, "width"),
    )
    in_specs = (
        P("width", PATCH),
        P("width", PATCH),
        P(PATCH),
        P(PATCH),
        P(PATCH),
        P(None, "width", None),
        P(None, "width"),
        P(None, "width", None),
        P(None, "width"),
        P(None, "width"),
        P(None, "width"),
        P(None, "width", None),
        P(None, "width"),
        P(None, "width", None),
        P(None, "width"),
        P(None, "width"),
        P(None, "width"),
    )
    out_specs = (P("width", PATCH), P("width", PATCH))
    return jax.shard_map(
        on_device, mesh=finer, in_specs=in_specs, out_specs=out_specs, check_vma=False
    )
```

```python
import functools

import jax
import jax.numpy as jnp
from jax import lax
from jax.experimental import pallas as pl
from jax.experimental.pallas import tpu as pltpu
from jax.sharding import Mesh
from jax.sharding import PartitionSpec as P

Z, Y, X = "patch_0", "patch_1", "patch_2"
PATCH = (Z, Y, X)
PLANE = (Y, X)
EPSILON = 1e-05
EDGE_BLOCK = 512
UPDATE_BLOCK = 1024
ROWS = 32
VMEM_LIMIT = 32 * 1024 * 1024


def dot(left, right, contract=((1,), (0,))):
    return lax.dot_general(left, right, (contract, ((), ())), preferred_element_type=jnp.float32)


def silu(v):
    h = 0.5 * v
    return h + h * jnp.tanh(h)


def layer_norm(values, gain, shift):
    width = values.shape[0]
    mean = jnp.sum(values, axis=0, keepdims=True) * (1.0 / width)
    square = jnp.sum(values * values, axis=0, keepdims=True) * (1.0 / width)
    return (values - mean) * lax.rsqrt(square - mean * mean + EPSILON) * gain + shift


def in_order(first, mine, other):
    return jnp.concatenate([jnp.where(first, mine, other), jnp.where(first, other, mine)], axis=0)


VMEM = pl.BlockSpec(memory_space=pltpu.VMEM)
SMEM = pl.BlockSpec(memory_space=pltpu.SMEM)
HBM = pl.BlockSpec(memory_space=pltpu.HBM)


def shape(dims, dtype=jnp.bfloat16):
    return jax.ShapeDtypeStruct(dims, dtype)


def kernel_call(body, name, out_shape, inputs, in_specs, out_specs, scratch, flops):
    inputs = [
        pltpu.with_memory_space_constraint(a, pltpu.HBM) if spec is HBM else a
        for a, spec in zip(inputs, in_specs)
    ]
    if isinstance(out_specs, list):
        out_shape = [
            pltpu.HBM(a.shape, a.dtype) if spec is HBM else a
            for a, spec in zip(out_shape, out_specs)
        ]
    return pl.pallas_call(
        body,
        in_specs=in_specs,
        out_specs=out_specs,
        out_shape=out_shape,
        scratch_shapes=scratch,
        compiler_params=pltpu.CompilerParams(vmem_limit_bytes=VMEM_LIMIT),
        cost_estimate=pl.CostEstimate(flops=flops, bytes_accessed=4 << 20, transcendentals=0),
        name=name,
    )(*inputs)


def started(pairs, sems):
    copies = [pltpu.make_async_copy(a, b, sems.at[i]) for i, (a, b) in enumerate(pairs)]
    for copy in copies:
        copy.start()
    return copies


def finish(copies):
    for copy in copies:
        copy.wait()


def held(arrays):
    return [pltpu.VMEM(a.shape, a.dtype) for a in arrays]


def columns_of(ref, start, length):
    return ref.at[:, pl.ds(start, length)]


def store_rows(mine, rows_ref, copies_ref):
    rows = mine.T
    rows_ref[...] = rows
    for i in range(copies_ref.shape[0]):
        copies_ref[i] = rows[: copies_ref.shape[1]]


def rows_kernel(nodes_ref, rows_ref, copies_ref, held_ref, sem):
    copies = started([(nodes_ref, held_ref)], sem)
    finish(copies)
    store_rows(held_ref[...], rows_ref, copies_ref)


def node_rows_of(nodes, columns):
    half, node_rows = nodes.shape
    return kernel_call(
        rows_kernel,
        "node_rows",
        [shape((node_rows, half)), shape((columns, node_rows // 8, half))],
        (nodes,),
        [HBM],
        [VMEM, VMEM],
        held([nodes]) + [pltpu.SemaphoreType.DMA((1,))],
        0,
    )


def gather_kernel(n, index_in, below_in, here_in, above_in, coarse_in, *refs):
    ready_in, out_ref, ready_out = refs[:n], refs[n], refs[n + 1 : 2 * n + 1]
    index_ref, near_ref, coarse_ref, sems, ready_sems = refs[2 * n + 1 :]
    rows = here_in.shape[0]
    copies = started(
        [
            (index_in, index_ref),
            (below_in, near_ref.at[pl.ds(0, rows)]),
            (here_in, near_ref.at[pl.ds(rows, rows)]),
            (above_in, near_ref.at[pl.ds(2 * rows, rows)]),
            (coarse_in, coarse_ref),
        ],
        sems,
    )
    ready_copies = started(list(zip(ready_in, ready_out)), ready_sems)
    finish(copies[:4])
    columns = index_ref[...].T
    lane = lax.broadcasted_iota(jnp.int32, (128, 128), 1)

    def selection(start, first, length):
        blocks = []
        for k in range(start // 128, (start + EDGE_BLOCK) // 128):
            index = jnp.broadcast_to(columns[:, k : k + 1], (128, 128))
            tiles = []
            for j in range(first, first + length, 128):
                tiles.append(jnp.where(index == lane + j, 1.0, 0.0).astype(jnp.bfloat16))
            blocks.append(jnp.concatenate(tiles, axis=1))
        return jnp.concatenate(blocks, axis=0)

    for start in range(0, out_ref.shape[0], EDGE_BLOCK):
        total = dot(selection(start, 0, 3 * rows), near_ref[...])
        if start == 0:
            finish(copies[4:])
        total = total + dot(selection(start, 3 * rows, coarse_ref.shape[0]), coarse_ref[...])
        out_ref[start : start + EDGE_BLOCK, :] = total.astype(jnp.bfloat16)
    finish(ready_copies)


def gathered(ready, index, below, here, above, coarse):
    slots = index.size
    rows, width = here.shape
    table = 3 * rows + coarse.shape[0]
    n = len(ready)
    return kernel_call(
        functools.partial(gather_kernel, n),
        "gather_senders",
        [shape((slots, width)), *[shape(a.shape, a.dtype) for a in ready]],
        (index, below, here, above, coarse, *ready),
        [HBM] * 4 + [pl.BlockSpec(memory_space=pl.ANY)] + [HBM] * n,
        [VMEM] * (1 + n),
        held([index, shape((3 * rows, width)), coarse])
        + [pltpu.SemaphoreType.DMA((5,)), pltpu.SemaphoreType.DMA((n,))],
        2 * slots * width * table,
    )


def prepare_kernel(layer, n_in, n_out, scalar_ref, *refs):
    ins, outs, refs = refs[:n_in], refs[n_in : n_in + n_out], refs[n_in + n_out :]
    held_out, refs = refs[:n_out], refs[n_out:]
    edge_held, node_held, hidden_weight_ref, out_held, vec_held, receiver_ref = refs[:6]
    in_sems, out_sems = refs[6:]
    before_ref, weights_ref, incidence_ref, vectors_ref = held_out[:4]
    first = scalar_ref[0] == 0
    count = scalar_ref[1]
    receiver, (wa, wb, ea, eb, va, vb, oa, ob, vec_a, vec_b) = ins[0], ins[1:11]
    edges_in, nodes_in = ins[11 : 11 + (n_in - 11) // 2], ins[11 + (n_in - 11) // 2 :]
    half = wa.shape[1]
    width = 2 * half

    def part(ref, start):
        return ref.at[layer, :, pl.ds(start, width)]

    def both(sources, target):
        if len(sources) == 1:
            return [(sources[0], target)]
        halves = (target.at[pl.ds(0, half)], target.at[pl.ds(half, half)])
        return list(zip(sources, halves))

    pairs = both(nodes_in, node_held) + [(receiver, receiver_ref)]
    pairs += [(vec_a.at[layer], vec_held.at[0]), (vec_b.at[layer], vec_held.at[1])]
    for k, target in ((2, hidden_weight_ref.at[1]), (0, hidden_weight_ref.at[0])):
        pairs += both((part(wa, k * width), part(wb, k * width)), target)
    pairs += both(edges_in, edge_held)
    pairs += both((ea.at[layer], eb.at[layer]), out_held.at[0])
    pairs += both((oa.at[layer], ob.at[layer]), out_held.at[1])
    pairs += both((part(wa, width), part(wb, width)), weights_ref.at[0])
    for k in (0, 1):
        pairs += both((part(va, k * width), part(vb, k * width)), weights_ref.at[2 + k])
    finish(started(pairs, in_sems))
    sent = [pltpu.make_async_copy(held_out[i], outs[i], out_sems.at[i]) for i in range(n_out)]

    vec = [vec_held[0].T, vec_held[1].T]
    hidden_vec = jnp.concatenate(vec, axis=0)
    feature_vec = in_order(first, *vec)
    nodes = node_held[...]
    edges = edge_held[...]
    if layer == 0:
        nodes = in_order(first, nodes[:half], nodes[half:])
        edges = in_order(first, edges[:half], edges[half:])
        held_out[4][...] = edges
        sent[4].start()
        held_out[5][...] = nodes
        sent[5].start()
    weights_ref[1] = out_held[0].T
    weights_ref[4] = out_held[1].T
    sent[1].start()
    vectors_ref[...] = jnp.concatenate([hidden_vec, feature_vec] + [hidden_vec] * 14, axis=1)
    sent[3].start()
    slots = incidence_ref.shape[1]
    live = lax.broadcasted_iota(jnp.int32, (1, slots), 1) < count
    incidence_ref[...] = jnp.where(
        (lax.broadcasted_iota(jnp.int32, incidence_ref.shape, 0) == receiver_ref[...]) & live,
        1.0,
        0.0,
    ).astype(jnp.bfloat16)
    sent[2].start()
    receiver_part = dot(hidden_weight_ref[1], nodes).astype(jnp.bfloat16)
    before = dot(hidden_weight_ref[0], edges) + dot(receiver_part, incidence_ref[...])
    before_ref[...] = before + hidden_vec[:, 0:1]
    sent[0].start()
    finish(sent)


def prepared(layer, scalars, edges, receiver, nodes, weights):
    slots = edges[0].shape[1]
    node_rows = nodes[0].shape[1]
    width = weights[0].shape[1] * 2
    inputs = (receiver, *weights, *edges, *nodes)
    out_shape = [
        shape((width, slots), jnp.float32),
        shape((5, width, width)),
        shape((node_rows, slots)),
        shape((width, 128), jnp.float32),
    ]
    if layer == 0:
        out_shape += [shape((width, slots)), shape((width, node_rows))]
    n_in, n_out = len(inputs), len(out_shape)
    ready = kernel_call(
        functools.partial(prepare_kernel, layer, n_in, n_out),
        "prepare_layer",
        out_shape,
        (scalars, *inputs),
        [SMEM] + [HBM] * n_in,
        [HBM] * n_out,
        held(
            [
                *out_shape,
                shape((width, slots)),
                shape((width, node_rows)),
                shape((2, width, width)),
                shape((2, width, width)),
                shape((2, *weights[8].shape[1:]), jnp.float32),
                receiver,
            ]
        )
        + [pltpu.SemaphoreType.DMA((21,)), pltpu.SemaphoreType.DMA((n_out,))],
        2 * slots * width * (width + node_rows),
    )
    if layer == 0:
        return ready
    return (*ready, *edges, *nodes)


def update_kernel(last_layer, n_out, scalar_ref, *refs):
    sent_a_ref, sent_b_ref, before_ref, weights_ref, incidence_ref, small_ref = refs[:6]
    edges_ref, nodes_ref, outs, refs = refs[6], refs[7], refs[8 : 8 + n_out], refs[8 + n_out :]
    edge_out_ref, node_out_ref, hidden_ref, mlp_ref, vectors_ref, out_sems = refs
    half = sent_a_ref.shape[1]
    width = 2 * half
    first = scalar_ref[0] == 0
    count = scalar_ref[1]
    sent_out = []

    def send(source, target):
        copy = pltpu.make_async_copy(source, target, out_sems.at[len(sent_out)])
        copy.start()
        sent_out.append(copy)

    small = small_ref[...]
    hidden_vec, feature_vec = small[:, 0:8], small[:, 8:16]
    for i, column in enumerate((1, 2, 3)):
        vectors_ref[i] = jnp.broadcast_to(feature_vec[:, column : column + 1], (width, 128))

    def spread(index, rows):
        return jnp.concatenate([vectors_ref[index, rows, :]] * (UPDATE_BLOCK // 128), axis=1)

    slots = edges_ref.shape[1]
    total = None
    for start in range(0, slots, UPDATE_BLOCK):
        here = slice(start, start + UPDATE_BLOCK)
        sent_a, sent_b = sent_a_ref[here, :], sent_b_ref[here, :]
        low = jnp.where(first, sent_a, sent_b)
        high = jnp.where(first, sent_b, sent_a)
        sent = jnp.concatenate([low, high], axis=1)
        mlp_ref[...] = dot(weights_ref[0], sent, ((1,), (1,)))
        for row in range(0, width, ROWS):
            rows = slice(row, row + ROWS)
            value = silu(mlp_ref[rows, :] + before_ref[rows, here])
            hidden_ref[rows, :] = value.astype(jnp.bfloat16)
        mlp_ref[...] = dot(weights_ref[1], hidden_ref[...])
        new_ref = hidden_ref if last_layer else columns_of(edge_out_ref, start, UPDATE_BLOCK)
        sums = jnp.zeros((8, UPDATE_BLOCK), jnp.float32)
        squares = jnp.zeros((8, UPDATE_BLOCK), jnp.float32)
        for row in range(0, width, ROWS):
            rows = slice(row, row + ROWS)
            value = mlp_ref[rows, :] + spread(0, rows)
            mlp_ref[rows, :] = value
            sums = sums + jnp.sum(value.reshape(ROWS // 8, 8, UPDATE_BLOCK), axis=0)
            squares = squares + jnp.sum((value * value).reshape(ROWS // 8, 8, UPDATE_BLOCK), axis=0)
        mean = jnp.sum(sums, axis=0, keepdims=True) * (1.0 / width)
        square = jnp.sum(squares, axis=0, keepdims=True) * (1.0 / width)
        scale = lax.rsqrt(square - mean * mean + EPSILON)
        live = lax.broadcasted_iota(jnp.int32, (1, UPDATE_BLOCK), 1) + start < count
        for row in range(0, width, ROWS):
            rows = slice(row, row + ROWS)
            value = (mlp_ref[rows, :] - mean) * scale * spread(1, rows) + spread(2, rows)
            value = value + edges_ref[rows, here].astype(jnp.float32)
            new_ref[rows, :] = jnp.where(live, value, 0.0).astype(jnp.bfloat16)
        updated = new_ref[...]
        part = dot(updated, incidence_ref[:, here], ((1,), (1,)))
        total = part if total is None else total + part
        if last_layer:
            edge_out_ref[:, here] = jnp.where(first, updated[:half], updated[half:])
        send(
            columns_of(edge_out_ref, start, UPDATE_BLOCK), columns_of(outs[0], start, UPDATE_BLOCK)
        )
    nodes = nodes_ref[...]
    aggregate = total.astype(jnp.bfloat16)
    node_before = dot(weights_ref[2], nodes) + dot(weights_ref[3], aggregate)
    node_hidden = silu(node_before + hidden_vec[:, 4:5]).astype(jnp.bfloat16)
    node_mlp = dot(weights_ref[4], node_hidden) + feature_vec[:, 5:6]
    new = nodes.astype(jnp.float32) + layer_norm(
        node_mlp, feature_vec[:, 6:7], feature_vec[:, 7:8]
    )
    new = new.astype(jnp.bfloat16)
    mine = jnp.where(first, new[:half], new[half:])
    if last_layer:
        node_out_ref[...] = mine
        send(node_out_ref, outs[1])
    else:
        node_out_ref[...] = new
        send(node_out_ref, outs[1])
        store_rows(mine, *outs[2:])
    finish(sent_out)


def updated_graph(last_layer, scalars, sent, ready, copies):
    slots = ready[0].shape[1]
    node_rows = ready[5].shape[1]
    half = sent[0].shape[1]
    width = 2 * half
    out_width = half if last_layer else width
    out_shape = [shape((out_width, slots)), shape((out_width, node_rows))]
    out_specs = [HBM, HBM]
    if not last_layer:
        out_shape += [shape((node_rows, half)), shape((copies, node_rows // 8, half))]
        out_specs = [HBM, HBM, VMEM, VMEM]
    n_out = len(out_shape)
    return kernel_call(
        functools.partial(update_kernel, last_layer, n_out),
        "update_graph",
        out_shape,
        (scalars, *sent, *ready),
        [SMEM] + [VMEM] * (2 + len(ready)),
        out_specs,
        held(
            [
                *out_shape[:2],
                shape((width, UPDATE_BLOCK)),
                shape((width, UPDATE_BLOCK), jnp.float32),
                shape((3, width, 128), jnp.float32),
            ]
        )
        + [pltpu.SemaphoreType.DMA((slots // UPDATE_BLOCK + 1,))],
        2 * slots * width * (2 * width + node_rows),
    )


def from_other(a):
    return lax.ppermute(a, "width", [(0, 1), (1, 0)])


def exchanged(rows, copies):
    size = lax.axis_size(PATCH)
    up = [(i, (i + 1) % size) for i in range(size)]
    down = [(j, i) for i, j in up]
    below, above = lax.ppermute(rows, PATCH, up), lax.ppermute(rows, PATCH, down)
    column = lax.all_to_all(copies, Z, split_axis=0, concat_axis=0, tiled=True)
    column = column.reshape(-1, rows.shape[1])
    plane = jnp.broadcast_to(column, (lax.axis_size(PLANE), *column.shape))
    coarse = lax.all_to_all(plane, PLANE, split_axis=0, concat_axis=0, tiled=True)
    return below, rows, above, coarse.reshape(-1, rows.shape[1])


def on_device(
    node_latents,
    edge_latents,
    senders,
    receivers,
    edge_count,
    edge_in_weight,
    edge_in_bias,
    edge_out_weight,
    edge_out_bias,
    edge_gain,
    edge_shift,
    node_in_weight,
    node_in_bias,
    node_out_weight,
    node_out_bias,
    node_gain,
    node_shift,
):
    half, node_rows = node_latents.shape
    layers = edge_in_weight.shape[0]
    coarse_rows = node_rows // 8
    patch_here = lax.axis_index(PATCH)
    patches = lax.axis_size(PATCH)
    plane = lax.axis_size(PLANE)
    columns = lax.axis_size(Z)
    scalars = jnp.stack([lax.axis_index("width"), edge_count[0]]).astype(jnp.int32)

    rows, copies = node_rows_of(node_latents, columns)
    table = exchanged(rows, copies)

    vectors = jnp.stack(
        [
            edge_in_bias,
            edge_out_bias,
            edge_gain,
            edge_shift,
            node_in_bias,
            node_out_bias,
            node_gain,
            node_shift,
        ],
        axis=1,
    )
    own = (edge_in_weight, edge_out_weight, node_in_weight, node_out_weight, vectors)
    weights = []
    for a in own:
        weights += [a, from_other(a)]

    owner = senders // node_rows
    within = senders - owner * node_rows
    place = (owner % plane) * (patches // plane) + owner // plane
    index = jnp.where(
        owner == patch_here,
        node_rows + within,
        jnp.where(
            owner == (patch_here + patches - 1) % patches,
            within,
            jnp.where(
                owner == (patch_here + 1) % patches,
                2 * node_rows + within,
                3 * node_rows + place * coarse_rows + within,
            ),
        ),
    )
    index = index.reshape(-1, 128)
    receiver = (receivers - patch_here * node_rows)[None, :]

    edges = (edge_latents, from_other(edge_latents))
    nodes = (node_latents, from_other(node_latents))
    table, weights, edges, nodes = lax.optimization_barrier((table, weights, edges, nodes))
    for layer in range(layers):
        last_layer = layer == layers - 1
        ready = prepared(layer, scalars, edges, receiver, nodes, weights)
        table, ready = lax.optimization_barrier((table, ready))
        sent, *ready = gathered(ready, index, *table)
        sent = (sent, from_other(sent))
        results = updated_graph(last_layer, scalars, sent, ready, columns)
        if not last_layer:
            edges, nodes = results[:1], results[1:2]
            table = exchanged(results[2], results[3])
    return (results[1], results[0])


def solution(mesh):
    finer = Mesh(
        mesh.devices.reshape(8, 4, 4, mesh.shape["width"]),
        (*PATCH, "width"),
    )
    in_specs = (
        P("width", PATCH),
        P("width", PATCH),
        P(PATCH),
        P(PATCH),
        P(PATCH),
        P(None, "width", None),
        P(None, "width"),
        P(None, "width", None),
        P(None, "width"),
        P(None, "width"),
        P(None, "width"),
        P(None, "width", None),
        P(None, "width"),
        P(None, "width", None),
        P(None, "width"),
        P(None, "width"),
        P(None, "width"),
    )
    out_specs = (P("width", PATCH), P("width", PATCH))
    return jax.shard_map(
        on_device, mesh=finer, in_specs=in_specs, out_specs=out_specs, check_vma=False
    )
```

```python
import functools

import jax
import jax.numpy as jnp
from jax import lax
from jax.experimental import pallas as pl
from jax.experimental.pallas import tpu as pltpu
from jax.sharding import Mesh
from jax.sharding import PartitionSpec as P

Z, Y, X = "patch_0", "patch_1", "patch_2"
PATCH = (Z, Y, X)
PLANE = (Y, X)
EPSILON = 1e-05
EDGE_BLOCK = 512
UPDATE_BLOCK = 1024
ROWS = 32
VMEM_LIMIT = 32 * 1024 * 1024


def dot(left, right, contract=((1,), (0,))):
    return lax.dot_general(left, right, (contract, ((), ())), preferred_element_type=jnp.float32)


def silu(v):
    h = 0.5 * v
    return h + h * jnp.tanh(h)


def layer_norm(values, gain, shift):
    width = values.shape[0]
    mean = jnp.sum(values, axis=0, keepdims=True) * (1.0 / width)
    square = jnp.sum(values * values, axis=0, keepdims=True) * (1.0 / width)
    return (values - mean) * lax.rsqrt(square - mean * mean + EPSILON) * gain + shift


def in_order(first, mine, other):
    return jnp.concatenate([jnp.where(first, mine, other), jnp.where(first, other, mine)], axis=0)


VMEM = pl.BlockSpec(memory_space=pltpu.VMEM)
SMEM = pl.BlockSpec(memory_space=pltpu.SMEM)
HBM = pl.BlockSpec(memory_space=pltpu.HBM)


def shape(dims, dtype=jnp.bfloat16):
    return jax.ShapeDtypeStruct(dims, dtype)


def kernel_call(body, name, out_shape, inputs, in_specs, out_specs, scratch, flops):
    inputs = [
        pltpu.with_memory_space_constraint(a, pltpu.HBM) if spec is HBM else a
        for a, spec in zip(inputs, in_specs)
    ]
    if isinstance(out_specs, list):
        out_shape = [
            pltpu.HBM(a.shape, a.dtype) if spec is HBM else a
            for a, spec in zip(out_shape, out_specs)
        ]
    return pl.pallas_call(
        body,
        in_specs=in_specs,
        out_specs=out_specs,
        out_shape=out_shape,
        scratch_shapes=scratch,
        compiler_params=pltpu.CompilerParams(vmem_limit_bytes=VMEM_LIMIT),
        cost_estimate=pl.CostEstimate(flops=flops, bytes_accessed=4 << 20, transcendentals=0),
        name=name,
    )(*inputs)


def started(pairs, sems):
    copies = [pltpu.make_async_copy(a, b, sems.at[i]) for i, (a, b) in enumerate(pairs)]
    for copy in copies:
        copy.start()
    return copies


def finish(copies):
    for copy in copies:
        copy.wait()


def held(arrays):
    return [pltpu.VMEM(a.shape, a.dtype) for a in arrays]


def columns_of(ref, start, length):
    return ref.at[:, pl.ds(start, length)]


def store_rows(mine, rows_ref, copies_ref):
    rows = mine.T
    rows_ref[...] = rows
    for i in range(copies_ref.shape[0]):
        copies_ref[i] = rows[: copies_ref.shape[1]]


def rows_kernel(nodes_ref, rows_ref, copies_ref, held_ref, sem):
    copies = started([(nodes_ref, held_ref)], sem)
    finish(copies)
    store_rows(held_ref[...], rows_ref, copies_ref)


def node_rows_of(nodes, columns):
    half, node_rows = nodes.shape
    return kernel_call(
        rows_kernel,
        "node_rows",
        [shape((node_rows, half)), shape((columns, node_rows // 8, half))],
        (nodes,),
        [HBM],
        [VMEM, VMEM],
        held([nodes]) + [pltpu.SemaphoreType.DMA((1,))],
        0,
    )


def gather_kernel(n, index_in, below_in, here_in, above_in, coarse_ref, *refs):
    ready_in, out_ref, ready_out = refs[:n], refs[n], refs[n + 1 : 2 * n + 1]
    index_ref, near_ref, sems, ready_sems = refs[2 * n + 1 :]
    rows = here_in.shape[0]
    copies = started(
        [
            (index_in, index_ref),
            (below_in, near_ref.at[pl.ds(0, rows)]),
            (here_in, near_ref.at[pl.ds(rows, rows)]),
            (above_in, near_ref.at[pl.ds(2 * rows, rows)]),
        ],
        sems,
    )
    ready_copies = started(list(zip(ready_in, ready_out)), ready_sems)
    finish(copies[:1])
    columns = index_ref[...].T
    lane = lax.broadcasted_iota(jnp.int32, (128, 128), 1)

    def selection(start, first, length):
        blocks = []
        for k in range(start // 128, (start + EDGE_BLOCK) // 128):
            index = jnp.broadcast_to(columns[:, k : k + 1], (128, 128))
            tiles = []
            for j in range(first, first + length, 128):
                tiles.append(jnp.where(index == lane + j, 1.0, 0.0).astype(jnp.bfloat16))
            blocks.append(jnp.concatenate(tiles, axis=1))
        return jnp.concatenate(blocks, axis=0)

    for start in range(0, out_ref.shape[0], EDGE_BLOCK):
        total = dot(selection(start, 3 * rows, coarse_ref.shape[0]), coarse_ref[...])
        if start == 0:
            finish(copies[1:])
        total = total + dot(selection(start, 0, 3 * rows), near_ref[...])
        out_ref[start : start + EDGE_BLOCK, :] = total.astype(jnp.bfloat16)
    finish(ready_copies)


def gathered(ready, index, below, here, above, coarse):
    slots = index.size
    rows, width = here.shape
    table = 3 * rows + coarse.shape[0]
    n = len(ready)
    return kernel_call(
        functools.partial(gather_kernel, n),
        "gather_senders",
        [shape((slots, width)), *[shape(a.shape, a.dtype) for a in ready]],
        (index, below, here, above, coarse, *ready),
        [HBM] * 4 + [VMEM] + [HBM] * n,
        [VMEM] * (1 + n),
        held([index, shape((3 * rows, width))])
        + [pltpu.SemaphoreType.DMA((4,)), pltpu.SemaphoreType.DMA((n,))],
        2 * slots * width * table,
    )


def prepare_kernel(layer, n_in, n_out, scalar_ref, *refs):
    ins, outs, refs = refs[:n_in], refs[n_in : n_in + n_out], refs[n_in + n_out :]
    held_out, refs = refs[:n_out], refs[n_out:]
    edge_held, node_held, hidden_weight_ref, out_held, vec_held, receiver_ref = refs[:6]
    in_sems, out_sems = refs[6:]
    before_ref, weights_ref, incidence_ref, vectors_ref = held_out[:4]
    first = scalar_ref[0] == 0
    count = scalar_ref[1]
    receiver, (wa, wb, ea, eb, va, vb, oa, ob, vec_a, vec_b) = ins[0], ins[1:11]
    edges_in, nodes_in = ins[11 : 11 + (n_in - 11) // 2], ins[11 + (n_in - 11) // 2 :]
    half = wa.shape[1]
    width = 2 * half

    def part(ref, start):
        return ref.at[layer, :, pl.ds(start, width)]

    def both(sources, target):
        if len(sources) == 1:
            return [(sources[0], target)]
        halves = (target.at[pl.ds(0, half)], target.at[pl.ds(half, half)])
        return list(zip(sources, halves))

    pairs = both(nodes_in, node_held) + [(receiver, receiver_ref)]
    pairs += [(vec_a.at[layer], vec_held.at[0]), (vec_b.at[layer], vec_held.at[1])]
    for k, target in ((2, hidden_weight_ref.at[1]), (0, hidden_weight_ref.at[0])):
        pairs += both((part(wa, k * width), part(wb, k * width)), target)
    pairs += both(edges_in, edge_held)
    pairs += both((ea.at[layer], eb.at[layer]), out_held.at[0])
    pairs += both((oa.at[layer], ob.at[layer]), out_held.at[1])
    pairs += both((part(wa, width), part(wb, width)), weights_ref.at[0])
    for k in (0, 1):
        pairs += both((part(va, k * width), part(vb, k * width)), weights_ref.at[2 + k])
    finish(started(pairs, in_sems))
    sent = [pltpu.make_async_copy(held_out[i], outs[i], out_sems.at[i]) for i in range(n_out)]

    vec = [vec_held[0].T, vec_held[1].T]
    hidden_vec = jnp.concatenate(vec, axis=0)
    feature_vec = in_order(first, *vec)
    nodes = node_held[...]
    edges = edge_held[...]
    if layer == 0:
        nodes = in_order(first, nodes[:half], nodes[half:])
        edges = in_order(first, edges[:half], edges[half:])
        held_out[4][...] = edges
        sent[4].start()
        held_out[5][...] = nodes
        sent[5].start()
    weights_ref[1] = out_held[0].T
    weights_ref[4] = out_held[1].T
    sent[1].start()
    vectors_ref[...] = jnp.concatenate([hidden_vec, feature_vec] + [hidden_vec] * 14, axis=1)
    sent[3].start()
    slots = incidence_ref.shape[1]
    live = lax.broadcasted_iota(jnp.int32, (1, slots), 1) < count
    incidence_ref[...] = jnp.where(
        (lax.broadcasted_iota(jnp.int32, incidence_ref.shape, 0) == receiver_ref[...]) & live,
        1.0,
        0.0,
    ).astype(jnp.bfloat16)
    sent[2].start()
    receiver_part = dot(hidden_weight_ref[1], nodes).astype(jnp.bfloat16)
    before = dot(hidden_weight_ref[0], edges) + dot(receiver_part, incidence_ref[...])
    before_ref[...] = before + hidden_vec[:, 0:1]
    sent[0].start()
    finish(sent)


def prepared(layer, scalars, edges, receiver, nodes, weights):
    slots = edges[0].shape[1]
    node_rows = nodes[0].shape[1]
    width = weights[0].shape[1] * 2
    inputs = (receiver, *weights, *edges, *nodes)
    out_shape = [
        shape((width, slots), jnp.float32),
        shape((5, width, width)),
        shape((node_rows, slots)),
        shape((width, 128), jnp.float32),
    ]
    if layer == 0:
        out_shape += [shape((width, slots)), shape((width, node_rows))]
    n_in, n_out = len(inputs), len(out_shape)
    ready = kernel_call(
        functools.partial(prepare_kernel, layer, n_in, n_out),
        "prepare_layer",
        out_shape,
        (scalars, *inputs),
        [SMEM] + [HBM] * n_in,
        [HBM] * n_out,
        held(
            [
                *out_shape,
                shape((width, slots)),
                shape((width, node_rows)),
                shape((2, width, width)),
                shape((2, width, width)),
                shape((2, *weights[8].shape[1:]), jnp.float32),
                receiver,
            ]
        )
        + [pltpu.SemaphoreType.DMA((21,)), pltpu.SemaphoreType.DMA((n_out,))],
        2 * slots * width * (width + node_rows),
    )
    if layer == 0:
        return ready
    return (*ready, *edges, *nodes)


def update_kernel(last_layer, n_out, scalar_ref, *refs):
    sent_a_ref, sent_b_ref, before_ref, weights_ref, incidence_ref, small_ref = refs[:6]
    edges_ref, nodes_ref, outs, refs = refs[6], refs[7], refs[8 : 8 + n_out], refs[8 + n_out :]
    edge_out_ref, node_out_ref, hidden_ref, mlp_ref, vectors_ref, out_sems = refs
    half = sent_a_ref.shape[1]
    width = 2 * half
    first = scalar_ref[0] == 0
    count = scalar_ref[1]
    sent_out = []

    def send(source, target):
        copy = pltpu.make_async_copy(source, target, out_sems.at[len(sent_out)])
        copy.start()
        sent_out.append(copy)

    small = small_ref[...]
    hidden_vec, feature_vec = small[:, 0:8], small[:, 8:16]
    for i, column in enumerate((1, 2, 3)):
        vectors_ref[i] = jnp.broadcast_to(feature_vec[:, column : column + 1], (width, 128))

    def spread(index, rows):
        return jnp.concatenate([vectors_ref[index, rows, :]] * (UPDATE_BLOCK // 128), axis=1)

    slots = edges_ref.shape[1]
    total = None
    for start in range(0, slots, UPDATE_BLOCK):
        here = slice(start, start + UPDATE_BLOCK)
        sent_a, sent_b = sent_a_ref[here, :], sent_b_ref[here, :]
        low = jnp.where(first, sent_a, sent_b)
        high = jnp.where(first, sent_b, sent_a)
        sent = jnp.concatenate([low, high], axis=1)
        mlp_ref[...] = dot(weights_ref[0], sent, ((1,), (1,)))
        for row in range(0, width, ROWS):
            rows = slice(row, row + ROWS)
            value = silu(mlp_ref[rows, :] + before_ref[rows, here])
            hidden_ref[rows, :] = value.astype(jnp.bfloat16)
        mlp_ref[...] = dot(weights_ref[1], hidden_ref[...])
        new_ref = hidden_ref if last_layer else columns_of(edge_out_ref, start, UPDATE_BLOCK)
        sums = jnp.zeros((8, UPDATE_BLOCK), jnp.float32)
        squares = jnp.zeros((8, UPDATE_BLOCK), jnp.float32)
        for row in range(0, width, ROWS):
            rows = slice(row, row + ROWS)
            value = mlp_ref[rows, :] + spread(0, rows)
            mlp_ref[rows, :] = value
            sums = sums + jnp.sum(value.reshape(ROWS // 8, 8, UPDATE_BLOCK), axis=0)
            squares = squares + jnp.sum((value * value).reshape(ROWS // 8, 8, UPDATE_BLOCK), axis=0)
        mean = jnp.sum(sums, axis=0, keepdims=True) * (1.0 / width)
        square = jnp.sum(squares, axis=0, keepdims=True) * (1.0 / width)
        scale = lax.rsqrt(square - mean * mean + EPSILON)
        live = lax.broadcasted_iota(jnp.int32, (1, UPDATE_BLOCK), 1) + start < count
        for row in range(0, width, ROWS):
            rows = slice(row, row + ROWS)
            value = (mlp_ref[rows, :] - mean) * scale * spread(1, rows) + spread(2, rows)
            value = value + edges_ref[rows, here].astype(jnp.float32)
            new_ref[rows, :] = jnp.where(live, value, 0.0).astype(jnp.bfloat16)
        updated = new_ref[...]
        part = dot(updated, incidence_ref[:, here], ((1,), (1,)))
        total = part if total is None else total + part
        if last_layer:
            edge_out_ref[:, here] = jnp.where(first, updated[:half], updated[half:])
        send(
            columns_of(edge_out_ref, start, UPDATE_BLOCK), columns_of(outs[0], start, UPDATE_BLOCK)
        )
    nodes = nodes_ref[...]
    aggregate = total.astype(jnp.bfloat16)
    node_before = dot(weights_ref[2], nodes) + dot(weights_ref[3], aggregate)
    node_hidden = silu(node_before + hidden_vec[:, 4:5]).astype(jnp.bfloat16)
    node_mlp = dot(weights_ref[4], node_hidden) + feature_vec[:, 5:6]
    new = nodes.astype(jnp.float32) + layer_norm(
        node_mlp, feature_vec[:, 6:7], feature_vec[:, 7:8]
    )
    new = new.astype(jnp.bfloat16)
    mine = jnp.where(first, new[:half], new[half:])
    if last_layer:
        node_out_ref[...] = mine
        send(node_out_ref, outs[1])
    else:
        node_out_ref[...] = new
        send(node_out_ref, outs[1])
        store_rows(mine, *outs[2:])
    finish(sent_out)


def updated_graph(last_layer, scalars, sent, ready, copies):
    slots = ready[0].shape[1]
    node_rows = ready[5].shape[1]
    half = sent[0].shape[1]
    width = 2 * half
    out_width = half if last_layer else width
    out_shape = [shape((out_width, slots)), shape((out_width, node_rows))]
    out_specs = [HBM, HBM]
    if not last_layer:
        out_shape += [shape((node_rows, half)), shape((copies, node_rows // 8, half))]
        out_specs = [HBM, HBM, VMEM, VMEM]
    n_out = len(out_shape)
    return kernel_call(
        functools.partial(update_kernel, last_layer, n_out),
        "update_graph",
        out_shape,
        (scalars, *sent, *ready),
        [SMEM] + [VMEM] * (2 + len(ready)),
        out_specs,
        held(
            [
                *out_shape[:2],
                shape((width, UPDATE_BLOCK)),
                shape((width, UPDATE_BLOCK), jnp.float32),
                shape((3, width, 128), jnp.float32),
            ]
        )
        + [pltpu.SemaphoreType.DMA((slots // UPDATE_BLOCK + 1,))],
        2 * slots * width * (2 * width + node_rows),
    )


def from_other(a):
    return lax.ppermute(a, "width", [(0, 1), (1, 0)])


def copies_kernel(rows_ref, copies_ref):
    rows = rows_ref[...]
    for i in range(copies_ref.shape[0]):
        copies_ref[i] = rows


def copied(rows, count):
    return kernel_call(
        copies_kernel, "copies", shape((count, *rows.shape)), (rows,), [VMEM], VMEM, [], 0
    )


def exchanged(rows, copies, others=()):
    size = lax.axis_size(PATCH)
    up = [(i, (i + 1) % size) for i in range(size)]
    down = [(j, i) for i, j in up]
    below, above = lax.ppermute(rows, PATCH, up), lax.ppermute(rows, PATCH, down)
    column = lax.all_to_all(copies, Z, split_axis=0, concat_axis=0, tiled=True)
    column = column.reshape(-1, rows.shape[1])
    column, others = lax.optimization_barrier((column, others))
    plane = copied(column, lax.axis_size(PLANE))
    coarse = lax.all_to_all(plane, PLANE, split_axis=0, concat_axis=0, tiled=True)
    return (below, rows, above, coarse.reshape(-1, rows.shape[1])), others


def on_device(
    node_latents,
    edge_latents,
    senders,
    receivers,
    edge_count,
    edge_in_weight,
    edge_in_bias,
    edge_out_weight,
    edge_out_bias,
    edge_gain,
    edge_shift,
    node_in_weight,
    node_in_bias,
    node_out_weight,
    node_out_bias,
    node_gain,
    node_shift,
):
    half, node_rows = node_latents.shape
    layers = edge_in_weight.shape[0]
    coarse_rows = node_rows // 8
    patch_here = lax.axis_index(PATCH)
    patches = lax.axis_size(PATCH)
    plane = lax.axis_size(PLANE)
    columns = lax.axis_size(Z)
    scalars = jnp.stack([lax.axis_index("width"), edge_count[0]]).astype(jnp.int32)

    rows, copies = node_rows_of(node_latents, columns)

    vectors = jnp.stack(
        [
            edge_in_bias,
            edge_out_bias,
            edge_gain,
            edge_shift,
            node_in_bias,
            node_out_bias,
            node_gain,
            node_shift,
        ],
        axis=1,
    )
    own = (edge_in_weight, edge_out_weight, node_in_weight, node_out_weight, vectors)
    weights = []
    for a in own:
        weights += [a, from_other(a)]

    owner = senders // node_rows
    within = senders - owner * node_rows
    place = (owner % plane) * (patches // plane) + owner // plane
    index = jnp.where(
        owner == patch_here,
        node_rows + within,
        jnp.where(
            owner == (patch_here + patches - 1) % patches,
            within,
            jnp.where(
                owner == (patch_here + 1) % patches,
                2 * node_rows + within,
                3 * node_rows + place * coarse_rows + within,
            ),
        ),
    )
    index = index.reshape(-1, 128)
    receiver = (receivers - patch_here * node_rows)[None, :]

    edges = (edge_latents, from_other(edge_latents))
    nodes = (node_latents, from_other(node_latents))
    others = (weights[1], weights[5], edges[1], index, receiver)
    table, others = exchanged(rows, copies, others)
    weights[1], weights[5], other_edges, index, receiver = others
    edges = (edges[0], other_edges)
    for layer in range(layers):
        last_layer = layer == layers - 1
        ready = prepared(layer, scalars, edges, receiver, nodes, weights)
        table, ready = lax.optimization_barrier((table, ready))
        sent, *ready = gathered(ready, index, *table)
        sent = (sent, from_other(sent))
        results = updated_graph(last_layer, scalars, sent, ready, columns)
        if not last_layer:
            edges, nodes = results[:1], results[1:2]
            table, _ = exchanged(results[2], results[3])
    return (results[1], results[0])


def solution(mesh):
    finer = Mesh(
        mesh.devices.reshape(8, 4, 4, mesh.shape["width"]),
        (*PATCH, "width"),
    )
    in_specs = (
        P("width", PATCH),
        P("width", PATCH),
        P(PATCH),
        P(PATCH),
        P(PATCH),
        P(None, "width", None),
        P(None, "width"),
        P(None, "width", None),
        P(None, "width"),
        P(None, "width"),
        P(None, "width"),
        P(None, "width", None),
        P(None, "width"),
        P(None, "width", None),
        P(None, "width"),
        P(None, "width"),
        P(None, "width"),
    )
    out_specs = (P("width", PATCH), P("width", PATCH))
    return jax.shard_map(
        on_device, mesh=finer, in_specs=in_specs, out_specs=out_specs, check_vma=False
    )
```

```python
import functools

import jax
import jax.numpy as jnp
from jax import lax
from jax.experimental import pallas as pl
from jax.experimental.pallas import tpu as pltpu
from jax.sharding import Mesh
from jax.sharding import PartitionSpec as P

Z, Y, X = "patch_0", "patch_1", "patch_2"
PATCH = (Z, Y, X)
PLANE = (Y, X)
EPSILON = 1e-05
EDGE_BLOCK = 512
UPDATE_BLOCK = 1024
ROWS = 32
VMEM_LIMIT = 32 * 1024 * 1024


def dot(left, right, contract=((1,), (0,))):
    return lax.dot_general(left, right, (contract, ((), ())), preferred_element_type=jnp.float32)


def silu(v):
    h = 0.5 * v
    return h + h * jnp.tanh(h)


def layer_norm(values, gain, shift):
    width = values.shape[0]
    mean = jnp.sum(values, axis=0, keepdims=True) * (1.0 / width)
    square = jnp.sum(values * values, axis=0, keepdims=True) * (1.0 / width)
    return (values - mean) * lax.rsqrt(square - mean * mean + EPSILON) * gain + shift


def in_order(first, mine, other):
    return jnp.concatenate([jnp.where(first, mine, other), jnp.where(first, other, mine)], axis=0)


VMEM = pl.BlockSpec(memory_space=pltpu.VMEM)
SMEM = pl.BlockSpec(memory_space=pltpu.SMEM)
HBM = pl.BlockSpec(memory_space=pltpu.HBM)
ANY = pl.BlockSpec(memory_space=pl.ANY)


def shape(dims, dtype=jnp.bfloat16):
    return jax.ShapeDtypeStruct(dims, dtype)


def kernel_call(body, name, out_shape, inputs, in_specs, out_specs, scratch, flops):
    inputs = [
        pltpu.with_memory_space_constraint(a, pltpu.HBM) if spec is HBM else a
        for a, spec in zip(inputs, in_specs)
    ]
    if isinstance(out_specs, list):
        out_shape = [
            pltpu.HBM(a.shape, a.dtype) if spec is HBM else a
            for a, spec in zip(out_shape, out_specs)
        ]
    return pl.pallas_call(
        body,
        in_specs=in_specs,
        out_specs=out_specs,
        out_shape=out_shape,
        scratch_shapes=scratch,
        compiler_params=pltpu.CompilerParams(vmem_limit_bytes=VMEM_LIMIT),
        cost_estimate=pl.CostEstimate(flops=flops, bytes_accessed=4 << 20, transcendentals=0),
        name=name,
    )(*inputs)


def started(pairs, sems):
    copies = [pltpu.make_async_copy(a, b, sems.at[i]) for i, (a, b) in enumerate(pairs)]
    for copy in copies:
        copy.start()
    return copies


def finish(copies):
    for copy in copies:
        copy.wait()


def held(arrays):
    return [pltpu.VMEM(a.shape, a.dtype) for a in arrays]


def columns_of(ref, start, length):
    return ref.at[:, pl.ds(start, length)]


def store_rows(mine, rows_ref, copies_ref):
    rows = mine.T
    rows_ref[...] = rows
    for i in range(copies_ref.shape[0]):
        copies_ref[i] = rows[: copies_ref.shape[1]]


def rows_kernel(nodes_ref, rows_ref, copies_ref, held_ref, sem):
    copies = started([(nodes_ref, held_ref)], sem)
    finish(copies)
    store_rows(held_ref[...], rows_ref, copies_ref)


def node_rows_of(nodes, columns):
    half, node_rows = nodes.shape
    return kernel_call(
        rows_kernel,
        "node_rows",
        [shape((node_rows, half)), shape((columns, node_rows // 8, half))],
        (nodes,),
        [HBM],
        [VMEM, VMEM],
        held([nodes]) + [pltpu.SemaphoreType.DMA((1,))],
        0,
    )


def gather_kernel(n, index_in, below_in, here_in, above_in, coarse_in, *refs):
    ready_in, out_ref, ready_out = refs[:n], refs[n], refs[n + 1 : 2 * n + 1]
    index_ref, near_ref, coarse_ref, sems, ready_sems = refs[2 * n + 1 :]
    rows = here_in.shape[0]
    copies = started(
        [
            (index_in, index_ref),
            (below_in, near_ref.at[pl.ds(0, rows)]),
            (here_in, near_ref.at[pl.ds(rows, rows)]),
            (above_in, near_ref.at[pl.ds(2 * rows, rows)]),
            (coarse_in, coarse_ref),
        ],
        sems,
    )
    ready_copies = started(list(zip(ready_in, ready_out)), ready_sems)
    finish(copies[:4])
    columns = index_ref[...].T
    lane = lax.broadcasted_iota(jnp.int32, (128, 128), 1)

    def selection(start, first, length):
        blocks = []
        for k in range(start // 128, (start + EDGE_BLOCK) // 128):
            index = jnp.broadcast_to(columns[:, k : k + 1], (128, 128))
            tiles = []
            for j in range(first, first + length, 128):
                tiles.append(jnp.where(index == lane + j, 1.0, 0.0).astype(jnp.bfloat16))
            blocks.append(jnp.concatenate(tiles, axis=1))
        return jnp.concatenate(blocks, axis=0)

    for start in range(0, out_ref.shape[0], EDGE_BLOCK):
        total = dot(selection(start, 0, 3 * rows), near_ref[...])
        if start == 0:
            finish(copies[4:])
        total = total + dot(selection(start, 3 * rows, coarse_ref.shape[0]), coarse_ref[...])
        out_ref[start : start + EDGE_BLOCK, :] = total.astype(jnp.bfloat16)
    finish(ready_copies)


def gathered(ready, index, below, here, above, coarse):
    slots = index.size
    rows, width = here.shape
    table = 3 * rows + coarse.shape[0]
    n = len(ready)
    return kernel_call(
        functools.partial(gather_kernel, n),
        "gather_senders",
        [shape((slots, width)), *[shape(a.shape, a.dtype) for a in ready]],
        (index, below, here, above, coarse, *ready),
        [HBM] * 4 + [ANY] + [HBM] * n,
        [VMEM] * (1 + n),
        held([index, shape((3 * rows, width)), coarse])
        + [pltpu.SemaphoreType.DMA((5,)), pltpu.SemaphoreType.DMA((n,))],
        2 * slots * width * table,
    )


def prepare_kernel(layer, n_in, n_out, scalar_ref, *refs):
    ins, outs, refs = refs[:n_in], refs[n_in : n_in + n_out], refs[n_in + n_out :]
    held_out, refs = refs[:n_out], refs[n_out:]
    edge_held, node_held, hidden_weight_ref, out_held, vec_held, receiver_ref = refs[:6]
    in_sems, out_sems = refs[6:]
    before_ref, weights_ref, incidence_ref, vectors_ref = held_out[:4]
    first = scalar_ref[0] == 0
    count = scalar_ref[1]
    receiver, (wa, wb, ea, eb, va, vb, oa, ob, vec_a, vec_b) = ins[0], ins[1:11]
    edges_in, nodes_in = ins[11 : 11 + (n_in - 11) // 2], ins[11 + (n_in - 11) // 2 :]
    half = wa.shape[1]
    width = 2 * half

    def part(ref, start):
        return ref.at[layer, :, pl.ds(start, width)]

    def both(sources, target):
        if len(sources) == 1:
            return [(sources[0], target)]
        halves = (target.at[pl.ds(0, half)], target.at[pl.ds(half, half)])
        return list(zip(sources, halves))

    pairs = both(nodes_in, node_held) + [(receiver, receiver_ref)]
    pairs += [(vec_a.at[layer], vec_held.at[0]), (vec_b.at[layer], vec_held.at[1])]
    for k, target in ((2, hidden_weight_ref.at[1]), (0, hidden_weight_ref.at[0])):
        pairs += both((part(wa, k * width), part(wb, k * width)), target)
    pairs += both(edges_in, edge_held)
    pairs += both((ea.at[layer], eb.at[layer]), out_held.at[0])
    pairs += both((oa.at[layer], ob.at[layer]), out_held.at[1])
    pairs += both((part(wa, width), part(wb, width)), weights_ref.at[0])
    for k in (0, 1):
        pairs += both((part(va, k * width), part(vb, k * width)), weights_ref.at[2 + k])
    finish(started(pairs, in_sems))
    sent = [pltpu.make_async_copy(held_out[i], outs[i], out_sems.at[i]) for i in range(n_out)]

    vec = [vec_held[0].T, vec_held[1].T]
    hidden_vec = jnp.concatenate(vec, axis=0)
    feature_vec = in_order(first, *vec)
    nodes = node_held[...]
    edges = edge_held[...]
    if layer == 0:
        nodes = in_order(first, nodes[:half], nodes[half:])
        edges = in_order(first, edges[:half], edges[half:])
        held_out[4][...] = edges
        sent[4].start()
        held_out[5][...] = nodes
        sent[5].start()
    weights_ref[1] = out_held[0].T
    weights_ref[4] = out_held[1].T
    sent[1].start()
    vectors_ref[...] = jnp.concatenate([hidden_vec, feature_vec] + [hidden_vec] * 14, axis=1)
    sent[3].start()
    slots = incidence_ref.shape[1]
    live = lax.broadcasted_iota(jnp.int32, (1, slots), 1) < count
    incidence_ref[...] = jnp.where(
        (lax.broadcasted_iota(jnp.int32, incidence_ref.shape, 0) == receiver_ref[...]) & live,
        1.0,
        0.0,
    ).astype(jnp.bfloat16)
    sent[2].start()
    receiver_part = dot(hidden_weight_ref[1], nodes).astype(jnp.bfloat16)
    before = dot(hidden_weight_ref[0], edges) + dot(receiver_part, incidence_ref[...])
    before_ref[...] = before + hidden_vec[:, 0:1]
    sent[0].start()
    finish(sent)


def prepared(layer, scalars, edges, receiver, nodes, weights):
    slots = edges[0].shape[1]
    node_rows = nodes[0].shape[1]
    width = weights[0].shape[1] * 2
    inputs = (receiver, *weights, *edges, *nodes)
    out_shape = [
        shape((width, slots), jnp.float32),
        shape((5, width, width)),
        shape((node_rows, slots)),
        shape((width, 128), jnp.float32),
    ]
    if layer == 0:
        out_shape += [shape((width, slots)), shape((width, node_rows))]
    n_in, n_out = len(inputs), len(out_shape)
    ready = kernel_call(
        functools.partial(prepare_kernel, layer, n_in, n_out),
        "prepare_layer",
        out_shape,
        (scalars, *inputs),
        [SMEM] + [HBM] * n_in,
        [HBM] * n_out,
        held(
            [
                *out_shape,
                shape((width, slots)),
                shape((width, node_rows)),
                shape((2, width, width)),
                shape((2, width, width)),
                shape((2, *weights[8].shape[1:]), jnp.float32),
                receiver,
            ]
        )
        + [pltpu.SemaphoreType.DMA((21,)), pltpu.SemaphoreType.DMA((n_out,))],
        2 * slots * width * (width + node_rows),
    )
    if layer == 0:
        return ready
    return (*ready, *edges, *nodes)


def update_kernel(last_layer, n_out, scalar_ref, *refs):
    sent_a_ref, sent_b_ref, before_ref, weights_ref, incidence_ref, small_ref = refs[:6]
    edges_ref, nodes_ref, outs, refs = refs[6], refs[7], refs[8 : 8 + n_out], refs[8 + n_out :]
    edge_out_ref, node_out_ref, hidden_ref, mlp_ref, vectors_ref, out_sems = refs
    half = sent_a_ref.shape[1]
    width = 2 * half
    first = scalar_ref[0] == 0
    count = scalar_ref[1]
    sent_out = []

    def send(source, target):
        copy = pltpu.make_async_copy(source, target, out_sems.at[len(sent_out)])
        copy.start()
        sent_out.append(copy)

    small = small_ref[...]
    hidden_vec, feature_vec = small[:, 0:8], small[:, 8:16]
    for i, column in enumerate((1, 2, 3)):
        vectors_ref[i] = jnp.broadcast_to(feature_vec[:, column : column + 1], (width, 128))

    def spread(index, rows):
        return jnp.concatenate([vectors_ref[index, rows, :]] * (UPDATE_BLOCK // 128), axis=1)

    slots = edges_ref.shape[1]
    total = None
    for start in range(0, slots, UPDATE_BLOCK):
        here = slice(start, start + UPDATE_BLOCK)
        sent_a, sent_b = sent_a_ref[here, :], sent_b_ref[here, :]
        low = jnp.where(first, sent_a, sent_b)
        high = jnp.where(first, sent_b, sent_a)
        sent = jnp.concatenate([low, high], axis=1)
        mlp_ref[...] = dot(weights_ref[0], sent, ((1,), (1,)))
        for row in range(0, width, ROWS):
            rows = slice(row, row + ROWS)
            value = silu(mlp_ref[rows, :] + before_ref[rows, here])
            hidden_ref[rows, :] = value.astype(jnp.bfloat16)
        mlp_ref[...] = dot(weights_ref[1], hidden_ref[...])
        new_ref = hidden_ref if last_layer else columns_of(edge_out_ref, start, UPDATE_BLOCK)
        sums = jnp.zeros((8, UPDATE_BLOCK), jnp.float32)
        squares = jnp.zeros((8, UPDATE_BLOCK), jnp.float32)
        for row in range(0, width, ROWS):
            rows = slice(row, row + ROWS)
            value = mlp_ref[rows, :] + spread(0, rows)
            mlp_ref[rows, :] = value
            sums = sums + jnp.sum(value.reshape(ROWS // 8, 8, UPDATE_BLOCK), axis=0)
            squares = squares + jnp.sum((value * value).reshape(ROWS // 8, 8, UPDATE_BLOCK), axis=0)
        mean = jnp.sum(sums, axis=0, keepdims=True) * (1.0 / width)
        square = jnp.sum(squares, axis=0, keepdims=True) * (1.0 / width)
        scale = lax.rsqrt(square - mean * mean + EPSILON)
        live = lax.broadcasted_iota(jnp.int32, (1, UPDATE_BLOCK), 1) + start < count
        for row in range(0, width, ROWS):
            rows = slice(row, row + ROWS)
            value = (mlp_ref[rows, :] - mean) * scale * spread(1, rows) + spread(2, rows)
            value = value + edges_ref[rows, here].astype(jnp.float32)
            new_ref[rows, :] = jnp.where(live, value, 0.0).astype(jnp.bfloat16)
        updated = new_ref[...]
        part = dot(updated, incidence_ref[:, here], ((1,), (1,)))
        total = part if total is None else total + part
        if last_layer:
            edge_out_ref[:, here] = jnp.where(first, updated[:half], updated[half:])
        send(
            columns_of(edge_out_ref, start, UPDATE_BLOCK), columns_of(outs[0], start, UPDATE_BLOCK)
        )
    nodes = nodes_ref[...]
    aggregate = total.astype(jnp.bfloat16)
    node_before = dot(weights_ref[2], nodes) + dot(weights_ref[3], aggregate)
    node_hidden = silu(node_before + hidden_vec[:, 4:5]).astype(jnp.bfloat16)
    node_mlp = dot(weights_ref[4], node_hidden) + feature_vec[:, 5:6]
    new = nodes.astype(jnp.float32) + layer_norm(
        node_mlp, feature_vec[:, 6:7], feature_vec[:, 7:8]
    )
    new = new.astype(jnp.bfloat16)
    mine = jnp.where(first, new[:half], new[half:])
    if last_layer:
        node_out_ref[...] = mine
        send(node_out_ref, outs[1])
    else:
        node_out_ref[...] = new
        send(node_out_ref, outs[1])
        store_rows(mine, *outs[2:])
    finish(sent_out)


def updated_graph(last_layer, scalars, sent, ready, copies):
    slots = ready[0].shape[1]
    node_rows = ready[5].shape[1]
    half = sent[0].shape[1]
    width = 2 * half
    out_width = half if last_layer else width
    out_shape = [shape((out_width, slots)), shape((out_width, node_rows))]
    out_specs = [HBM, HBM]
    if not last_layer:
        out_shape += [shape((node_rows, half)), shape((copies, node_rows // 8, half))]
        out_specs = [HBM, HBM, VMEM, VMEM]
    n_out = len(out_shape)
    return kernel_call(
        functools.partial(update_kernel, last_layer, n_out),
        "update_graph",
        out_shape,
        (scalars, *sent, *ready),
        [SMEM] + [VMEM] * (2 + len(ready)),
        out_specs,
        held(
            [
                *out_shape[:2],
                shape((width, UPDATE_BLOCK)),
                shape((width, UPDATE_BLOCK), jnp.float32),
                shape((3, width, 128), jnp.float32),
            ]
        )
        + [pltpu.SemaphoreType.DMA((slots // UPDATE_BLOCK + 1,))],
        2 * slots * width * (2 * width + node_rows),
    )


def from_other(a):
    return lax.ppermute(a, "width", [(0, 1), (1, 0)])


def copies_kernel(rows_ref, copies_ref):
    rows = rows_ref[...]
    for i in range(copies_ref.shape[0]):
        copies_ref[i] = rows


def copied(rows, count):
    return kernel_call(
        copies_kernel, "copies", shape((count, *rows.shape)), (rows,), [VMEM], VMEM, [], 0
    )


def exchanged(rows, copies, others=()):
    size = lax.axis_size(PATCH)
    up = [(i, (i + 1) % size) for i in range(size)]
    down = [(j, i) for i, j in up]
    below, above = lax.ppermute(rows, PATCH, up), lax.ppermute(rows, PATCH, down)
    column = lax.all_to_all(copies, Z, split_axis=0, concat_axis=0, tiled=True)
    column = column.reshape(-1, rows.shape[1])
    column, others = lax.optimization_barrier((column, others))
    plane = copied(column, lax.axis_size(PLANE))
    coarse = lax.all_to_all(plane, PLANE, split_axis=0, concat_axis=0, tiled=True)
    return (below, rows, above, coarse.reshape(-1, rows.shape[1])), others


def on_device(
    node_latents,
    edge_latents,
    senders,
    receivers,
    edge_count,
    edge_in_weight,
    edge_in_bias,
    edge_out_weight,
    edge_out_bias,
    edge_gain,
    edge_shift,
    node_in_weight,
    node_in_bias,
    node_out_weight,
    node_out_bias,
    node_gain,
    node_shift,
):
    half, node_rows = node_latents.shape
    layers = edge_in_weight.shape[0]
    coarse_rows = node_rows // 8
    patch_here = lax.axis_index(PATCH)
    patches = lax.axis_size(PATCH)
    plane = lax.axis_size(PLANE)
    columns = lax.axis_size(Z)
    scalars = jnp.stack([lax.axis_index("width"), edge_count[0]]).astype(jnp.int32)

    rows, copies = node_rows_of(node_latents, columns)

    vectors = jnp.stack(
        [
            edge_in_bias,
            edge_out_bias,
            edge_gain,
            edge_shift,
            node_in_bias,
            node_out_bias,
            node_gain,
            node_shift,
        ],
        axis=1,
    )
    own = (edge_in_weight, edge_out_weight, node_in_weight, node_out_weight, vectors)
    weights = []
    for a in own:
        weights += [a, from_other(a)]

    owner = senders // node_rows
    within = senders - owner * node_rows
    place = (owner % plane) * (patches // plane) + owner // plane
    index = jnp.where(
        owner == patch_here,
        node_rows + within,
        jnp.where(
            owner == (patch_here + patches - 1) % patches,
            within,
            jnp.where(
                owner == (patch_here + 1) % patches,
                2 * node_rows + within,
                3 * node_rows + place * coarse_rows + within,
            ),
        ),
    )
    index = index.reshape(-1, 128)
    receiver = (receivers - patch_here * node_rows)[None, :]

    edges = (edge_latents, from_other(edge_latents))
    nodes = (node_latents, from_other(node_latents))
    others = (weights[1], weights[5], edges[1], index, receiver)
    table, others = exchanged(rows, copies, others)
    weights[1], weights[5], other_edges, index, receiver = others
    edges = (edges[0], other_edges)
    for layer in range(layers):
        last_layer = layer == layers - 1
        ready = prepared(layer, scalars, edges, receiver, nodes, weights)
        table, ready = lax.optimization_barrier((table, ready))
        sent, *ready = gathered(ready, index, *table)
        sent = (sent, from_other(sent))
        results = updated_graph(last_layer, scalars, sent, ready, columns)
        if not last_layer:
            edges, nodes = results[:1], results[1:2]
            table, _ = exchanged(results[2], results[3])
    return (results[1], results[0])


def solution(mesh):
    finer = Mesh(
        mesh.devices.reshape(8, 4, 4, mesh.shape["width"]),
        (*PATCH, "width"),
    )
    in_specs = (
        P("width", PATCH),
        P("width", PATCH),
        P(PATCH),
        P(PATCH),
        P(PATCH),
        P(None, "width", None),
        P(None, "width"),
        P(None, "width", None),
        P(None, "width"),
        P(None, "width"),
        P(None, "width"),
        P(None, "width", None),
        P(None, "width"),
        P(None, "width", None),
        P(None, "width"),
        P(None, "width"),
        P(None, "width"),
    )
    out_specs = (P("width", PATCH), P("width", PATCH))
    return jax.shard_map(
        on_device, mesh=finer, in_specs=in_specs, out_specs=out_specs, check_vma=False
    )
```

```python
import functools

import jax
import jax.numpy as jnp
from jax import lax
from jax.experimental import pallas as pl
from jax.experimental.pallas import tpu as pltpu
from jax.sharding import Mesh
from jax.sharding import PartitionSpec as P

Z, Y, X = "patch_0", "patch_1", "patch_2"
PATCH = (Z, Y, X)
PLANE = (Y, X)
EPSILON = 1e-05
EDGE_BLOCK = 512
UPDATE_BLOCK = 1024
ROWS = 32
VMEM_LIMIT = 32 * 1024 * 1024


def dot(left, right, contract=((1,), (0,))):
    return lax.dot_general(left, right, (contract, ((), ())), preferred_element_type=jnp.float32)


def silu(v):
    h = 0.5 * v
    return h + h * jnp.tanh(h)


def layer_norm(values, gain, shift):
    width = values.shape[0]
    mean = jnp.sum(values, axis=0, keepdims=True) * (1.0 / width)
    square = jnp.sum(values * values, axis=0, keepdims=True) * (1.0 / width)
    return (values - mean) * lax.rsqrt(square - mean * mean + EPSILON) * gain + shift


def in_order(first, mine, other):
    return jnp.concatenate([jnp.where(first, mine, other), jnp.where(first, other, mine)], axis=0)


VMEM = pl.BlockSpec(memory_space=pltpu.VMEM)
SMEM = pl.BlockSpec(memory_space=pltpu.SMEM)
HBM = pl.BlockSpec(memory_space=pltpu.HBM)
ANY = pl.BlockSpec(memory_space=pl.ANY)


def shape(dims, dtype=jnp.bfloat16):
    return jax.ShapeDtypeStruct(dims, dtype)


def kernel_call(body, name, out_shape, inputs, in_specs, out_specs, scratch, flops):
    inputs = [
        pltpu.with_memory_space_constraint(a, pltpu.HBM) if spec is HBM else a
        for a, spec in zip(inputs, in_specs)
    ]
    if isinstance(out_specs, list):
        out_shape = [
            pltpu.HBM(a.shape, a.dtype) if spec is HBM else a
            for a, spec in zip(out_shape, out_specs)
        ]
    return pl.pallas_call(
        body,
        in_specs=in_specs,
        out_specs=out_specs,
        out_shape=out_shape,
        scratch_shapes=scratch,
        compiler_params=pltpu.CompilerParams(vmem_limit_bytes=VMEM_LIMIT),
        cost_estimate=pl.CostEstimate(flops=flops, bytes_accessed=4 << 20, transcendentals=0),
        name=name,
    )(*inputs)


def started(pairs, sems):
    copies = [pltpu.make_async_copy(a, b, sems.at[i]) for i, (a, b) in enumerate(pairs)]
    for copy in copies:
        copy.start()
    return copies


def finish(copies):
    for copy in copies:
        copy.wait()


def held(arrays):
    return [pltpu.VMEM(a.shape, a.dtype) for a in arrays]


def columns_of(ref, start, length):
    return ref.at[:, pl.ds(start, length)]


def store_rows(rows, mine, rows_ref, copies_ref):
    rows_ref[...] = rows
    for i in range(copies_ref.shape[0]):
        copies_ref[i] = mine[: copies_ref.shape[1]]


def rows_kernel(nodes_ref, rows_ref, copies_ref, held_ref, sem):
    copies = started([(nodes_ref, held_ref)], sem)
    finish(copies)
    rows = held_ref[...].T
    store_rows(rows, rows, rows_ref, copies_ref)


def node_rows_of(nodes, columns):
    half, node_rows = nodes.shape
    return kernel_call(
        rows_kernel,
        "node_rows",
        [shape((node_rows, half)), shape((columns, node_rows // 8, half))],
        (nodes,),
        [HBM],
        [VMEM, VMEM],
        held([nodes]) + [pltpu.SemaphoreType.DMA((1,))],
        0,
    )


def gather_kernel(n, scalar_ref, index_in, rows_in, beside_in, coarse_in, *refs):
    ready_in, out_ref, ready_out = refs[:n], refs[n], refs[n + 1 : 2 * n + 1]
    index_ref, here_ref, beside_ref, coarse_ref, sems, ready_sems = refs[2 * n + 1 :]
    core = scalar_ref[0]
    rows, half = here_ref.shape
    mine = pl.ds(pl.multiple_of(core * half, half), half)
    copies = started(
        [
            (index_in, index_ref),
            (rows_in.at[:, mine], here_ref),
            (beside_in, beside_ref),
            (coarse_in, coarse_ref),
        ],
        sems,
    )
    ready_copies = started(list(zip(ready_in, ready_out)), ready_sems)
    finish(copies[:3])
    columns = index_ref[...].T
    lane = lax.broadcasted_iota(jnp.int32, (128, 128), 1)

    def selection(start, first, length):
        blocks = []
        for k in range(start // 128, (start + EDGE_BLOCK) // 128):
            index = jnp.broadcast_to(columns[:, k : k + 1], (128, 128))
            tiles = []
            for j in range(0, length, 128):
                tiles.append(jnp.where(index == lane + (first + j), 1.0, 0.0).astype(jnp.bfloat16))
            blocks.append(jnp.concatenate(tiles, axis=1) if len(tiles) > 1 else tiles[0])
        return jnp.concatenate(blocks, axis=0)

    for start in range(0, out_ref.shape[0], EDGE_BLOCK):
        near = dot(selection(start, core * (2 * rows), rows), beside_ref[...])
        total = dot(selection(start, rows, rows), here_ref[...])
        if start == 0:
            finish(copies[3:])
        total = total + dot(selection(start, 3 * rows, coarse_ref.shape[0]), coarse_ref[...])
        block = slice(start, start + EDGE_BLOCK)
        low = near[:, :half] + jnp.where(core == 0, total, 0.0)
        high = near[:, half:] + jnp.where(core == 0, 0.0, total)
        out_ref[block, :half] = low.astype(jnp.bfloat16)
        out_ref[block, half:] = high.astype(jnp.bfloat16)
    finish(ready_copies)


def gathered(scalars, ready, index, rows, beside, coarse):
    slots = index.size
    node_rows, width = rows.shape
    half = width // 2
    table = 3 * node_rows + coarse.shape[0]
    n = len(ready)
    return kernel_call(
        functools.partial(gather_kernel, n),
        "gather_senders",
        [shape((slots, width)), *[shape(a.shape, a.dtype) for a in ready]],
        (scalars, index, rows, beside, coarse, *ready),
        [SMEM] + [HBM] * 3 + [ANY] + [HBM] * n,
        [VMEM] * (1 + n),
        held([index, shape((node_rows, half)), beside, coarse])
        + [pltpu.SemaphoreType.DMA((4,)), pltpu.SemaphoreType.DMA((n,))],
        2 * slots * half * table,
    )


def prepare_kernel(layer, n_in, n_out, scalar_ref, *refs):
    ins, outs, refs = refs[:n_in], refs[n_in : n_in + n_out], refs[n_in + n_out :]
    held_out, refs = refs[:n_out], refs[n_out:]
    edge_held, node_held, hidden_weight_ref, out_held, vec_held, receiver_ref = refs[:6]
    in_sems, out_sems = refs[6:]
    before_ref, weights_ref, incidence_ref, vectors_ref = held_out[:4]
    first = scalar_ref[0] == 0
    count = scalar_ref[1]
    receiver, (wa, wb, ea, eb, va, vb, oa, ob, vec_a, vec_b) = ins[0], ins[1:11]
    edges_in, nodes_in = ins[11 : 11 + (n_in - 11) // 2], ins[11 + (n_in - 11) // 2 :]
    half = wa.shape[1]
    width = 2 * half

    def part(ref, start):
        return ref.at[layer, :, pl.ds(start, width)]

    def both(sources, target):
        if len(sources) == 1:
            return [(sources[0], target)]
        halves = (target.at[pl.ds(0, half)], target.at[pl.ds(half, half)])
        return list(zip(sources, halves))

    pairs = both(nodes_in, node_held) + [(receiver, receiver_ref)]
    pairs += [(vec_a.at[layer], vec_held.at[0]), (vec_b.at[layer], vec_held.at[1])]
    for k, target in ((2, hidden_weight_ref.at[1]), (0, hidden_weight_ref.at[0])):
        pairs += both((part(wa, k * width), part(wb, k * width)), target)
    pairs += both(edges_in, edge_held)
    pairs += both((ea.at[layer], eb.at[layer]), out_held.at[0])
    pairs += both((oa.at[layer], ob.at[layer]), out_held.at[1])
    pairs += both((part(wa, width), part(wb, width)), weights_ref.at[0])
    for k in (0, 1):
        pairs += both((part(va, k * width), part(vb, k * width)), weights_ref.at[2 + k])
    finish(started(pairs, in_sems))
    sent = [pltpu.make_async_copy(held_out[i], outs[i], out_sems.at[i]) for i in range(n_out)]

    vec = [vec_held[0].T, vec_held[1].T]
    hidden_vec = jnp.concatenate(vec, axis=0)
    feature_vec = in_order(first, *vec)
    nodes = node_held[...]
    edges = edge_held[...]
    if layer == 0:
        nodes = in_order(first, nodes[:half], nodes[half:])
        edges = in_order(first, edges[:half], edges[half:])
        held_out[4][...] = edges
        sent[4].start()
        held_out[5][...] = nodes
        sent[5].start()
    weights_ref[1] = out_held[0].T
    weights_ref[4] = out_held[1].T
    sent[1].start()
    vectors_ref[...] = jnp.concatenate([hidden_vec, feature_vec] + [hidden_vec] * 14, axis=1)
    sent[3].start()
    slots = incidence_ref.shape[1]
    live = lax.broadcasted_iota(jnp.int32, (1, slots), 1) < count
    incidence_ref[...] = jnp.where(
        (lax.broadcasted_iota(jnp.int32, incidence_ref.shape, 0) == receiver_ref[...]) & live,
        1.0,
        0.0,
    ).astype(jnp.bfloat16)
    sent[2].start()
    receiver_part = dot(hidden_weight_ref[1], nodes).astype(jnp.bfloat16)
    before = dot(hidden_weight_ref[0], edges) + dot(receiver_part, incidence_ref[...])
    before_ref[...] = before + hidden_vec[:, 0:1]
    sent[0].start()
    finish(sent)


def prepared(layer, scalars, edges, receiver, nodes, weights):
    slots = edges[0].shape[1]
    node_rows = nodes[0].shape[1]
    width = weights[0].shape[1] * 2
    inputs = (receiver, *weights, *edges, *nodes)
    out_shape = [
        shape((width, slots), jnp.float32),
        shape((5, width, width)),
        shape((node_rows, slots)),
        shape((width, 128), jnp.float32),
    ]
    if layer == 0:
        out_shape += [shape((width, slots)), shape((width, node_rows))]
    n_in, n_out = len(inputs), len(out_shape)
    ready = kernel_call(
        functools.partial(prepare_kernel, layer, n_in, n_out),
        "prepare_layer",
        out_shape,
        (scalars, *inputs),
        [SMEM] + [HBM] * n_in,
        [HBM] * n_out,
        held(
            [
                *out_shape,
                shape((width, slots)),
                shape((width, node_rows)),
                shape((2, width, width)),
                shape((2, width, width)),
                shape((2, *weights[8].shape[1:]), jnp.float32),
                receiver,
            ]
        )
        + [pltpu.SemaphoreType.DMA((21,)), pltpu.SemaphoreType.DMA((n_out,))],
        2 * slots * width * (width + node_rows),
    )
    if layer == 0:
        return ready
    return (*ready, *edges, *nodes)


def update_kernel(last_layer, n_out, scalar_ref, *refs):
    sent_a_ref, sent_b_ref, before_ref, weights_ref, incidence_ref, small_ref = refs[:6]
    edges_ref, nodes_ref, outs, refs = refs[6], refs[7], refs[8 : 8 + n_out], refs[8 + n_out :]
    edge_out_ref, node_out_ref, hidden_ref, mlp_ref, vectors_ref, out_sems = refs
    width = sent_a_ref.shape[1]
    half = width // 2
    first = scalar_ref[0] == 0
    count = scalar_ref[1]
    sent_out = []

    def send(source, target):
        copy = pltpu.make_async_copy(source, target, out_sems.at[len(sent_out)])
        copy.start()
        sent_out.append(copy)

    small = small_ref[...]
    hidden_vec, feature_vec = small[:, 0:8], small[:, 8:16]
    for i, column in enumerate((1, 2, 3)):
        vectors_ref[i] = jnp.broadcast_to(feature_vec[:, column : column + 1], (width, 128))

    def spread(index, rows):
        return jnp.concatenate([vectors_ref[index, rows, :]] * (UPDATE_BLOCK // 128), axis=1)

    slots = edges_ref.shape[1]
    total = None
    for start in range(0, slots, UPDATE_BLOCK):
        here = slice(start, start + UPDATE_BLOCK)
        sent = sent_a_ref[here, :] + sent_b_ref[here, :]
        mlp_ref[...] = dot(weights_ref[0], sent, ((1,), (1,)))
        for row in range(0, width, ROWS):
            rows = slice(row, row + ROWS)
            value = silu(mlp_ref[rows, :] + before_ref[rows, here])
            hidden_ref[rows, :] = value.astype(jnp.bfloat16)
        mlp_ref[...] = dot(weights_ref[1], hidden_ref[...])
        new_ref = hidden_ref if last_layer else columns_of(edge_out_ref, start, UPDATE_BLOCK)
        sums = jnp.zeros((8, UPDATE_BLOCK), jnp.float32)
        squares = jnp.zeros((8, UPDATE_BLOCK), jnp.float32)
        for row in range(0, width, ROWS):
            rows = slice(row, row + ROWS)
            value = mlp_ref[rows, :] + spread(0, rows)
            mlp_ref[rows, :] = value
            sums = sums + jnp.sum(value.reshape(ROWS // 8, 8, UPDATE_BLOCK), axis=0)
            squares = squares + jnp.sum((value * value).reshape(ROWS // 8, 8, UPDATE_BLOCK), axis=0)
        mean = jnp.sum(sums, axis=0, keepdims=True) * (1.0 / width)
        square = jnp.sum(squares, axis=0, keepdims=True) * (1.0 / width)
        scale = lax.rsqrt(square - mean * mean + EPSILON)
        live = lax.broadcasted_iota(jnp.int32, (1, UPDATE_BLOCK), 1) + start < count
        for row in range(0, width, ROWS):
            rows = slice(row, row + ROWS)
            value = (mlp_ref[rows, :] - mean) * scale * spread(1, rows) + spread(2, rows)
            value = value + edges_ref[rows, here].astype(jnp.float32)
            new_ref[rows, :] = jnp.where(live, value, 0.0).astype(jnp.bfloat16)
        updated = new_ref[...]
        part = dot(updated, incidence_ref[:, here], ((1,), (1,)))
        total = part if total is None else total + part
        if last_layer:
            edge_out_ref[:, here] = jnp.where(first, updated[:half], updated[half:])
        send(
            columns_of(edge_out_ref, start, UPDATE_BLOCK), columns_of(outs[0], start, UPDATE_BLOCK)
        )
    nodes = nodes_ref[...]
    aggregate = total.astype(jnp.bfloat16)
    node_before = dot(weights_ref[2], nodes) + dot(weights_ref[3], aggregate)
    node_hidden = silu(node_before + hidden_vec[:, 4:5]).astype(jnp.bfloat16)
    node_mlp = dot(weights_ref[4], node_hidden) + feature_vec[:, 5:6]
    new = nodes.astype(jnp.float32) + layer_norm(
        node_mlp, feature_vec[:, 6:7], feature_vec[:, 7:8]
    )
    new = new.astype(jnp.bfloat16)
    mine = jnp.where(first, new[:half], new[half:])
    if last_layer:
        node_out_ref[...] = mine
        send(node_out_ref, outs[1])
    else:
        node_out_ref[...] = new
        send(node_out_ref, outs[1])
        rows = new.T
        store_rows(rows, jnp.where(first, rows[:, :half], rows[:, half:]), *outs[2:])
    finish(sent_out)


def updated_graph(last_layer, scalars, sent, ready, copies):
    slots = ready[0].shape[1]
    node_rows = ready[5].shape[1]
    width = sent[0].shape[1]
    half = width // 2
    out_width = half if last_layer else width
    out_shape = [shape((out_width, slots)), shape((out_width, node_rows))]
    out_specs = [HBM, HBM]
    if not last_layer:
        out_shape += [shape((node_rows, width)), shape((copies, node_rows // 8, half))]
        out_specs = [HBM, HBM, VMEM, VMEM]
    n_out = len(out_shape)
    return kernel_call(
        functools.partial(update_kernel, last_layer, n_out),
        "update_graph",
        out_shape,
        (scalars, *sent, *ready),
        [SMEM] + [VMEM] * (2 + len(ready)),
        out_specs,
        held(
            [
                *out_shape[:2],
                shape((width, UPDATE_BLOCK)),
                shape((width, UPDATE_BLOCK), jnp.float32),
                shape((3, width, 128), jnp.float32),
            ]
        )
        + [pltpu.SemaphoreType.DMA((slots // UPDATE_BLOCK + 1,))],
        2 * slots * width * (2 * width + node_rows),
    )


def from_other(a):
    return lax.ppermute(a, "width", [(0, 1), (1, 0)])


def copies_kernel(rows_ref, copies_ref):
    rows = rows_ref[...]
    for i in range(copies_ref.shape[0]):
        copies_ref[i] = rows


def copied(rows, count):
    return kernel_call(
        copies_kernel, "copies", shape((count, *rows.shape)), (rows,), [VMEM], VMEM, [], 0
    )


def exchanged(rows, copies, others=()):
    size = lax.axis_size(PATCH)
    pairs = []
    for i in range(size):
        pairs += [(2 * i, (i + 1) % size * 2), (2 * i + 1, (i - 1) % size * 2 + 1)]
    beside = lax.ppermute(rows, (*PATCH, "width"), pairs)
    column = lax.all_to_all(copies, Z, split_axis=0, concat_axis=0, tiled=True)
    column = column.reshape(-1, copies.shape[2])
    column, others = lax.optimization_barrier((column, others))
    plane = copied(column, lax.axis_size(PLANE))
    coarse = lax.all_to_all(plane, PLANE, split_axis=0, concat_axis=0, tiled=True)
    return (rows, beside, coarse.reshape(-1, copies.shape[2])), others


def on_device(
    node_latents,
    edge_latents,
    senders,
    receivers,
    edge_count,
    edge_in_weight,
    edge_in_bias,
    edge_out_weight,
    edge_out_bias,
    edge_gain,
    edge_shift,
    node_in_weight,
    node_in_bias,
    node_out_weight,
    node_out_bias,
    node_gain,
    node_shift,
):
    half, node_rows = node_latents.shape
    layers = edge_in_weight.shape[0]
    coarse_rows = node_rows // 8
    patch_here = lax.axis_index(PATCH)
    patches = lax.axis_size(PATCH)
    plane = lax.axis_size(PLANE)
    columns = lax.axis_size(Z)
    scalars = jnp.stack([lax.axis_index("width"), edge_count[0]]).astype(jnp.int32)

    rows, copies = node_rows_of(node_latents, columns)

    vectors = jnp.stack(
        [
            edge_in_bias,
            edge_out_bias,
            edge_gain,
            edge_shift,
            node_in_bias,
            node_out_bias,
            node_gain,
            node_shift,
        ],
        axis=1,
    )
    own = (edge_in_weight, edge_out_weight, node_in_weight, node_out_weight, vectors)
    weights = []
    for a in own:
        weights += [a, from_other(a)]

    owner = senders // node_rows
    within = senders - owner * node_rows
    place = (owner % plane) * (patches // plane) + owner // plane
    index = jnp.where(
        owner == patch_here,
        node_rows + within,
        jnp.where(
            owner == (patch_here + patches - 1) % patches,
            within,
            jnp.where(
                owner == (patch_here + 1) % patches,
                2 * node_rows + within,
                3 * node_rows + place * coarse_rows + within,
            ),
        ),
    )
    index = index.reshape(-1, 128)
    receiver = (receivers - patch_here * node_rows)[None, :]

    edges = (edge_latents, from_other(edge_latents))
    nodes = (node_latents, from_other(node_latents))
    others = (weights[1], weights[5], edges[1], index, receiver)
    other_rows = from_other(rows)
    rows = jnp.where(
        lax.axis_index("width") == 0,
        jnp.concatenate([rows, other_rows], axis=1),
        jnp.concatenate([other_rows, rows], axis=1),
    )
    table, others = exchanged(rows, copies, others)
    weights[1], weights[5], other_edges, index, receiver = others
    edges = (edges[0], other_edges)
    for layer in range(layers):
        last_layer = layer == layers - 1
        ready = prepared(layer, scalars, edges, receiver, nodes, weights)
        table, ready = lax.optimization_barrier((table, ready))
        sent, *ready = gathered(scalars, ready, index, *table)
        sent = (sent, from_other(sent))
        results = updated_graph(last_layer, scalars, sent, ready, columns)
        if not last_layer:
            edges, nodes = results[:1], results[1:2]
            table, _ = exchanged(results[2], results[3])
    return (results[1], results[0])


def solution(mesh):
    finer = Mesh(
        mesh.devices.reshape(8, 4, 4, mesh.shape["width"]),
        (*PATCH, "width"),
    )
    in_specs = (
        P("width", PATCH),
        P("width", PATCH),
        P(PATCH),
        P(PATCH),
        P(PATCH),
        P(None, "width", None),
        P(None, "width"),
        P(None, "width", None),
        P(None, "width"),
        P(None, "width"),
        P(None, "width"),
        P(None, "width", None),
        P(None, "width"),
        P(None, "width", None),
        P(None, "width"),
        P(None, "width"),
        P(None, "width"),
    )
    out_specs = (P("width", PATCH), P("width", PATCH))
    return jax.shard_map(
        on_device, mesh=finer, in_specs=in_specs, out_specs=out_specs, check_vma=False
    )
```

```python
import functools

import jax
import jax.numpy as jnp
from jax import lax
from jax.experimental import pallas as pl
from jax.experimental.pallas import tpu as pltpu
from jax.sharding import Mesh
from jax.sharding import PartitionSpec as P

Z, Y, X = "patch_0", "patch_1", "patch_2"
PATCH = (Z, Y, X)
PLANE = (Y, X)
EPSILON = 1e-05
EDGE_BLOCK = 512
UPDATE_BLOCK = 1024
ROWS = 32
VMEM_LIMIT = 32 * 1024 * 1024


def dot(left, right, contract=((1,), (0,))):
    return lax.dot_general(left, right, (contract, ((), ())), preferred_element_type=jnp.float32)


def silu(v):
    h = 0.5 * v
    return h + h * jnp.tanh(h)


def layer_norm(values, gain, shift):
    width = values.shape[0]
    mean = jnp.sum(values, axis=0, keepdims=True) * (1.0 / width)
    square = jnp.sum(values * values, axis=0, keepdims=True) * (1.0 / width)
    return (values - mean) * lax.rsqrt(square - mean * mean + EPSILON) * gain + shift


def in_order(first, mine, other):
    return jnp.concatenate([jnp.where(first, mine, other), jnp.where(first, other, mine)], axis=0)


VMEM = pl.BlockSpec(memory_space=pltpu.VMEM)
SMEM = pl.BlockSpec(memory_space=pltpu.SMEM)
HBM = pl.BlockSpec(memory_space=pltpu.HBM)
ANY = pl.BlockSpec(memory_space=pl.ANY)


def shape(dims, dtype=jnp.bfloat16):
    return jax.ShapeDtypeStruct(dims, dtype)


def kernel_call(body, name, out_shape, inputs, in_specs, out_specs, scratch, flops):
    inputs = [
        pltpu.with_memory_space_constraint(a, pltpu.HBM) if spec is HBM else a
        for a, spec in zip(inputs, in_specs)
    ]
    if isinstance(out_specs, list):
        out_shape = [
            pltpu.HBM(a.shape, a.dtype) if spec is HBM else a
            for a, spec in zip(out_shape, out_specs)
        ]
    return pl.pallas_call(
        body,
        in_specs=in_specs,
        out_specs=out_specs,
        out_shape=out_shape,
        scratch_shapes=scratch,
        compiler_params=pltpu.CompilerParams(vmem_limit_bytes=VMEM_LIMIT),
        cost_estimate=pl.CostEstimate(flops=flops, bytes_accessed=4 << 20, transcendentals=0),
        name=name,
    )(*inputs)


def started(pairs, sems):
    copies = [pltpu.make_async_copy(a, b, sems.at[i]) for i, (a, b) in enumerate(pairs)]
    for copy in copies:
        copy.start()
    return copies


def finish(copies):
    for copy in copies:
        copy.wait()


def held(arrays):
    return [pltpu.VMEM(a.shape, a.dtype) for a in arrays]


def columns_of(ref, start, length):
    return ref.at[:, pl.ds(start, length)]


def store_rows(rows, mine, rows_ref, copies_ref):
    rows_ref[...] = rows
    for i in range(copies_ref.shape[0]):
        copies_ref[i] = mine[: copies_ref.shape[1]]


def rows_kernel(nodes_ref, rows_ref, copies_ref, held_ref, sem):
    copies = started([(nodes_ref, held_ref)], sem)
    finish(copies)
    rows = held_ref[...].T
    store_rows(rows, rows, rows_ref, copies_ref)


def node_rows_of(nodes, columns):
    half, node_rows = nodes.shape
    return kernel_call(
        rows_kernel,
        "node_rows",
        [shape((node_rows, half)), shape((columns, node_rows // 8, half))],
        (nodes,),
        [HBM],
        [VMEM, VMEM],
        held([nodes]) + [pltpu.SemaphoreType.DMA((1,))],
        0,
    )


def gather_kernel(n, scalar_ref, index_in, rows_in, beside_in, coarse_in, *refs):
    ready_in, out_ref, ready_out = refs[:n], refs[n], refs[n + 1 : 2 * n + 1]
    index_ref, here_ref, beside_ref, coarse_ref, sems, ready_sems = refs[2 * n + 1 :]
    core = scalar_ref[0]
    rows, half = here_ref.shape
    mine = pl.ds(pl.multiple_of(core * half, half), half)
    copies = started(
        [
            (index_in, index_ref),
            (rows_in.at[:, mine], here_ref),
            (beside_in, beside_ref),
            (coarse_in, coarse_ref),
        ],
        sems,
    )
    ready_copies = started(list(zip(ready_in, ready_out)), ready_sems)
    finish(copies[:3])
    columns = index_ref[...].T
    lane = lax.broadcasted_iota(jnp.int32, (128, 128), 1)

    def selection(start, first, length):
        blocks = []
        for k in range(start // 128, (start + EDGE_BLOCK) // 128):
            index = jnp.broadcast_to(columns[:, k : k + 1], (128, 128))
            tiles = []
            for j in range(0, length, 128):
                tiles.append(jnp.where(index == lane + (first + j), 1.0, 0.0).astype(jnp.bfloat16))
            blocks.append(jnp.concatenate(tiles, axis=1) if len(tiles) > 1 else tiles[0])
        return jnp.concatenate(blocks, axis=0)

    for start in range(0, out_ref.shape[0], EDGE_BLOCK):
        near = dot(selection(start, core * (2 * rows), rows), beside_ref[...])
        total = dot(selection(start, rows, rows), here_ref[...])
        if start == 0:
            finish(copies[3:])
        total = total + dot(selection(start, 3 * rows, coarse_ref.shape[0]), coarse_ref[...])
        block = slice(start, start + EDGE_BLOCK)
        low = near[:, :half] + jnp.where(core == 0, total, 0.0)
        high = near[:, half:] + jnp.where(core == 0, 0.0, total)
        out_ref[block, :half] = low.astype(jnp.bfloat16)
        out_ref[block, half:] = high.astype(jnp.bfloat16)
    finish(ready_copies)


def gathered(scalars, ready, index, rows, beside, coarse):
    slots = index.size
    node_rows, width = rows.shape
    half = width // 2
    table = 3 * node_rows + coarse.shape[0]
    n = len(ready)
    return kernel_call(
        functools.partial(gather_kernel, n),
        "gather_senders",
        [shape((slots, width)), *[shape(a.shape, a.dtype) for a in ready]],
        (scalars, index, rows, beside, coarse, *ready),
        [SMEM] + [HBM] * 3 + [ANY] + [HBM] * n,
        [VMEM] * (1 + n),
        held([index, shape((node_rows, half)), beside, coarse])
        + [pltpu.SemaphoreType.DMA((4,)), pltpu.SemaphoreType.DMA((n,))],
        2 * slots * half * table,
    )


def prepare_kernel(layer, n_in, n_out, scalar_ref, *refs):
    ins, outs, refs = refs[:n_in], refs[n_in : n_in + n_out], refs[n_in + n_out :]
    held_out, refs = refs[:n_out], refs[n_out:]
    edge_held, node_held, hidden_weight_ref, out_held, vec_held, receiver_ref = refs[:6]
    in_sems, out_sems = refs[6:]
    before_ref, weights_ref, incidence_ref, vectors_ref = held_out[:4]
    first = scalar_ref[0] == 0
    count = scalar_ref[1]
    receiver, (wa, wb, ea, eb, va, vb, oa, ob, vec_a, vec_b) = ins[0], ins[1:11]
    edges_in, nodes_in = ins[11 : 11 + (n_in - 11) // 2], ins[11 + (n_in - 11) // 2 :]
    half = wa.shape[1]
    width = 2 * half

    def part(ref, start):
        return ref.at[layer, :, pl.ds(start, width)]

    def both(sources, target):
        if len(sources) == 1:
            return [(sources[0], target)]
        halves = (target.at[pl.ds(0, half)], target.at[pl.ds(half, half)])
        return list(zip(sources, halves))

    pairs = both(nodes_in, node_held) + [(receiver, receiver_ref)]
    pairs += [(vec_a.at[layer], vec_held.at[0]), (vec_b.at[layer], vec_held.at[1])]
    for k, target in ((2, hidden_weight_ref.at[1]), (0, hidden_weight_ref.at[0])):
        pairs += both((part(wa, k * width), part(wb, k * width)), target)
    pairs += both(edges_in, edge_held)
    pairs += both((ea.at[layer], eb.at[layer]), out_held.at[0])
    pairs += both((oa.at[layer], ob.at[layer]), out_held.at[1])
    pairs += both((part(wa, width), part(wb, width)), weights_ref.at[0])
    for k in (0, 1):
        pairs += both((part(va, k * width), part(vb, k * width)), weights_ref.at[2 + k])
    finish(started(pairs, in_sems))
    sent = [pltpu.make_async_copy(held_out[i], outs[i], out_sems.at[i]) for i in range(n_out)]

    vec = [vec_held[0].T, vec_held[1].T]
    hidden_vec = jnp.concatenate(vec, axis=0)
    feature_vec = in_order(first, *vec)
    nodes = node_held[...]
    edges = edge_held[...]
    if layer == 0:
        nodes = in_order(first, nodes[:half], nodes[half:])
        edges = in_order(first, edges[:half], edges[half:])
        held_out[4][...] = edges
        sent[4].start()
        held_out[5][...] = nodes
        sent[5].start()
    weights_ref[1] = out_held[0].T
    weights_ref[4] = out_held[1].T
    sent[1].start()
    vectors_ref[...] = jnp.concatenate([hidden_vec, feature_vec] + [hidden_vec] * 14, axis=1)
    sent[3].start()
    slots = incidence_ref.shape[1]
    live = lax.broadcasted_iota(jnp.int32, (1, slots), 1) < count
    incidence_ref[...] = jnp.where(
        (lax.broadcasted_iota(jnp.int32, incidence_ref.shape, 0) == receiver_ref[...]) & live,
        1.0,
        0.0,
    ).astype(jnp.bfloat16)
    sent[2].start()
    receiver_part = dot(hidden_weight_ref[1], nodes).astype(jnp.bfloat16)
    before = dot(hidden_weight_ref[0], edges) + dot(receiver_part, incidence_ref[...])
    before_ref[...] = before + hidden_vec[:, 0:1]
    sent[0].start()
    finish(sent)


def prepared(layer, scalars, edges, receiver, nodes, weights):
    slots = edges[0].shape[1]
    node_rows = nodes[0].shape[1]
    width = weights[0].shape[1] * 2
    inputs = (receiver, *weights, *edges, *nodes)
    out_shape = [
        shape((width, slots), jnp.float32),
        shape((5, width, width)),
        shape((node_rows, slots)),
        shape((width, 128), jnp.float32),
    ]
    if layer == 0:
        out_shape += [shape((width, slots)), shape((width, node_rows))]
    n_in, n_out = len(inputs), len(out_shape)
    ready = kernel_call(
        functools.partial(prepare_kernel, layer, n_in, n_out),
        "prepare_layer",
        out_shape,
        (scalars, *inputs),
        [SMEM] + [HBM] * n_in,
        [HBM] * n_out,
        held(
            [
                *out_shape,
                shape((width, slots)),
                shape((width, node_rows)),
                shape((2, width, width)),
                shape((2, width, width)),
                shape((2, *weights[8].shape[1:]), jnp.float32),
                receiver,
            ]
        )
        + [pltpu.SemaphoreType.DMA((21,)), pltpu.SemaphoreType.DMA((n_out,))],
        2 * slots * width * (width + node_rows),
    )
    if layer == 0:
        return ready
    return (*ready, *edges, *nodes)


def update_kernel(last_layer, n_out, scalar_ref, *refs):
    sent_a_ref, sent_b_ref, before_ref, weights_ref, incidence_ref, small_ref = refs[:6]
    edges_ref, nodes_ref, outs, refs = refs[6], refs[7], refs[8 : 8 + n_out], refs[8 + n_out :]
    edge_out_ref, node_out_ref, hidden_ref, mlp_ref, vectors_ref, out_sems = refs
    width = sent_a_ref.shape[1]
    half = width // 2
    first = scalar_ref[0] == 0
    count = scalar_ref[1]
    sent_out = []

    def send(source, target):
        copy = pltpu.make_async_copy(source, target, out_sems.at[len(sent_out)])
        copy.start()
        sent_out.append(copy)

    small = small_ref[...]
    hidden_vec, feature_vec = small[:, 0:8], small[:, 8:16]
    for i, column in enumerate((1, 2, 3)):
        vectors_ref[i] = jnp.broadcast_to(feature_vec[:, column : column + 1], (width, 128))

    def spread(index, rows):
        return jnp.concatenate([vectors_ref[index, rows, :]] * (UPDATE_BLOCK // 128), axis=1)

    slots = edges_ref.shape[1]
    total = None
    for start in range(0, slots, UPDATE_BLOCK):
        here = slice(start, start + UPDATE_BLOCK)
        sent = sent_a_ref[here, :] + sent_b_ref[here, :]
        mlp_ref[...] = dot(weights_ref[0], sent, ((1,), (1,)))
        for row in range(0, width, ROWS):
            rows = slice(row, row + ROWS)
            value = silu(mlp_ref[rows, :] + before_ref[rows, here])
            hidden_ref[rows, :] = value.astype(jnp.bfloat16)
        mlp_ref[...] = dot(weights_ref[1], hidden_ref[...])
        new_ref = hidden_ref if last_layer else columns_of(edge_out_ref, start, UPDATE_BLOCK)
        sums = jnp.zeros((8, UPDATE_BLOCK), jnp.float32)
        squares = jnp.zeros((8, UPDATE_BLOCK), jnp.float32)
        for row in range(0, width, ROWS):
            rows = slice(row, row + ROWS)
            value = mlp_ref[rows, :] + spread(0, rows)
            mlp_ref[rows, :] = value
            sums = sums + jnp.sum(value.reshape(ROWS // 8, 8, UPDATE_BLOCK), axis=0)
            squares = squares + jnp.sum((value * value).reshape(ROWS // 8, 8, UPDATE_BLOCK), axis=0)
        mean = jnp.sum(sums, axis=0, keepdims=True) * (1.0 / width)
        square = jnp.sum(squares, axis=0, keepdims=True) * (1.0 / width)
        scale = lax.rsqrt(square - mean * mean + EPSILON)
        live = lax.broadcasted_iota(jnp.int32, (1, UPDATE_BLOCK), 1) + start < count
        for row in range(0, width, ROWS):
            rows = slice(row, row + ROWS)
            value = (mlp_ref[rows, :] - mean) * scale * spread(1, rows) + spread(2, rows)
            value = value + edges_ref[rows, here].astype(jnp.float32)
            new_ref[rows, :] = jnp.where(live, value, 0.0).astype(jnp.bfloat16)
        updated = new_ref[...]
        part = dot(updated, incidence_ref[:, here], ((1,), (1,)))
        total = part if total is None else total + part
        if last_layer:
            edge_out_ref[:, here] = jnp.where(first, updated[:half], updated[half:])
        send(
            columns_of(edge_out_ref, start, UPDATE_BLOCK), columns_of(outs[0], start, UPDATE_BLOCK)
        )
    nodes = nodes_ref[...]
    aggregate = total.astype(jnp.bfloat16)
    node_before = dot(weights_ref[2], nodes) + dot(weights_ref[3], aggregate)
    node_hidden = silu(node_before + hidden_vec[:, 4:5]).astype(jnp.bfloat16)
    node_mlp = dot(weights_ref[4], node_hidden) + feature_vec[:, 5:6]
    new = nodes.astype(jnp.float32) + layer_norm(
        node_mlp, feature_vec[:, 6:7], feature_vec[:, 7:8]
    )
    new = new.astype(jnp.bfloat16)
    mine = jnp.where(first, new[:half], new[half:])
    if last_layer:
        node_out_ref[...] = mine
        send(node_out_ref, outs[1])
    else:
        node_out_ref[...] = new
        send(node_out_ref, outs[1])
        rows = new.T
        store_rows(rows, jnp.where(first, rows[:, :half], rows[:, half:]), *outs[2:])
    finish(sent_out)


def updated_graph(last_layer, scalars, sent, ready, copies):
    slots = ready[0].shape[1]
    node_rows = ready[5].shape[1]
    width = sent[0].shape[1]
    half = width // 2
    out_width = half if last_layer else width
    out_shape = [shape((out_width, slots)), shape((out_width, node_rows))]
    out_specs = [HBM, HBM]
    if not last_layer:
        out_shape += [shape((node_rows, width)), shape((copies, node_rows // 8, half))]
        out_specs = [HBM, HBM, VMEM, VMEM]
    n_out = len(out_shape)
    return kernel_call(
        functools.partial(update_kernel, last_layer, n_out),
        "update_graph",
        out_shape,
        (scalars, *sent, *ready),
        [SMEM] + [VMEM] * (2 + len(ready)),
        out_specs,
        held(
            [
                *out_shape[:2],
                shape((width, UPDATE_BLOCK)),
                shape((width, UPDATE_BLOCK), jnp.float32),
                shape((3, width, 128), jnp.float32),
            ]
        )
        + [pltpu.SemaphoreType.DMA((slots // UPDATE_BLOCK + 1,))],
        2 * slots * width * (2 * width + node_rows),
    )


def from_other(a):
    return lax.ppermute(a, "width", [(0, 1), (1, 0)])


def copies_kernel(rows_ref, copies_ref):
    rows = rows_ref[...]
    for i in range(copies_ref.shape[0]):
        copies_ref[i] = rows


def copied(rows, count):
    return kernel_call(
        copies_kernel, "copies", shape((count, *rows.shape)), (rows,), [VMEM], VMEM, [], 0
    )


def exchanged(rows, copies, others=()):
    size = lax.axis_size(PATCH)
    pairs = []
    for i in range(size):
        pairs += [(2 * i, (i + 1) % size * 2), (2 * i + 1, (i - 1) % size * 2 + 1)]
    beside = lax.ppermute(rows, (*PATCH, "width"), pairs)
    column = lax.all_to_all(copies, Z, split_axis=0, concat_axis=0, tiled=True)
    column = column.reshape(-1, copies.shape[2])
    column, others = lax.optimization_barrier((column, others))
    plane = copied(column, lax.axis_size(PLANE))
    coarse = lax.all_to_all(plane, PLANE, split_axis=0, concat_axis=0, tiled=True)
    return (rows, beside, coarse.reshape(-1, copies.shape[2])), others


def on_device(
    node_latents,
    edge_latents,
    senders,
    receivers,
    edge_count,
    edge_in_weight,
    edge_in_bias,
    edge_out_weight,
    edge_out_bias,
    edge_gain,
    edge_shift,
    node_in_weight,
    node_in_bias,
    node_out_weight,
    node_out_bias,
    node_gain,
    node_shift,
):
    half, node_rows = node_latents.shape
    layers = edge_in_weight.shape[0]
    coarse_rows = node_rows // 8
    patch_here = lax.axis_index(PATCH)
    patches = lax.axis_size(PATCH)
    plane = lax.axis_size(PLANE)
    columns = lax.axis_size(Z)
    scalars = jnp.stack([lax.axis_index("width"), edge_count[0]]).astype(jnp.int32)

    rows, copies = node_rows_of(node_latents, columns)

    vectors = jnp.stack(
        [
            edge_in_bias,
            edge_out_bias,
            edge_gain,
            edge_shift,
            node_in_bias,
            node_out_bias,
            node_gain,
            node_shift,
        ],
        axis=1,
    )
    own = (edge_in_weight, edge_out_weight, node_in_weight, node_out_weight, vectors)
    weights = []
    for a in own:
        weights += [a, from_other(a)]

    owner = senders // node_rows
    within = senders - owner * node_rows
    place = (owner % plane) * (patches // plane) + owner // plane
    index = jnp.where(
        owner == patch_here,
        node_rows + within,
        jnp.where(
            owner == (patch_here + patches - 1) % patches,
            within,
            jnp.where(
                owner == (patch_here + 1) % patches,
                2 * node_rows + within,
                3 * node_rows + place * coarse_rows + within,
            ),
        ),
    )
    index = index.reshape(-1, 128)
    receiver = (receivers - patch_here * node_rows)[None, :]

    edges = (edge_latents, from_other(edge_latents))
    nodes = (node_latents, from_other(node_latents))
    others = (weights[1], weights[5], edges[1], index, receiver)
    other_rows = from_other(rows)
    rows = jnp.where(
        lax.axis_index("width") == 0,
        jnp.concatenate([rows, other_rows], axis=1),
        jnp.concatenate([other_rows, rows], axis=1),
    )
    table, others = exchanged(rows, copies, others)
    weights[1], weights[5], other_edges, index, receiver = others
    edges = (edges[0], other_edges)
    ready = prepared(0, scalars, edges, receiver, nodes, weights)
    table, ready = lax.optimization_barrier((table, ready))
    for layer in range(layers):
        last_layer = layer == layers - 1
        sent, *ready = gathered(scalars, ready, index, *table)
        sent = (sent, from_other(sent))
        results = updated_graph(last_layer, scalars, sent, ready, columns)
        if not last_layer:
            edges, nodes = results[:1], results[1:2]
            ready = prepared(layer + 1, scalars, edges, receiver, nodes, weights)
            table, ready = exchanged(results[2], results[3], ready)
    return (results[1], results[0])


def solution(mesh):
    finer = Mesh(
        mesh.devices.reshape(8, 4, 4, mesh.shape["width"]),
        (*PATCH, "width"),
    )
    in_specs = (
        P("width", PATCH),
        P("width", PATCH),
        P(PATCH),
        P(PATCH),
        P(PATCH),
        P(None, "width", None),
        P(None, "width"),
        P(None, "width", None),
        P(None, "width"),
        P(None, "width"),
        P(None, "width"),
        P(None, "width", None),
        P(None, "width"),
        P(None, "width", None),
        P(None, "width"),
        P(None, "width"),
        P(None, "width"),
    )
    out_specs = (P("width", PATCH), P("width", PATCH))
    return jax.shard_map(
        on_device, mesh=finer, in_specs=in_specs, out_specs=out_specs, check_vma=False
    )
```

```python
import functools

import jax
import jax.numpy as jnp
from jax import lax
from jax.experimental import pallas as pl
from jax.experimental.pallas import tpu as pltpu
from jax.sharding import Mesh
from jax.sharding import PartitionSpec as P

Z, Y, X = "patch_0", "patch_1", "patch_2"
PATCH = (Z, Y, X)
PLANE = (Y, X)
EPSILON = 1e-05
EDGE_BLOCK = 512
UPDATE_BLOCK = 1024
ROWS = 32
VMEM_LIMIT = 32 * 1024 * 1024


def dot(left, right, contract=((1,), (0,))):
    return lax.dot_general(left, right, (contract, ((), ())), preferred_element_type=jnp.float32)


def silu(v):
    h = 0.5 * v
    return h + h * jnp.tanh(h)


def layer_norm(values, gain, shift):
    width = values.shape[0]
    mean = jnp.sum(values, axis=0, keepdims=True) * (1.0 / width)
    square = jnp.sum(values * values, axis=0, keepdims=True) * (1.0 / width)
    return (values - mean) * lax.rsqrt(square - mean * mean + EPSILON) * gain + shift


def in_order(first, mine, other):
    return jnp.concatenate([jnp.where(first, mine, other), jnp.where(first, other, mine)], axis=0)


VMEM = pl.BlockSpec(memory_space=pltpu.VMEM)
SMEM = pl.BlockSpec(memory_space=pltpu.SMEM)
HBM = pl.BlockSpec(memory_space=pltpu.HBM)
ANY = pl.BlockSpec(memory_space=pl.ANY)


def shape(dims, dtype=jnp.bfloat16):
    return jax.ShapeDtypeStruct(dims, dtype)


def kernel_call(body, name, out_shape, inputs, in_specs, out_specs, scratch, flops):
    inputs = [
        pltpu.with_memory_space_constraint(a, pltpu.HBM) if spec is HBM else a
        for a, spec in zip(inputs, in_specs)
    ]
    if isinstance(out_specs, list):
        out_shape = [
            pltpu.HBM(a.shape, a.dtype) if spec is HBM else a
            for a, spec in zip(out_shape, out_specs)
        ]
    return pl.pallas_call(
        body,
        in_specs=in_specs,
        out_specs=out_specs,
        out_shape=out_shape,
        scratch_shapes=scratch,
        compiler_params=pltpu.CompilerParams(vmem_limit_bytes=VMEM_LIMIT),
        cost_estimate=pl.CostEstimate(flops=flops, bytes_accessed=4 << 20, transcendentals=0),
        name=name,
    )(*inputs)


def started(pairs, sems):
    copies = [pltpu.make_async_copy(a, b, sems.at[i]) for i, (a, b) in enumerate(pairs)]
    for copy in copies:
        copy.start()
    return copies


def finish(copies):
    for copy in copies:
        copy.wait()


def held(arrays):
    return [pltpu.VMEM(a.shape, a.dtype) for a in arrays]


def columns_of(ref, start, length):
    return ref.at[:, pl.ds(start, length)]


def store_rows(rows, mine, rows_ref, copies_ref):
    rows_ref[...] = rows
    for i in range(copies_ref.shape[0]):
        copies_ref[i] = mine[: copies_ref.shape[1]]


def rows_kernel(nodes_ref, rows_ref, copies_ref, held_ref, sem):
    copies = started([(nodes_ref, held_ref)], sem)
    finish(copies)
    rows = held_ref[...].T
    store_rows(rows, rows, rows_ref, copies_ref)


def node_rows_of(nodes, columns):
    half, node_rows = nodes.shape
    return kernel_call(
        rows_kernel,
        "node_rows",
        [shape((node_rows, half)), shape((columns, node_rows // 8, half))],
        (nodes,),
        [HBM],
        [VMEM, VMEM],
        held([nodes]) + [pltpu.SemaphoreType.DMA((1,))],
        0,
    )


def gather_kernel(n, scalar_ref, index_in, rows_in, beside_in, other_in, coarse_in, *refs):
    ready_in, out_ref, ready_out = refs[:n], refs[n], refs[n + 1 : 2 * n + 1]
    index_ref, near_ref, coarse_ref, sems, ready_sems = refs[2 * n + 1 :]
    core = scalar_ref[0]
    rows, half = other_in.shape
    mine = pl.ds(pl.multiple_of(core * half, half), half)

    def slot(i):
        return near_ref.at[pl.ds(pl.multiple_of(i * rows, rows), rows)]

    copies = started(
        [
            (index_in, index_ref),
            (rows_in.at[:, mine], slot(1)),
            (beside_in.at[:, mine], slot(2 * core)),
            (other_in, slot(2 - 2 * core)),
            (coarse_in, coarse_ref),
        ],
        sems,
    )
    ready_copies = started(list(zip(ready_in, ready_out)), ready_sems)
    finish(copies[:4])
    columns = index_ref[...].T
    lane = lax.broadcasted_iota(jnp.int32, (128, 128), 1)

    def selection(start, first, length):
        blocks = []
        for k in range(start // 128, (start + EDGE_BLOCK) // 128):
            index = jnp.broadcast_to(columns[:, k : k + 1], (128, 128))
            tiles = []
            for j in range(first, first + length, 128):
                tiles.append(jnp.where(index == lane + j, 1.0, 0.0).astype(jnp.bfloat16))
            blocks.append(jnp.concatenate(tiles, axis=1))
        return jnp.concatenate(blocks, axis=0)

    for start in range(0, out_ref.shape[0], EDGE_BLOCK):
        total = dot(selection(start, 0, 3 * rows), near_ref[...])
        if start == 0:
            finish(copies[4:])
        total = total + dot(selection(start, 3 * rows, coarse_ref.shape[0]), coarse_ref[...])
        out_ref[start : start + EDGE_BLOCK, :] = total.astype(jnp.bfloat16)
    finish(ready_copies)


def gathered(scalars, ready, index, rows, beside, other, coarse):
    slots = index.size
    node_rows, half = other.shape
    table = 3 * node_rows + coarse.shape[0]
    n = len(ready)
    return kernel_call(
        functools.partial(gather_kernel, n),
        "gather_senders",
        [shape((slots, half)), *[shape(a.shape, a.dtype) for a in ready]],
        (scalars, index, rows, beside, other, coarse, *ready),
        [SMEM] + [HBM] * 4 + [ANY] + [HBM] * n,
        [VMEM] * (1 + n),
        held([index, shape((3 * node_rows, half)), coarse])
        + [pltpu.SemaphoreType.DMA((5,)), pltpu.SemaphoreType.DMA((n,))],
        2 * slots * half * table,
    )


def prepare_kernel(layer, n_in, n_out, scalar_ref, *refs):
    ins, outs, refs = refs[:n_in], refs[n_in : n_in + n_out], refs[n_in + n_out :]
    held_out, refs = refs[:n_out], refs[n_out:]
    edge_held, node_held, hidden_weight_ref, out_held, vec_held, receiver_ref = refs[:6]
    in_sems, out_sems = refs[6:]
    before_ref, weights_ref, incidence_ref, vectors_ref = held_out[:4]
    first = scalar_ref[0] == 0
    count = scalar_ref[1]
    receiver, (wa, wb, ea, eb, va, vb, oa, ob, vec_a, vec_b) = ins[0], ins[1:11]
    edges_in, nodes_in = ins[11 : 11 + (n_in - 11) // 2], ins[11 + (n_in - 11) // 2 :]
    half = wa.shape[1]
    width = 2 * half

    def part(ref, start):
        return ref.at[layer, :, pl.ds(start, width)]

    def both(sources, target):
        if len(sources) == 1:
            return [(sources[0], target)]
        halves = (target.at[pl.ds(0, half)], target.at[pl.ds(half, half)])
        return list(zip(sources, halves))

    pairs = both(nodes_in, node_held) + [(receiver, receiver_ref)]
    pairs += [(vec_a.at[layer], vec_held.at[0]), (vec_b.at[layer], vec_held.at[1])]
    for k, target in ((2, hidden_weight_ref.at[1]), (0, hidden_weight_ref.at[0])):
        pairs += both((part(wa, k * width), part(wb, k * width)), target)
    pairs += both(edges_in, edge_held)
    pairs += both((ea.at[layer], eb.at[layer]), out_held.at[0])
    pairs += both((oa.at[layer], ob.at[layer]), out_held.at[1])
    pairs += both((part(wa, width), part(wb, width)), weights_ref.at[0])
    for k in (0, 1):
        pairs += both((part(va, k * width), part(vb, k * width)), weights_ref.at[2 + k])
    finish(started(pairs, in_sems))
    sent = [pltpu.make_async_copy(held_out[i], outs[i], out_sems.at[i]) for i in range(n_out)]

    vec = [vec_held[0].T, vec_held[1].T]
    hidden_vec = jnp.concatenate(vec, axis=0)
    feature_vec = in_order(first, *vec)
    nodes = node_held[...]
    edges = edge_held[...]
    if layer == 0:
        nodes = in_order(first, nodes[:half], nodes[half:])
        edges = in_order(first, edges[:half], edges[half:])
        held_out[4][...] = edges
        sent[4].start()
        held_out[5][...] = nodes
        sent[5].start()
    weights_ref[1] = out_held[0].T
    weights_ref[4] = out_held[1].T
    sent[1].start()
    vectors_ref[...] = jnp.concatenate([hidden_vec, feature_vec] + [hidden_vec] * 14, axis=1)
    sent[3].start()
    slots = incidence_ref.shape[1]
    live = lax.broadcasted_iota(jnp.int32, (1, slots), 1) < count
    incidence_ref[...] = jnp.where(
        (lax.broadcasted_iota(jnp.int32, incidence_ref.shape, 0) == receiver_ref[...]) & live,
        1.0,
        0.0,
    ).astype(jnp.bfloat16)
    sent[2].start()
    receiver_part = dot(hidden_weight_ref[1], nodes).astype(jnp.bfloat16)
    before = dot(hidden_weight_ref[0], edges) + dot(receiver_part, incidence_ref[...])
    before_ref[...] = before + hidden_vec[:, 0:1]
    sent[0].start()
    finish(sent)


def prepared(layer, scalars, edges, receiver, nodes, weights):
    slots = edges[0].shape[1]
    node_rows = nodes[0].shape[1]
    width = weights[0].shape[1] * 2
    inputs = (receiver, *weights, *edges, *nodes)
    out_shape = [
        shape((width, slots), jnp.float32),
        shape((5, width, width)),
        shape((node_rows, slots)),
        shape((width, 128), jnp.float32),
    ]
    if layer == 0:
        out_shape += [shape((width, slots)), shape((width, node_rows))]
    n_in, n_out = len(inputs), len(out_shape)
    ready = kernel_call(
        functools.partial(prepare_kernel, layer, n_in, n_out),
        "prepare_layer",
        out_shape,
        (scalars, *inputs),
        [SMEM] + [HBM] * n_in,
        [HBM] * n_out,
        held(
            [
                *out_shape,
                shape((width, slots)),
                shape((width, node_rows)),
                shape((2, width, width)),
                shape((2, width, width)),
                shape((2, *weights[8].shape[1:]), jnp.float32),
                receiver,
            ]
        )
        + [pltpu.SemaphoreType.DMA((21,)), pltpu.SemaphoreType.DMA((n_out,))],
        2 * slots * width * (width + node_rows),
    )
    if layer == 0:
        return ready
    return (*ready, *edges, *nodes)


def update_kernel(last_layer, n_out, scalar_ref, *refs):
    sent_a_ref, sent_b_ref, before_ref, weights_ref, incidence_ref, small_ref = refs[:6]
    edges_ref, nodes_ref, outs, refs = refs[6], refs[7], refs[8 : 8 + n_out], refs[8 + n_out :]
    edge_out_ref, node_out_ref, hidden_ref, mlp_ref, vectors_ref, out_sems = refs
    half = sent_a_ref.shape[1]
    width = 2 * half
    first = scalar_ref[0] == 0
    count = scalar_ref[1]
    sent_out = []

    def send(source, target):
        copy = pltpu.make_async_copy(source, target, out_sems.at[len(sent_out)])
        copy.start()
        sent_out.append(copy)

    small = small_ref[...]
    hidden_vec, feature_vec = small[:, 0:8], small[:, 8:16]
    for i, column in enumerate((1, 2, 3)):
        vectors_ref[i] = jnp.broadcast_to(feature_vec[:, column : column + 1], (width, 128))

    def spread(index, rows):
        return jnp.concatenate([vectors_ref[index, rows, :]] * (UPDATE_BLOCK // 128), axis=1)

    slots = edges_ref.shape[1]
    total = None
    for start in range(0, slots, UPDATE_BLOCK):
        here = slice(start, start + UPDATE_BLOCK)
        sent_a, sent_b = sent_a_ref[here, :], sent_b_ref[here, :]
        low = jnp.where(first, sent_a, sent_b)
        high = jnp.where(first, sent_b, sent_a)
        sent = jnp.concatenate([low, high], axis=1)
        mlp_ref[...] = dot(weights_ref[0], sent, ((1,), (1,)))
        for row in range(0, width, ROWS):
            rows = slice(row, row + ROWS)
            value = silu(mlp_ref[rows, :] + before_ref[rows, here])
            hidden_ref[rows, :] = value.astype(jnp.bfloat16)
        mlp_ref[...] = dot(weights_ref[1], hidden_ref[...])
        new_ref = hidden_ref if last_layer else columns_of(edge_out_ref, start, UPDATE_BLOCK)
        sums = jnp.zeros((8, UPDATE_BLOCK), jnp.float32)
        squares = jnp.zeros((8, UPDATE_BLOCK), jnp.float32)
        for row in range(0, width, ROWS):
            rows = slice(row, row + ROWS)
            value = mlp_ref[rows, :] + spread(0, rows)
            mlp_ref[rows, :] = value
            sums = sums + jnp.sum(value.reshape(ROWS // 8, 8, UPDATE_BLOCK), axis=0)
            squares = squares + jnp.sum((value * value).reshape(ROWS // 8, 8, UPDATE_BLOCK), axis=0)
        mean = jnp.sum(sums, axis=0, keepdims=True) * (1.0 / width)
        square = jnp.sum(squares, axis=0, keepdims=True) * (1.0 / width)
        scale = lax.rsqrt(square - mean * mean + EPSILON)
        live = lax.broadcasted_iota(jnp.int32, (1, UPDATE_BLOCK), 1) + start < count
        for row in range(0, width, ROWS):
            rows = slice(row, row + ROWS)
            value = (mlp_ref[rows, :] - mean) * scale * spread(1, rows) + spread(2, rows)
            value = value + edges_ref[rows, here].astype(jnp.float32)
            new_ref[rows, :] = jnp.where(live, value, 0.0).astype(jnp.bfloat16)
        updated = new_ref[...]
        part = dot(updated, incidence_ref[:, here], ((1,), (1,)))
        total = part if total is None else total + part
        if last_layer:
            edge_out_ref[:, here] = jnp.where(first, updated[:half], updated[half:])
        send(
            columns_of(edge_out_ref, start, UPDATE_BLOCK), columns_of(outs[0], start, UPDATE_BLOCK)
        )
    nodes = nodes_ref[...]
    aggregate = total.astype(jnp.bfloat16)
    node_before = dot(weights_ref[2], nodes) + dot(weights_ref[3], aggregate)
    node_hidden = silu(node_before + hidden_vec[:, 4:5]).astype(jnp.bfloat16)
    node_mlp = dot(weights_ref[4], node_hidden) + feature_vec[:, 5:6]
    new = nodes.astype(jnp.float32) + layer_norm(
        node_mlp, feature_vec[:, 6:7], feature_vec[:, 7:8]
    )
    new = new.astype(jnp.bfloat16)
    mine = jnp.where(first, new[:half], new[half:])
    if last_layer:
        node_out_ref[...] = mine
        send(node_out_ref, outs[1])
    else:
        node_out_ref[...] = new
        send(node_out_ref, outs[1])
        rows = new.T
        store_rows(rows, jnp.where(first, rows[:, :half], rows[:, half:]), *outs[2:])
    finish(sent_out)


def updated_graph(last_layer, scalars, sent, ready, copies):
    slots = ready[0].shape[1]
    node_rows = ready[5].shape[1]
    half = sent[0].shape[1]
    width = 2 * half
    out_width = half if last_layer else width
    out_shape = [shape((out_width, slots)), shape((out_width, node_rows))]
    out_specs = [HBM, HBM]
    if not last_layer:
        out_shape += [shape((node_rows, width)), shape((copies, node_rows // 8, half))]
        out_specs = [HBM, HBM, VMEM, VMEM]
    n_out = len(out_shape)
    return kernel_call(
        functools.partial(update_kernel, last_layer, n_out),
        "update_graph",
        out_shape,
        (scalars, *sent, *ready),
        [SMEM] + [VMEM] * (2 + len(ready)),
        out_specs,
        held(
            [
                *out_shape[:2],
                shape((width, UPDATE_BLOCK)),
                shape((width, UPDATE_BLOCK), jnp.float32),
                shape((3, width, 128), jnp.float32),
            ]
        )
        + [pltpu.SemaphoreType.DMA((slots // UPDATE_BLOCK + 1,))],
        2 * slots * width * (2 * width + node_rows),
    )


def from_other(a):
    return lax.ppermute(a, "width", [(0, 1), (1, 0)])


def copies_kernel(rows_ref, copies_ref):
    rows = rows_ref[...]
    for i in range(copies_ref.shape[0]):
        copies_ref[i] = rows


def copied(rows, count):
    return kernel_call(
        copies_kernel, "copies", shape((count, *rows.shape)), (rows,), [VMEM], VMEM, [], 0
    )


def exchanged(rows, copies, others=()):
    size = lax.axis_size(PATCH)
    pairs = []
    for i in range(size):
        pairs += [(2 * i, (i + 1) % size * 2), (2 * i + 1, (i - 1) % size * 2 + 1)]
    beside = lax.ppermute(rows, (*PATCH, "width"), pairs)
    column = lax.all_to_all(copies, Z, split_axis=0, concat_axis=0, tiled=True)
    column = column.reshape(-1, copies.shape[2])
    column, others = lax.optimization_barrier((column, others))
    plane = copied(column, lax.axis_size(PLANE))
    coarse = lax.all_to_all(plane, PLANE, split_axis=0, concat_axis=0, tiled=True)
    return (rows, beside, coarse.reshape(-1, copies.shape[2])), others


def completed(table, ready):
    rows, beside, coarse = table
    beside, ready = lax.optimization_barrier((beside, ready))
    half = coarse.shape[1]
    theirs = (1 - lax.axis_index("width")) * half
    other = from_other(lax.dynamic_slice_in_dim(beside, theirs, half, 1))
    return (rows, beside, other, coarse), ready


def on_device(
    node_latents,
    edge_latents,
    senders,
    receivers,
    edge_count,
    edge_in_weight,
    edge_in_bias,
    edge_out_weight,
    edge_out_bias,
    edge_gain,
    edge_shift,
    node_in_weight,
    node_in_bias,
    node_out_weight,
    node_out_bias,
    node_gain,
    node_shift,
):
    half, node_rows = node_latents.shape
    layers = edge_in_weight.shape[0]
    coarse_rows = node_rows // 8
    patch_here = lax.axis_index(PATCH)
    patches = lax.axis_size(PATCH)
    plane = lax.axis_size(PLANE)
    columns = lax.axis_size(Z)
    scalars = jnp.stack([lax.axis_index("width"), edge_count[0]]).astype(jnp.int32)

    rows, copies = node_rows_of(node_latents, columns)

    vectors = jnp.stack(
        [
            edge_in_bias,
            edge_out_bias,
            edge_gain,
            edge_shift,
            node_in_bias,
            node_out_bias,
            node_gain,
            node_shift,
        ],
        axis=1,
    )
    own = (edge_in_weight, edge_out_weight, node_in_weight, node_out_weight, vectors)
    weights = []
    for a in own:
        weights += [a, from_other(a)]

    owner = senders // node_rows
    within = senders - owner * node_rows
    place = (owner % plane) * (patches // plane) + owner // plane
    index = jnp.where(
        owner == patch_here,
        node_rows + within,
        jnp.where(
            owner == (patch_here + patches - 1) % patches,
            within,
            jnp.where(
                owner == (patch_here + 1) % patches,
                2 * node_rows + within,
                3 * node_rows + place * coarse_rows + within,
            ),
        ),
    )
    index = index.reshape(-1, 128)
    receiver = (receivers - patch_here * node_rows)[None, :]

    edges = (edge_latents, from_other(edge_latents))
    nodes = (node_latents, from_other(node_latents))
    others = (weights[1], weights[5], edges[1], index, receiver)
    other_rows = from_other(rows)
    rows = jnp.where(
        lax.axis_index("width") == 0,
        jnp.concatenate([rows, other_rows], axis=1),
        jnp.concatenate([other_rows, rows], axis=1),
    )
    table, others = exchanged(rows, copies, others)
    weights[1], weights[5], other_edges, index, receiver = others
    edges = (edges[0], other_edges)
    for layer in range(layers):
        last_layer = layer == layers - 1
        ready = prepared(layer, scalars, edges, receiver, nodes, weights)
        table, ready = completed(table, ready)
        table, ready = lax.optimization_barrier((table, ready))
        sent, *ready = gathered(scalars, ready, index, *table)
        sent = (sent, from_other(sent))
        results = updated_graph(last_layer, scalars, sent, ready, columns)
        if not last_layer:
            edges, nodes = results[:1], results[1:2]
            table, _ = exchanged(results[2], results[3])
    return (results[1], results[0])


def solution(mesh):
    finer = Mesh(
        mesh.devices.reshape(8, 4, 4, mesh.shape["width"]),
        (*PATCH, "width"),
    )
    in_specs = (
        P("width", PATCH),
        P("width", PATCH),
        P(PATCH),
        P(PATCH),
        P(PATCH),
        P(None, "width", None),
        P(None, "width"),
        P(None, "width", None),
        P(None, "width"),
        P(None, "width"),
        P(None, "width"),
        P(None, "width", None),
        P(None, "width"),
        P(None, "width", None),
        P(None, "width"),
        P(None, "width"),
        P(None, "width"),
    )
    out_specs = (P("width", PATCH), P("width", PATCH))
    return jax.shard_map(
        on_device, mesh=finer, in_specs=in_specs, out_specs=out_specs, check_vma=False
    )
```

```python
import functools

import jax
import jax.numpy as jnp
from jax import lax
from jax.experimental import pallas as pl
from jax.experimental.pallas import tpu as pltpu
from jax.sharding import Mesh
from jax.sharding import PartitionSpec as P

Z, Y, X = "patch_0", "patch_1", "patch_2"
PATCH = (Z, Y, X)
PLANE = (Y, X)
EPSILON = 1e-05
EDGE_BLOCK = 512
UPDATE_BLOCK = 1024
ROWS = 32
VMEM_LIMIT = 32 * 1024 * 1024


def dot(left, right, contract=((1,), (0,))):
    return lax.dot_general(left, right, (contract, ((), ())), preferred_element_type=jnp.float32)


def silu(v):
    h = 0.5 * v
    return h + h * jnp.tanh(h)


def layer_norm(values, gain, shift):
    width = values.shape[0]
    mean = jnp.sum(values, axis=0, keepdims=True) * (1.0 / width)
    square = jnp.sum(values * values, axis=0, keepdims=True) * (1.0 / width)
    return (values - mean) * lax.rsqrt(square - mean * mean + EPSILON) * gain + shift


def in_order(first, mine, other):
    return jnp.concatenate([jnp.where(first, mine, other), jnp.where(first, other, mine)], axis=0)


VMEM = pl.BlockSpec(memory_space=pltpu.VMEM)
SMEM = pl.BlockSpec(memory_space=pltpu.SMEM)
HBM = pl.BlockSpec(memory_space=pltpu.HBM)
ANY = pl.BlockSpec(memory_space=pl.ANY)


def shape(dims, dtype=jnp.bfloat16):
    return jax.ShapeDtypeStruct(dims, dtype)


def kernel_call(body, name, out_shape, inputs, in_specs, out_specs, scratch, flops):
    inputs = [
        pltpu.with_memory_space_constraint(a, pltpu.HBM) if spec is HBM else a
        for a, spec in zip(inputs, in_specs)
    ]
    if isinstance(out_specs, list):
        out_shape = [
            pltpu.HBM(a.shape, a.dtype) if spec is HBM else a
            for a, spec in zip(out_shape, out_specs)
        ]
    return pl.pallas_call(
        body,
        in_specs=in_specs,
        out_specs=out_specs,
        out_shape=out_shape,
        scratch_shapes=scratch,
        compiler_params=pltpu.CompilerParams(vmem_limit_bytes=VMEM_LIMIT),
        cost_estimate=pl.CostEstimate(flops=flops, bytes_accessed=4 << 20, transcendentals=0),
        name=name,
    )(*inputs)


def started(pairs, sems):
    copies = [pltpu.make_async_copy(a, b, sems.at[i]) for i, (a, b) in enumerate(pairs)]
    for copy in copies:
        copy.start()
    return copies


def finish(copies):
    for copy in copies:
        copy.wait()


def held(arrays):
    return [pltpu.VMEM(a.shape, a.dtype) for a in arrays]


def columns_of(ref, start, length):
    return ref.at[:, pl.ds(start, length)]


def store_rows(rows, mine, rows_ref, copies_ref):
    rows_ref[...] = rows
    for i in range(copies_ref.shape[0]):
        copies_ref[i] = mine[: copies_ref.shape[1]]


def rows_kernel(nodes_ref, rows_ref, copies_ref, held_ref, sem):
    copies = started([(nodes_ref, held_ref)], sem)
    finish(copies)
    rows = held_ref[...].T
    store_rows(rows, rows, rows_ref, copies_ref)


def node_rows_of(nodes, columns):
    half, node_rows = nodes.shape
    return kernel_call(
        rows_kernel,
        "node_rows",
        [shape((node_rows, half)), shape((columns, node_rows // 8, half))],
        (nodes,),
        [HBM],
        [VMEM, VMEM],
        held([nodes]) + [pltpu.SemaphoreType.DMA((1,))],
        0,
    )


def gather_kernel(n, scalar_ref, index_in, rows_in, beside_in, other_in, coarse_in, *refs):
    ready_in, out_ref, ready_out = refs[:n], refs[n], refs[n + 1 : 2 * n + 1]
    index_ref, near_ref, coarse_ref, sems, ready_sems = refs[2 * n + 1 :]
    core = scalar_ref[0]
    rows, half = other_in.shape
    mine = pl.ds(pl.multiple_of(core * half, half), half)

    def slot(i):
        return near_ref.at[pl.ds(pl.multiple_of(i * rows, rows), rows)]

    copies = started(
        [
            (index_in, index_ref),
            (rows_in.at[:, mine], slot(1)),
            (beside_in.at[:, mine], slot(2 * core)),
            (other_in, slot(2 - 2 * core)),
            (coarse_in, coarse_ref),
        ],
        sems,
    )
    ready_copies = started(list(zip(ready_in, ready_out)), ready_sems)
    finish(copies[:4])
    columns = index_ref[...].T
    lane = lax.broadcasted_iota(jnp.int32, (128, 128), 1)

    def selection(start, first, length):
        blocks = []
        for k in range(start // 128, (start + EDGE_BLOCK) // 128):
            index = jnp.broadcast_to(columns[:, k : k + 1], (128, 128))
            tiles = []
            for j in range(first, first + length, 128):
                tiles.append(jnp.where(index == lane + j, 1.0, 0.0).astype(jnp.bfloat16))
            blocks.append(jnp.concatenate(tiles, axis=1))
        return jnp.concatenate(blocks, axis=0)

    for start in range(0, out_ref.shape[0], EDGE_BLOCK):
        total = dot(selection(start, 0, 3 * rows), near_ref[...])
        if start == 0:
            finish(copies[4:])
        total = total + dot(selection(start, 3 * rows, coarse_ref.shape[0]), coarse_ref[...])
        out_ref[start : start + EDGE_BLOCK, :] = total.astype(jnp.bfloat16)
    finish(ready_copies)


def gathered(scalars, ready, index, rows, beside, other, coarse):
    slots = index.size
    node_rows, half = other.shape
    table = 3 * node_rows + coarse.shape[0]
    n = len(ready)
    return kernel_call(
        functools.partial(gather_kernel, n),
        "gather_senders",
        [shape((slots, half)), *[shape(a.shape, a.dtype) for a in ready]],
        (scalars, index, rows, beside, other, coarse, *ready),
        [SMEM] + [HBM] * 4 + [ANY] + [HBM] * n,
        [VMEM] * (1 + n),
        held([index, shape((3 * node_rows, half)), coarse])
        + [pltpu.SemaphoreType.DMA((5,)), pltpu.SemaphoreType.DMA((n,))],
        2 * slots * half * table,
    )


def prepare_kernel(layer, n_in, n_out, scalar_ref, *refs):
    ins, outs, refs = refs[:n_in], refs[n_in : n_in + n_out], refs[n_in + n_out :]
    held_out, refs = refs[:n_out], refs[n_out:]
    edge_held, node_held, hidden_weight_ref, out_held, vec_held, receiver_ref = refs[:6]
    in_sems, out_sems = refs[6:]
    before_ref, weights_ref, incidence_ref, vectors_ref = held_out[:4]
    first = scalar_ref[0] == 0
    count = scalar_ref[1]
    receiver, (wa, wb, ea, eb, va, vb, oa, ob, vec_a, vec_b) = ins[0], ins[1:11]
    edges_in, nodes_in = ins[11 : 11 + (n_in - 11) // 2], ins[11 + (n_in - 11) // 2 :]
    half = wa.shape[1]
    width = 2 * half

    def part(ref, start):
        return ref.at[layer, :, pl.ds(start, width)]

    def both(sources, target):
        if len(sources) == 1:
            return [(sources[0], target)]
        halves = (target.at[pl.ds(0, half)], target.at[pl.ds(half, half)])
        return list(zip(sources, halves))

    pairs = both(nodes_in, node_held) + [(receiver, receiver_ref)]
    pairs += [(vec_a.at[layer], vec_held.at[0]), (vec_b.at[layer], vec_held.at[1])]
    for k, target in ((2, hidden_weight_ref.at[1]), (0, hidden_weight_ref.at[0])):
        pairs += both((part(wa, k * width), part(wb, k * width)), target)
    pairs += both(edges_in, edge_held)
    pairs += both((ea.at[layer], eb.at[layer]), out_held.at[0])
    pairs += both((oa.at[layer], ob.at[layer]), out_held.at[1])
    pairs += both((part(wa, width), part(wb, width)), weights_ref.at[0])
    for k in (0, 1):
        pairs += both((part(va, k * width), part(vb, k * width)), weights_ref.at[2 + k])
    finish(started(pairs, in_sems))
    sent = [pltpu.make_async_copy(held_out[i], outs[i], out_sems.at[i]) for i in range(n_out)]

    vec = [vec_held[0].T, vec_held[1].T]
    hidden_vec = jnp.concatenate(vec, axis=0)
    feature_vec = in_order(first, *vec)
    nodes = node_held[...]
    edges = edge_held[...]
    if layer == 0:
        nodes = in_order(first, nodes[:half], nodes[half:])
        edges = in_order(first, edges[:half], edges[half:])
        held_out[4][...] = edges
        sent[4].start()
        held_out[5][...] = nodes
        sent[5].start()
    weights_ref[1] = out_held[0].T
    weights_ref[4] = out_held[1].T
    sent[1].start()
    vectors_ref[...] = jnp.concatenate([hidden_vec, feature_vec] + [hidden_vec] * 14, axis=1)
    sent[3].start()
    slots = incidence_ref.shape[1]
    live = lax.broadcasted_iota(jnp.int32, (1, slots), 1) < count
    incidence_ref[...] = jnp.where(
        (lax.broadcasted_iota(jnp.int32, incidence_ref.shape, 0) == receiver_ref[...]) & live,
        1.0,
        0.0,
    ).astype(jnp.bfloat16)
    sent[2].start()
    receiver_part = dot(hidden_weight_ref[1], nodes).astype(jnp.bfloat16)
    before = dot(hidden_weight_ref[0], edges) + dot(receiver_part, incidence_ref[...])
    before_ref[...] = before + hidden_vec[:, 0:1]
    sent[0].start()
    finish(sent)


def prepared(layer, scalars, edges, receiver, nodes, weights):
    slots = edges[0].shape[1]
    node_rows = nodes[0].shape[1]
    width = weights[0].shape[1] * 2
    inputs = (receiver, *weights, *edges, *nodes)
    out_shape = [
        shape((width, slots), jnp.float32),
        shape((5, width, width)),
        shape((node_rows, slots)),
        shape((width, 128), jnp.float32),
    ]
    if layer == 0:
        out_shape += [shape((width, slots)), shape((width, node_rows))]
    n_in, n_out = len(inputs), len(out_shape)
    ready = kernel_call(
        functools.partial(prepare_kernel, layer, n_in, n_out),
        "prepare_layer",
        out_shape,
        (scalars, *inputs),
        [SMEM] + [HBM] * n_in,
        [HBM] * n_out,
        held(
            [
                *out_shape,
                shape((width, slots)),
                shape((width, node_rows)),
                shape((2, width, width)),
                shape((2, width, width)),
                shape((2, *weights[8].shape[1:]), jnp.float32),
                receiver,
            ]
        )
        + [pltpu.SemaphoreType.DMA((21,)), pltpu.SemaphoreType.DMA((n_out,))],
        2 * slots * width * (width + node_rows),
    )
    if layer == 0:
        return ready
    return (*ready, *edges, *nodes)


def update_kernel(last_layer, block, n_out, scalar_ref, *refs):
    sent_a_ref, sent_b_ref, before_ref, weights_ref, incidence_ref, small_ref = refs[:6]
    edges_ref, nodes_ref, outs, refs = refs[6], refs[7], refs[8 : 8 + n_out], refs[8 + n_out :]
    edge_out_ref, node_out_ref, hidden_ref, mlp_ref, vectors_ref, out_sems = refs
    half = sent_a_ref.shape[1]
    width = 2 * half
    first = scalar_ref[0] == 0
    count = scalar_ref[1]
    sent_out = []

    def send(source, target):
        copy = pltpu.make_async_copy(source, target, out_sems.at[len(sent_out)])
        copy.start()
        sent_out.append(copy)

    small = small_ref[...]
    hidden_vec, feature_vec = small[:, 0:8], small[:, 8:16]
    for i, column in enumerate((1, 2, 3)):
        vectors_ref[i] = jnp.broadcast_to(feature_vec[:, column : column + 1], (width, 128))

    def spread(index, rows):
        return jnp.concatenate([vectors_ref[index, rows, :]] * (block // 128), axis=1)

    slots = edges_ref.shape[1]
    total = None
    for start in range(0, slots, block):
        here = slice(start, start + block)
        sent_a, sent_b = sent_a_ref[here, :], sent_b_ref[here, :]
        low = jnp.where(first, sent_a, sent_b)
        high = jnp.where(first, sent_b, sent_a)
        sent = jnp.concatenate([low, high], axis=1)
        mlp_ref[...] = dot(weights_ref[0], sent, ((1,), (1,)))
        for row in range(0, width, ROWS):
            rows = slice(row, row + ROWS)
            value = silu(mlp_ref[rows, :] + before_ref[rows, here])
            hidden_ref[rows, :] = value.astype(jnp.bfloat16)
        mlp_ref[...] = dot(weights_ref[1], hidden_ref[...])
        new_ref = hidden_ref if last_layer else columns_of(edge_out_ref, start, block)
        sums = jnp.zeros((8, block), jnp.float32)
        squares = jnp.zeros((8, block), jnp.float32)
        for row in range(0, width, ROWS):
            rows = slice(row, row + ROWS)
            value = mlp_ref[rows, :] + spread(0, rows)
            mlp_ref[rows, :] = value
            sums = sums + jnp.sum(value.reshape(ROWS // 8, 8, block), axis=0)
            squares = squares + jnp.sum((value * value).reshape(ROWS // 8, 8, block), axis=0)
        mean = jnp.sum(sums, axis=0, keepdims=True) * (1.0 / width)
        square = jnp.sum(squares, axis=0, keepdims=True) * (1.0 / width)
        scale = lax.rsqrt(square - mean * mean + EPSILON)
        live = lax.broadcasted_iota(jnp.int32, (1, block), 1) + start < count
        for row in range(0, width, ROWS):
            rows = slice(row, row + ROWS)
            value = (mlp_ref[rows, :] - mean) * scale * spread(1, rows) + spread(2, rows)
            value = value + edges_ref[rows, here].astype(jnp.float32)
            new_ref[rows, :] = jnp.where(live, value, 0.0).astype(jnp.bfloat16)
        updated = new_ref[...]
        part = dot(updated, incidence_ref[:, here], ((1,), (1,)))
        total = part if total is None else total + part
        if last_layer:
            edge_out_ref[:, here] = jnp.where(first, updated[:half], updated[half:])
        send(
            columns_of(edge_out_ref, start, block), columns_of(outs[0], start, block)
        )
    nodes = nodes_ref[...]
    aggregate = total.astype(jnp.bfloat16)
    node_before = dot(weights_ref[2], nodes) + dot(weights_ref[3], aggregate)
    node_hidden = silu(node_before + hidden_vec[:, 4:5]).astype(jnp.bfloat16)
    node_mlp = dot(weights_ref[4], node_hidden) + feature_vec[:, 5:6]
    new = nodes.astype(jnp.float32) + layer_norm(
        node_mlp, feature_vec[:, 6:7], feature_vec[:, 7:8]
    )
    new = new.astype(jnp.bfloat16)
    mine = jnp.where(first, new[:half], new[half:])
    if last_layer:
        node_out_ref[...] = mine
        send(node_out_ref, outs[1])
    else:
        node_out_ref[...] = new
        send(node_out_ref, outs[1])
        rows = new.T
        store_rows(rows, jnp.where(first, rows[:, :half], rows[:, half:]), *outs[2:])
    finish(sent_out)


def updated_graph(last_layer, scalars, sent, ready, copies):
    block = UPDATE_BLOCK if last_layer else UPDATE_BLOCK // 2
    slots = ready[0].shape[1]
    node_rows = ready[5].shape[1]
    half = sent[0].shape[1]
    width = 2 * half
    out_width = half if last_layer else width
    out_shape = [shape((out_width, slots)), shape((out_width, node_rows))]
    out_specs = [HBM, HBM]
    if not last_layer:
        out_shape += [shape((node_rows, width)), shape((copies, node_rows // 8, half))]
        out_specs = [HBM, HBM, VMEM, VMEM]
    n_out = len(out_shape)
    return kernel_call(
        functools.partial(update_kernel, last_layer, block, n_out),
        "update_graph",
        out_shape,
        (scalars, *sent, *ready),
        [SMEM] + [VMEM] * (2 + len(ready)),
        out_specs,
        held(
            [
                *out_shape[:2],
                shape((width, block)),
                shape((width, block), jnp.float32),
                shape((3, width, 128), jnp.float32),
            ]
        )
        + [pltpu.SemaphoreType.DMA((slots // block + 1,))],
        2 * slots * width * (2 * width + node_rows),
    )


def from_other(a):
    return lax.ppermute(a, "width", [(0, 1), (1, 0)])


def copies_kernel(rows_ref, copies_ref, sems):
    finish(started([(rows_ref, copies_ref.at[i]) for i in range(copies_ref.shape[0])], sems))


def copied(rows, count):
    sems = [pltpu.SemaphoreType.DMA((count,))]
    return kernel_call(
        copies_kernel, "copies", [shape((count, *rows.shape))], (rows,), [VMEM], [HBM], sems, 0
    )[0]


def exchanged(rows, copies, others=()):
    size = lax.axis_size(PATCH)
    pairs = []
    for i in range(size):
        pairs += [(2 * i, (i + 1) % size * 2), (2 * i + 1, (i - 1) % size * 2 + 1)]
    beside = lax.ppermute(rows, (*PATCH, "width"), pairs)
    column = lax.all_to_all(copies, Z, split_axis=0, concat_axis=0, tiled=True)
    column = column.reshape(-1, copies.shape[2])
    column, others = lax.optimization_barrier((column, others))
    plane = copied(column, lax.axis_size(PLANE))
    coarse = lax.all_to_all(plane, PLANE, split_axis=0, concat_axis=0, tiled=True)
    return (rows, beside, coarse.reshape(-1, copies.shape[2])), others


def completed(table, ready):
    rows, beside, coarse = table
    beside, ready = lax.optimization_barrier((beside, ready))
    half = coarse.shape[1]
    theirs = (1 - lax.axis_index("width")) * half
    other = from_other(lax.dynamic_slice_in_dim(beside, theirs, half, 1))
    return (rows, beside, other, coarse), ready


def on_device(
    node_latents,
    edge_latents,
    senders,
    receivers,
    edge_count,
    edge_in_weight,
    edge_in_bias,
    edge_out_weight,
    edge_out_bias,
    edge_gain,
    edge_shift,
    node_in_weight,
    node_in_bias,
    node_out_weight,
    node_out_bias,
    node_gain,
    node_shift,
):
    half, node_rows = node_latents.shape
    layers = edge_in_weight.shape[0]
    coarse_rows = node_rows // 8
    patch_here = lax.axis_index(PATCH)
    patches = lax.axis_size(PATCH)
    plane = lax.axis_size(PLANE)
    columns = lax.axis_size(Z)
    scalars = jnp.stack([lax.axis_index("width"), edge_count[0]]).astype(jnp.int32)

    rows, copies = node_rows_of(node_latents, columns)

    vectors = jnp.stack(
        [
            edge_in_bias,
            edge_out_bias,
            edge_gain,
            edge_shift,
            node_in_bias,
            node_out_bias,
            node_gain,
            node_shift,
        ],
        axis=1,
    )
    own = (edge_in_weight, edge_out_weight, node_in_weight, node_out_weight, vectors)
    weights = []
    for a in own:
        weights += [a, from_other(a)]

    owner = senders // node_rows
    within = senders - owner * node_rows
    place = (owner % plane) * (patches // plane) + owner // plane
    index = jnp.where(
        owner == patch_here,
        node_rows + within,
        jnp.where(
            owner == (patch_here + patches - 1) % patches,
            within,
            jnp.where(
                owner == (patch_here + 1) % patches,
                2 * node_rows + within,
                3 * node_rows + place * coarse_rows + within,
            ),
        ),
    )
    index = index.reshape(-1, 128)
    receiver = (receivers - patch_here * node_rows)[None, :]

    edges = (edge_latents, from_other(edge_latents))
    nodes = (node_latents, from_other(node_latents))
    others = (weights[1], weights[5], edges[1], index, receiver)
    other_rows = from_other(rows)
    rows = jnp.where(
        lax.axis_index("width") == 0,
        jnp.concatenate([rows, other_rows], axis=1),
        jnp.concatenate([other_rows, rows], axis=1),
    )
    table, others = exchanged(rows, copies, others)
    weights[1], weights[5], other_edges, index, receiver = others
    edges = (edges[0], other_edges)
    for layer in range(layers):
        last_layer = layer == layers - 1
        ready = prepared(layer, scalars, edges, receiver, nodes, weights)
        table, ready = completed(table, ready)
        table, ready = lax.optimization_barrier((table, ready))
        sent, *ready = gathered(scalars, ready, index, *table)
        sent = (sent, from_other(sent))
        results = updated_graph(last_layer, scalars, sent, ready, columns)
        if not last_layer:
            edges, nodes = results[:1], results[1:2]
            table, _ = exchanged(results[2], results[3])
    return (results[1], results[0])


def solution(mesh):
    finer = Mesh(
        mesh.devices.reshape(8, 4, 4, mesh.shape["width"]),
        (*PATCH, "width"),
    )
    in_specs = (
        P("width", PATCH),
        P("width", PATCH),
        P(PATCH),
        P(PATCH),
        P(PATCH),
        P(None, "width", None),
        P(None, "width"),
        P(None, "width", None),
        P(None, "width"),
        P(None, "width"),
        P(None, "width"),
        P(None, "width", None),
        P(None, "width"),
        P(None, "width", None),
        P(None, "width"),
        P(None, "width"),
        P(None, "width"),
    )
    out_specs = (P("width", PATCH), P("width", PATCH))
    return jax.shard_map(
        on_device, mesh=finer, in_specs=in_specs, out_specs=out_specs, check_vma=False
    )
```

```python
import functools

import jax
import jax.numpy as jnp
from jax import lax
from jax.experimental import pallas as pl
from jax.experimental.pallas import tpu as pltpu
from jax.sharding import Mesh
from jax.sharding import PartitionSpec as P

Z, Y, X = "patch_0", "patch_1", "patch_2"
PATCH = (Z, Y, X)
PLANE = (Y, X)
EPSILON = 1e-05
EDGE_BLOCK = 512
UPDATE_BLOCK = 1024
ROWS = 32
VMEM_LIMIT = 32 * 1024 * 1024


def dot(left, right, contract=((1,), (0,))):
    return lax.dot_general(left, right, (contract, ((), ())), preferred_element_type=jnp.float32)


def silu(v):
    h = 0.5 * v
    return h + h * jnp.tanh(h)


def layer_norm(values, gain, shift):
    width = values.shape[0]
    mean = jnp.sum(values, axis=0, keepdims=True) * (1.0 / width)
    square = jnp.sum(values * values, axis=0, keepdims=True) * (1.0 / width)
    return (values - mean) * lax.rsqrt(square - mean * mean + EPSILON) * gain + shift


def in_order(first, mine, other):
    return jnp.concatenate([jnp.where(first, mine, other), jnp.where(first, other, mine)], axis=0)


VMEM = pl.BlockSpec(memory_space=pltpu.VMEM)
SMEM = pl.BlockSpec(memory_space=pltpu.SMEM)
HBM = pl.BlockSpec(memory_space=pltpu.HBM)
ANY = pl.BlockSpec(memory_space=pl.ANY)


def shape(dims, dtype=jnp.bfloat16):
    return jax.ShapeDtypeStruct(dims, dtype)


def kernel_call(body, name, out_shape, inputs, in_specs, out_specs, scratch, flops):
    inputs = [
        pltpu.with_memory_space_constraint(a, pltpu.HBM) if spec is HBM else a
        for a, spec in zip(inputs, in_specs)
    ]
    if isinstance(out_specs, list):
        out_shape = [
            pltpu.HBM(a.shape, a.dtype) if spec is HBM else a
            for a, spec in zip(out_shape, out_specs)
        ]
    return pl.pallas_call(
        body,
        in_specs=in_specs,
        out_specs=out_specs,
        out_shape=out_shape,
        scratch_shapes=scratch,
        compiler_params=pltpu.CompilerParams(vmem_limit_bytes=VMEM_LIMIT),
        cost_estimate=pl.CostEstimate(flops=flops, bytes_accessed=4 << 20, transcendentals=0),
        name=name,
    )(*inputs)


def started(pairs, sems):
    copies = [pltpu.make_async_copy(a, b, sems.at[i]) for i, (a, b) in enumerate(pairs)]
    for copy in copies:
        copy.start()
    return copies


def finish(copies):
    for copy in copies:
        copy.wait()


def held(arrays):
    return [pltpu.VMEM(a.shape, a.dtype) for a in arrays]


def columns_of(ref, start, length):
    return ref.at[:, pl.ds(start, length)]


def store_rows(rows, mine, rows_ref, copies_ref):
    rows_ref[...] = rows
    for i in range(copies_ref.shape[0]):
        copies_ref[i] = mine[: copies_ref.shape[1]]


def rows_kernel(nodes_ref, rows_ref, copies_ref, held_ref, sem):
    copies = started([(nodes_ref, held_ref)], sem)
    finish(copies)
    rows = held_ref[...].T
    store_rows(rows, rows, rows_ref, copies_ref)


def node_rows_of(nodes, columns):
    half, node_rows = nodes.shape
    return kernel_call(
        rows_kernel,
        "node_rows",
        [shape((node_rows, half)), shape((columns, node_rows // 8, half))],
        (nodes,),
        [HBM],
        [VMEM, VMEM],
        held([nodes]) + [pltpu.SemaphoreType.DMA((1,))],
        0,
    )


def gather_kernel(n, scalar_ref, index_in, rows_in, beside_in, other_in, coarse_in, *refs):
    ready_in, out_ref, ready_out = refs[:n], refs[n], refs[n + 1 : 2 * n + 1]
    index_ref, near_ref, coarse_ref, sems, ready_sems = refs[2 * n + 1 :]
    core = scalar_ref[0]
    rows, half = other_in.shape
    mine = pl.ds(pl.multiple_of(core * half, half), half)

    def slot(i):
        return near_ref.at[pl.ds(pl.multiple_of(i * rows, rows), rows)]

    copies = started(
        [
            (index_in, index_ref),
            (rows_in.at[:, mine], slot(1)),
            (beside_in.at[:, mine], slot(2 * core)),
            (other_in, slot(2 - 2 * core)),
            (coarse_in, coarse_ref),
        ],
        sems,
    )
    ready_copies = started(list(zip(ready_in, ready_out)), ready_sems)
    finish(copies[:4])
    columns = index_ref[...].T
    lane = lax.broadcasted_iota(jnp.int32, (128, 128), 1)

    def selection(start, first, length):
        blocks = []
        for k in range(start // 128, (start + EDGE_BLOCK) // 128):
            index = jnp.broadcast_to(columns[:, k : k + 1], (128, 128))
            tiles = []
            for j in range(first, first + length, 128):
                tiles.append(jnp.where(index == lane + j, 1.0, 0.0).astype(jnp.bfloat16))
            blocks.append(jnp.concatenate(tiles, axis=1))
        return jnp.concatenate(blocks, axis=0)

    for start in range(0, out_ref.shape[0], EDGE_BLOCK):
        total = dot(selection(start, 0, 3 * rows), near_ref[...])
        if start == 0:
            finish(copies[4:])
        total = total + dot(selection(start, 3 * rows, coarse_ref.shape[0]), coarse_ref[...])
        out_ref[start : start + EDGE_BLOCK, :] = total.astype(jnp.bfloat16)
    finish(ready_copies)


def gathered(scalars, ready, index, rows, beside, other, coarse):
    slots = index.size
    node_rows, half = other.shape
    table = 3 * node_rows + coarse.shape[0]
    n = len(ready)
    return kernel_call(
        functools.partial(gather_kernel, n),
        "gather_senders",
        [shape((slots, half)), *[shape(a.shape, a.dtype) for a in ready]],
        (scalars, index, rows, beside, other, coarse, *ready),
        [SMEM] + [HBM] * 4 + [ANY] + [HBM] * n,
        [VMEM] * (1 + n),
        held([index, shape((3 * node_rows, half)), coarse])
        + [pltpu.SemaphoreType.DMA((5,)), pltpu.SemaphoreType.DMA((n,))],
        2 * slots * half * table,
    )


def prepare_kernel(layer, n_in, n_out, scalar_ref, *refs):
    ins, outs, refs = refs[:n_in], refs[n_in : n_in + n_out], refs[n_in + n_out :]
    held_out, refs = refs[:n_out], refs[n_out:]
    edge_held, node_held, hidden_weight_ref, out_held, vec_held, receiver_ref = refs[:6]
    in_sems, out_sems = refs[6:]
    before_ref, weights_ref, incidence_ref, vectors_ref = held_out[:4]
    first = scalar_ref[0] == 0
    count = scalar_ref[1]
    receiver, (wa, wb, ea, eb, va, vb, oa, ob, vec_a, vec_b) = ins[0], ins[1:11]
    edges_in, nodes_in = ins[11 : 11 + (n_in - 11) // 2], ins[11 + (n_in - 11) // 2 :]
    half = wa.shape[1]
    width = 2 * half

    def part(ref, start):
        return ref.at[layer, :, pl.ds(start, width)]

    def both(sources, target):
        if len(sources) == 1:
            return [(sources[0], target)]
        halves = (target.at[pl.ds(0, half)], target.at[pl.ds(half, half)])
        return list(zip(sources, halves))

    pairs = both(nodes_in, node_held) + [(receiver, receiver_ref)]
    pairs += [(vec_a.at[layer], vec_held.at[0]), (vec_b.at[layer], vec_held.at[1])]
    for k, target in ((2, hidden_weight_ref.at[1]), (0, hidden_weight_ref.at[0])):
        pairs += both((part(wa, k * width), part(wb, k * width)), target)
    pairs += both(edges_in, edge_held)
    pairs += both((ea.at[layer], eb.at[layer]), out_held.at[0])
    pairs += both((oa.at[layer], ob.at[layer]), out_held.at[1])
    pairs += both((part(wa, width), part(wb, width)), weights_ref.at[0])
    for k in (0, 1):
        pairs += both((part(va, k * width), part(vb, k * width)), weights_ref.at[2 + k])
    finish(started(pairs, in_sems))
    sent = [pltpu.make_async_copy(held_out[i], outs[i], out_sems.at[i]) for i in range(n_out)]

    vec = [vec_held[0].T, vec_held[1].T]
    hidden_vec = jnp.concatenate(vec, axis=0)
    feature_vec = in_order(first, *vec)
    nodes = node_held[...]
    edges = edge_held[...]
    if layer == 0:
        nodes = in_order(first, nodes[:half], nodes[half:])
        edges = in_order(first, edges[:half], edges[half:])
        held_out[4][...] = edges
        sent[4].start()
        held_out[5][...] = nodes
        sent[5].start()
    weights_ref[1] = out_held[0].T
    weights_ref[4] = out_held[1].T
    sent[1].start()
    vectors_ref[...] = jnp.concatenate([hidden_vec, feature_vec] + [hidden_vec] * 14, axis=1)
    sent[3].start()
    slots = incidence_ref.shape[1]
    live = lax.broadcasted_iota(jnp.int32, (1, slots), 1) < count
    incidence_ref[...] = jnp.where(
        (lax.broadcasted_iota(jnp.int32, incidence_ref.shape, 0) == receiver_ref[...]) & live,
        1.0,
        0.0,
    ).astype(jnp.bfloat16)
    sent[2].start()
    receiver_part = dot(hidden_weight_ref[1], nodes).astype(jnp.bfloat16)
    before = dot(hidden_weight_ref[0], edges) + dot(receiver_part, incidence_ref[...])
    before_ref[...] = (before + hidden_vec[:, 0:1]).astype(jnp.bfloat16)
    sent[0].start()
    finish(sent)


def prepared(layer, scalars, edges, receiver, nodes, weights):
    slots = edges[0].shape[1]
    node_rows = nodes[0].shape[1]
    width = weights[0].shape[1] * 2
    inputs = (receiver, *weights, *edges, *nodes)
    out_shape = [
        shape((width, slots)),
        shape((5, width, width)),
        shape((node_rows, slots)),
        shape((width, 128), jnp.float32),
    ]
    if layer == 0:
        out_shape += [shape((width, slots)), shape((width, node_rows))]
    n_in, n_out = len(inputs), len(out_shape)
    ready = kernel_call(
        functools.partial(prepare_kernel, layer, n_in, n_out),
        "prepare_layer",
        out_shape,
        (scalars, *inputs),
        [SMEM] + [HBM] * n_in,
        [HBM] * n_out,
        held(
            [
                *out_shape,
                shape((width, slots)),
                shape((width, node_rows)),
                shape((2, width, width)),
                shape((2, width, width)),
                shape((2, *weights[8].shape[1:]), jnp.float32),
                receiver,
            ]
        )
        + [pltpu.SemaphoreType.DMA((21,)), pltpu.SemaphoreType.DMA((n_out,))],
        2 * slots * width * (width + node_rows),
    )
    if layer == 0:
        return ready
    return (*ready, *edges, *nodes)


def update_kernel(last_layer, block, n_out, scalar_ref, *refs):
    sent_a_ref, sent_b_ref, before_ref, weights_ref, incidence_ref, small_ref = refs[:6]
    edges_ref, nodes_ref, outs, refs = refs[6], refs[7], refs[8 : 8 + n_out], refs[8 + n_out :]
    edge_out_ref, node_out_ref, hidden_ref, mlp_ref, vectors_ref, out_sems = refs
    half = sent_a_ref.shape[1]
    width = 2 * half
    first = scalar_ref[0] == 0
    count = scalar_ref[1]
    sent_out = []

    def send(source, target):
        copy = pltpu.make_async_copy(source, target, out_sems.at[len(sent_out)])
        copy.start()
        sent_out.append(copy)

    small = small_ref[...]
    hidden_vec, feature_vec = small[:, 0:8], small[:, 8:16]
    for i, column in enumerate((1, 2, 3)):
        vectors_ref[i] = jnp.broadcast_to(feature_vec[:, column : column + 1], (width, 128))

    def spread(index, rows):
        return jnp.concatenate([vectors_ref[index, rows, :]] * (block // 128), axis=1)

    slots = edges_ref.shape[1]
    total = None
    for start in range(0, slots, block):
        here = slice(start, start + block)
        sent_a, sent_b = sent_a_ref[here, :], sent_b_ref[here, :]
        low = jnp.where(first, sent_a, sent_b)
        high = jnp.where(first, sent_b, sent_a)
        sent = jnp.concatenate([low, high], axis=1)
        mlp_ref[...] = dot(weights_ref[0], sent, ((1,), (1,)))
        for row in range(0, width, ROWS):
            rows = slice(row, row + ROWS)
            value = silu(mlp_ref[rows, :] + before_ref[rows, here].astype(jnp.float32))
            hidden_ref[rows, :] = value.astype(jnp.bfloat16)
        mlp_ref[...] = dot(weights_ref[1], hidden_ref[...])
        new_ref = hidden_ref if last_layer else columns_of(edge_out_ref, start, block)
        sums = jnp.zeros((8, block), jnp.float32)
        squares = jnp.zeros((8, block), jnp.float32)
        for row in range(0, width, ROWS):
            rows = slice(row, row + ROWS)
            value = mlp_ref[rows, :] + spread(0, rows)
            mlp_ref[rows, :] = value
            sums = sums + jnp.sum(value.reshape(ROWS // 8, 8, block), axis=0)
            squares = squares + jnp.sum((value * value).reshape(ROWS // 8, 8, block), axis=0)
        mean = jnp.sum(sums, axis=0, keepdims=True) * (1.0 / width)
        square = jnp.sum(squares, axis=0, keepdims=True) * (1.0 / width)
        scale = lax.rsqrt(square - mean * mean + EPSILON)
        live = lax.broadcasted_iota(jnp.int32, (1, block), 1) + start < count
        for row in range(0, width, ROWS):
            rows = slice(row, row + ROWS)
            value = (mlp_ref[rows, :] - mean) * scale * spread(1, rows) + spread(2, rows)
            value = value + edges_ref[rows, here].astype(jnp.float32)
            new_ref[rows, :] = jnp.where(live, value, 0.0).astype(jnp.bfloat16)
        updated = new_ref[...]
        part = dot(updated, incidence_ref[:, here], ((1,), (1,)))
        total = part if total is None else total + part
        if last_layer:
            edge_out_ref[:, here] = jnp.where(first, updated[:half], updated[half:])
        send(
            columns_of(edge_out_ref, start, block), columns_of(outs[0], start, block)
        )
    nodes = nodes_ref[...]
    aggregate = total.astype(jnp.bfloat16)
    node_before = dot(weights_ref[2], nodes) + dot(weights_ref[3], aggregate)
    node_hidden = silu(node_before + hidden_vec[:, 4:5]).astype(jnp.bfloat16)
    node_mlp = dot(weights_ref[4], node_hidden) + feature_vec[:, 5:6]
    new = nodes.astype(jnp.float32) + layer_norm(
        node_mlp, feature_vec[:, 6:7], feature_vec[:, 7:8]
    )
    new = new.astype(jnp.bfloat16)
    mine = jnp.where(first, new[:half], new[half:])
    if last_layer:
        node_out_ref[...] = mine
        send(node_out_ref, outs[1])
    else:
        node_out_ref[...] = new
        send(node_out_ref, outs[1])
        rows = new.T
        store_rows(rows, jnp.where(first, rows[:, :half], rows[:, half:]), *outs[2:])
    finish(sent_out)


def updated_graph(last_layer, scalars, sent, ready, copies):
    block = UPDATE_BLOCK if last_layer else UPDATE_BLOCK // 2
    slots = ready[0].shape[1]
    node_rows = ready[5].shape[1]
    half = sent[0].shape[1]
    width = 2 * half
    out_width = half if last_layer else width
    out_shape = [shape((out_width, slots)), shape((out_width, node_rows))]
    out_specs = [HBM, HBM]
    if not last_layer:
        out_shape += [shape((node_rows, width)), shape((copies, node_rows // 8, half))]
        out_specs = [HBM, HBM, VMEM, VMEM]
    n_out = len(out_shape)
    return kernel_call(
        functools.partial(update_kernel, last_layer, block, n_out),
        "update_graph",
        out_shape,
        (scalars, *sent, *ready),
        [SMEM] + [VMEM] * (2 + len(ready)),
        out_specs,
        held(
            [
                *out_shape[:2],
                shape((width, block)),
                shape((width, block), jnp.float32),
                shape((3, width, 128), jnp.float32),
            ]
        )
        + [pltpu.SemaphoreType.DMA((slots // block + 1,))],
        2 * slots * width * (2 * width + node_rows),
    )


def from_other(a):
    return lax.ppermute(a, "width", [(0, 1), (1, 0)])


def copies_kernel(rows_ref, copies_ref, sems):
    finish(started([(rows_ref, copies_ref.at[i]) for i in range(copies_ref.shape[0])], sems))


def copied(rows, count):
    sems = [pltpu.SemaphoreType.DMA((count,))]
    return kernel_call(
        copies_kernel, "copies", [shape((count, *rows.shape))], (rows,), [VMEM], [HBM], sems, 0
    )[0]


def exchanged(rows, copies, others=()):
    size = lax.axis_size(PATCH)
    pairs = []
    for i in range(size):
        pairs += [(2 * i, (i + 1) % size * 2), (2 * i + 1, (i - 1) % size * 2 + 1)]
    beside = lax.ppermute(rows, (*PATCH, "width"), pairs)
    column = lax.all_to_all(copies, Z, split_axis=0, concat_axis=0, tiled=True)
    column = column.reshape(-1, copies.shape[2])
    column, others = lax.optimization_barrier((column, others))
    plane = copied(column, lax.axis_size(PLANE))
    coarse = lax.all_to_all(plane, PLANE, split_axis=0, concat_axis=0, tiled=True)
    return (rows, beside, coarse.reshape(-1, copies.shape[2])), others


def completed(table, ready):
    rows, beside, coarse = table
    beside, ready = lax.optimization_barrier((beside, ready))
    half = coarse.shape[1]
    theirs = (1 - lax.axis_index("width")) * half
    other = from_other(lax.dynamic_slice_in_dim(beside, theirs, half, 1))
    return (rows, beside, other, coarse), ready


def on_device(
    node_latents,
    edge_latents,
    senders,
    receivers,
    edge_count,
    edge_in_weight,
    edge_in_bias,
    edge_out_weight,
    edge_out_bias,
    edge_gain,
    edge_shift,
    node_in_weight,
    node_in_bias,
    node_out_weight,
    node_out_bias,
    node_gain,
    node_shift,
):
    half, node_rows = node_latents.shape
    layers = edge_in_weight.shape[0]
    coarse_rows = node_rows // 8
    patch_here = lax.axis_index(PATCH)
    patches = lax.axis_size(PATCH)
    plane = lax.axis_size(PLANE)
    columns = lax.axis_size(Z)
    scalars = jnp.stack([lax.axis_index("width"), edge_count[0]]).astype(jnp.int32)

    rows, copies = node_rows_of(node_latents, columns)

    vectors = jnp.stack(
        [
            edge_in_bias,
            edge_out_bias,
            edge_gain,
            edge_shift,
            node_in_bias,
            node_out_bias,
            node_gain,
            node_shift,
        ],
        axis=1,
    )
    own = (edge_in_weight, edge_out_weight, node_in_weight, node_out_weight, vectors)
    weights = []
    for a in own:
        weights += [a, from_other(a)]

    owner = senders // node_rows
    within = senders - owner * node_rows
    place = (owner % plane) * (patches // plane) + owner // plane
    index = jnp.where(
        owner == patch_here,
        node_rows + within,
        jnp.where(
            owner == (patch_here + patches - 1) % patches,
            within,
            jnp.where(
                owner == (patch_here + 1) % patches,
                2 * node_rows + within,
                3 * node_rows + place * coarse_rows + within,
            ),
        ),
    )
    index = index.reshape(-1, 128)
    receiver = (receivers - patch_here * node_rows)[None, :]

    edges = (edge_latents, from_other(edge_latents))
    nodes = (node_latents, from_other(node_latents))
    others = (weights[1], weights[5], edges[1], index, receiver)
    other_rows = from_other(rows)
    rows = jnp.where(
        lax.axis_index("width") == 0,
        jnp.concatenate([rows, other_rows], axis=1),
        jnp.concatenate([other_rows, rows], axis=1),
    )
    table, others = exchanged(rows, copies, others)
    weights[1], weights[5], other_edges, index, receiver = others
    edges = (edges[0], other_edges)
    for layer in range(layers):
        last_layer = layer == layers - 1
        ready = prepared(layer, scalars, edges, receiver, nodes, weights)
        table, ready = completed(table, ready)
        table, ready = lax.optimization_barrier((table, ready))
        sent, *ready = gathered(scalars, ready, index, *table)
        sent = (sent, from_other(sent))
        results = updated_graph(last_layer, scalars, sent, ready, columns)
        if not last_layer:
            edges, nodes = results[:1], results[1:2]
            table, _ = exchanged(results[2], results[3])
    return (results[1], results[0])


def solution(mesh):
    finer = Mesh(
        mesh.devices.reshape(8, 4, 4, mesh.shape["width"]),
        (*PATCH, "width"),
    )
    in_specs = (
        P("width", PATCH),
        P("width", PATCH),
        P(PATCH),
        P(PATCH),
        P(PATCH),
        P(None, "width", None),
        P(None, "width"),
        P(None, "width", None),
        P(None, "width"),
        P(None, "width"),
        P(None, "width"),
        P(None, "width", None),
        P(None, "width"),
        P(None, "width", None),
        P(None, "width"),
        P(None, "width"),
        P(None, "width"),
    )
    out_specs = (P("width", PATCH), P("width", PATCH))
    return jax.shard_map(
        on_device, mesh=finer, in_specs=in_specs, out_specs=out_specs, check_vma=False
    )
```
